32 devices in a mesh: pop: 8 (over z, x), mp: 4 (over y, core).
Axes of the slice: x: 2, y: 2, z: 4, core: 2. Of those that a mesh axis runs over, the one named last changes fastest.
Arguments:
- context: bfloat16 [3072, 5120], P('pop', 'mp'), may hold values from -9 to 9
- out_weight: bfloat16 [5120, 5120], P('mp'), may hold values from -0.078125 to 0.078125
- residual: bfloat16 [3072, 5120], P('pop', 'mp'), may hold values from -6 to 6
- target: bfloat16 [3072, 5120], P('pop', 'mp'), may hold values from -9 to 9
- norm_gain: float32 [5120], replicated, may hold values from 0.5 to 1.5
- left_factors: bfloat16 [128, 5120], P('pop'), may hold values from -6 to 6
- right_factors: bfloat16 [128, 5120], P('pop'), may hold values from -8 to 8
- member_ranks: int32 [128], P('pop'), may hold values from 0 to 127, each once
Outputs:
- update: float32 [5120, 5120], P('pop', 'mp')
- fitness: float32 [128], P('pop')
- base: float32 [3072, 5120], P('pop', 'mp')
The draws below stay inside these ranges and needn't reach their ends.
Inputs may be any that keep to these rules, and one draw needn't show every extreme that they name: `member_ranks`: each number from 0 to 127 appears exactly once.
All inputs are finite; a program needn't handle non-finite values.
Results may differ from the reference program's by a relative error of at most 0.0095.
Values may be sent and summed in bfloat16 or wider, within the bound.
A program may use at most 64 MiB of HBM per device.

```python
import math
import jax
import jax.numpy as jnp
from jax import lax

D = 5120
TOK = 384
MEM_DEV = 16
MEMBERS = 128
TOKENS = 3072
N_POP = 8
N_MP = 4


def stream_draw(key):
    normal_part = jax.random.normal(jax.random.fold_in(key, 11), (TOKENS, D), jnp.float32)
    return jnp.clip(normal_part, -6.0, 6.0)


def shared_direction(key, salt):
    vector = jax.random.normal(jax.random.fold_in(key, salt), (1, D), jnp.float32)
    return jnp.clip(vector, -4.0, 4.0)


def draw_residual(key, part):
    return stream_draw(key).astype(jnp.bfloat16)


def draw_context(key, part):
    normal_part = jnp.clip(jax.random.normal(jax.random.fold_in(key, 33), (TOKENS, D), jnp.float32), -6.0, 6.0)
    common = shared_direction(key, 31)
    return jnp.clip(normal_part + 0.7 * common, -9.0, 9.0).astype(jnp.bfloat16)


def draw_right_factors(key, part):
    normal_part = jnp.clip(jax.random.normal(jax.random.fold_in(key, 34), (MEMBERS, D), jnp.float32), -6.0, 6.0)
    flips = jax.random.bernoulli(jax.random.fold_in(key, 35), 0.5, (MEMBERS, 1)).astype(jnp.float32)
    member_sign = 2.0 * flips - 1.0
    common = shared_direction(key, 32)
    return jnp.clip(normal_part + 0.5 * member_sign * common, -8.0, 8.0).astype(jnp.bfloat16)


def draw_target(key, part):
    stream = stream_draw(key)
    jitter = jax.random.normal(jax.random.fold_in(key, 12), (TOKENS, D), jnp.float32)
    mixed = stream + 0.2 * jnp.clip(jitter, -6.0, 6.0)
    normed = mixed / jnp.sqrt(jnp.mean(mixed * mixed, axis=1, keepdims=True) + 1e-06)
    noise = 0.3 * jnp.clip(jax.random.normal(jax.random.fold_in(key, 13), (TOKENS, D), jnp.float32), -6.0, 6.0)
    common = shared_direction(key, 32)
    return jnp.clip(normed + noise + 0.5 * common, -9.0, 9.0).astype(jnp.bfloat16)


def level_of(stream_key, dims, shards, smallest, largest):
    def one(position, shards_of):
        steps = jax.random.uniform(jax.random.fold_in(jax.random.fold_in(stream_key, 6), position), (shards_of,), jnp.float32, smallest / len(shards), largest / len(shards))
        return jnp.repeat(jnp.exp(steps), dims[position] // shards_of).reshape((-1,) + (1,) * (len(dims) - position - 1))

    gain = one(*shards[0])
    for cut in shards[1:]:
        gain = gain * one(*cut)
    return gain


def scatter_about(rng, extent, deviation, bound, pieces=(), kind=jnp.bfloat16):
    drawn = deviation * jax.random.normal(rng, extent, jnp.float32)
    if pieces:
        drawn = drawn * level_of(rng, extent, pieces, -0.22, 0.18)
    return jnp.clip(drawn, -bound, bound).astype(kind)


def setup_inputs(seed: int = 0) -> dict:
    keys = jax.random.split(jax.random.key(seed), 9)
    return {
        "context": draw_context(jax.random.fold_in(keys[8], 71), 0),
        "out_weight": scatter_about(keys[1], (D, D), D ** -0.5, 0.078125, ((0, 4),)),
        "residual": draw_residual(jax.random.fold_in(keys[8], 71), 0),
        "target": draw_target(jax.random.fold_in(keys[8], 71), 0),
        "norm_gain": jnp.clip(1.0 + 0.1 * jax.random.normal(keys[4], (D,), jnp.float32), 0.5, 1.5),
        "left_factors": scatter_about(keys[5], (MEMBERS, D), 1.0, 6.0, ((0, 8),)),
        "right_factors": draw_right_factors(jax.random.fold_in(keys[8], 71), 0),
        "member_ranks": jax.random.permutation(keys[7], MEMBERS).astype(jnp.int32),
    }


SIGMA = 1.0
EPSILON = 1e-06

def member_errors(stream, right_rows, projected, norm_gain, target_rows):
    factor = SIGMA / math.sqrt(D)
    hidden = stream[:, None, :] + factor * projected[:, :, None] * right_rows[None, :, :]
    meansq = lax.optimization_barrier(jnp.mean(hidden * hidden, axis=2, keepdims=True))
    normed = norm_gain * hidden * lax.rsqrt(meansq + EPSILON)
    differ = normed - target_rows[:, None, :]
    return lax.optimization_barrier(jnp.sum(differ * differ, axis=2))

def utility(member_ranks, count_all):
    levels = jnp.arange(count_all).astype(jnp.float32)
    ceiling = math.log(count_all / 2 + 1)
    baseline = jnp.maximum(0.0, ceiling - jnp.log(levels + 1.0))
    shaped = jnp.maximum(0.0, ceiling - jnp.log(member_ranks.astype(jnp.float32) + 1.0))
    return shaped / jnp.sum(baseline) - 1.0 / count_all

def reference(context, out_weight, residual, target, norm_gain, left_factors, right_factors, member_ranks):
    shard_width = D // N_MP
    stream = residual.astype(jnp.float32)
    for block in range(N_MP):
        offset = block * shard_width
        partial_value = jnp.dot(context[:, offset:offset + shard_width], out_weight[offset:offset + shard_width], preferred_element_type=jnp.float32)
        stream = stream + lax.optimization_barrier(partial_value.astype(jnp.bfloat16)).astype(jnp.float32)

    def scored(grouped):
        context_group, stream_group, target_group, left_group, right_group = grouped
        projected = lax.dot_general(context_group, left_group, (((1,), (1,)), ((), ())), preferred_element_type=jnp.float32)
        errors = member_errors(stream_group, right_group.astype(jnp.float32), projected, norm_gain, target_group.astype(jnp.float32))
        return -lax.optimization_barrier(jnp.sum(errors, axis=0)) / (TOK * D)
    fitness = lax.map(scored, (context.reshape(N_POP, TOK, D), stream.reshape(N_POP, TOK, D), target.reshape(N_POP, TOK, D), left_factors.reshape(N_POP, MEM_DEV, D), right_factors.reshape(N_POP, MEM_DEV, D))).reshape(MEMBERS)
    centre = fitness - jnp.mean(fitness)
    spread = jnp.sqrt(jnp.mean(centre * centre) + 1e-05)
    weight = utility(member_ranks, MEMBERS) + centre / spread / MEMBERS
    weighted = (weight[:, None] * left_factors.astype(jnp.float32)).astype(jnp.bfloat16)
    update = lax.dot_general(weighted, right_factors, (((0,), (0,)), ((), ())), preferred_element_type=jnp.float32) * (math.sqrt(MEMBERS) / SIGMA)
    return (update, fitness, stream)
```

```python
import functools
import math

import jax
import jax.numpy as jnp
from jax import lax
from jax.experimental import pallas as pl
from jax.experimental.pallas import tpu as pltpu
from jax.sharding import PartitionSpec as P

SIGMA = 1.0
EPSILON = 1e-06


def error_sums(stream, lifted, right_rows, gain_part, target_rows, inverse):
    hidden = stream[:, None, :] + lifted[:, :, None] * right_rows[None, :, :]
    differ = gain_part * hidden * inverse[:, :, None] - target_rows[:, None, :]
    return jnp.sum(differ * differ, axis=(0, 2))


def utility(member_ranks, count_all):
    levels = jnp.arange(count_all).astype(jnp.float32)
    ceiling = math.log(count_all / 2 + 1)
    baseline = jnp.maximum(0.0, ceiling - jnp.log(levels + 1.0))
    shaped = jnp.maximum(0.0, ceiling - jnp.log(member_ranks.astype(jnp.float32) + 1.0))
    return shaped / jnp.sum(baseline) - 1.0 / count_all


def shards(
    context, out_weight, residual, target, norm_gain, left_factors, right_factors, member_ranks
):
    tok_count = context.shape[0]
    shard_width = context.shape[1]
    full_width = out_weight.shape[1]
    factor = SIGMA / math.sqrt(full_width)
    offset = lax.axis_index("mp") * shard_width
    left_cols = lax.dynamic_slice_in_dim(left_factors, offset, shard_width, 1)
    right_cols = lax.dynamic_slice_in_dim(right_factors, offset, shard_width, 1)
    partial_value = jnp.dot(context, out_weight, preferred_element_type=jnp.float32)
    projected = lax.dot_general(
        context, left_cols, (((1,), (1,)), ((), ())), preferred_element_type=jnp.float32
    )
    summed = lax.psum_scatter(
        partial_value.astype(jnp.bfloat16), "mp", scatter_dimension=1, tiled=True
    ).astype(jnp.float32)
    stream = residual.astype(jnp.float32) + summed
    gain_part = lax.dynamic_slice_in_dim(norm_gain, offset, shard_width, 0)
    factor_f = right_cols.astype(jnp.float32)
    crossed = jnp.dot(stream, factor_f.T, precision=lax.Precision.HIGHEST)
    per_token = jnp.sum(stream * stream, axis=1)
    per_member = jnp.sum(factor_f * factor_f, axis=1)
    projected, crossed, per_token, per_member = lax.psum(
        (projected, crossed, per_token, per_member), "mp"
    )
    lifted = factor * projected
    meansq = (
        per_token[:, None] + 2.0 * lifted * crossed + lifted * lifted * per_member[None, :]
    ) / full_width
    inverse = lax.rsqrt(meansq + EPSILON)
    local_error = error_sums(
        stream, lifted, factor_f, gain_part, target.astype(jnp.float32), inverse
    )
    member_total = lax.psum(local_error, "mp")
    fitness = -member_total / (tok_count * full_width)
    everyone = lax.all_gather(fitness, "pop", axis=0, tiled=True)
    count_all = everyone.shape[0]
    average = jnp.mean(everyone)
    centre = everyone - average
    spread = jnp.sqrt(jnp.mean(centre * centre) + 1e-05)
    weight = utility(member_ranks, count_all) + (fitness - average) / spread / count_all
    weighted = (weight[:, None] * left_factors.astype(jnp.float32)).astype(jnp.bfloat16)
    weighted_rows = lax.all_to_all(weighted, "pop", split_axis=1, concat_axis=0, tiled=True)
    right_all = lax.all_gather(right_cols, "pop", axis=0, tiled=True)
    update = lax.dot_general(
        weighted_rows, right_all, (((0,), (0,)), ((), ())), preferred_element_type=jnp.float32
    ) * (math.sqrt(count_all) / SIGMA)
    return (update, fitness, stream)


BLK = 256
LANES = 128
F32 = jnp.float32
BF = jnp.bfloat16


def nt_dot(a, b):
    return lax.dot_general(a, b, (((1,), (1,)), ((), ())), preferred_element_type=F32)


def split_two(x):
    hi = x.astype(BF)
    return hi, (x - hi.astype(F32)).astype(BF)


def halves(parts):
    return jnp.concatenate([piece for part in parts for piece in split_two(part)], axis=1)


def row_picker(count):
    shape = (8, count * 2 * LANES)
    owner = lax.broadcasted_iota(jnp.int32, shape, 1) // (2 * LANES)
    return jnp.where(owner == lax.broadcasted_iota(jnp.int32, shape, 0), 1.0, 0.0).astype(BF)


def flip(index, bits):
    for bit in (1, 2, 4):
        if bits & bit:
            index = index + bit - 2 * bit * ((index // bit) % 2)
    return index


def kernel(
    n_pop, n_mp, ctx_h, w_h, res_h, tgt_h, gain_h, left_h, right_h, ranks_h,
    base, weighted, right_all, fit_out,
    w_v, ctx, res, tgt, lcols, gain, right, ranks, send, recv, lall, rall,
    sq_s, sq_a, sq_e, sq_t, lin, lin_in, lin_out, lin_far, post, post_in, fits,
    w_sem, half_sem, near_sem, loc_sem, sent, r_a, r_y, r_b,
    s_lin, r_lin, s_far, r_far, s_post, r_post, s_l, r_l, s_r, r_r, s_f, r_f, rounds,
):
    tok, width = ctx.shape
    mem = right.shape[0]
    full = right.shape[1]
    rows = full // n_pop
    chunks = width // BLK
    units = width // LANES
    per = mem // n_mp
    members = mem * n_pop
    p = lax.axis_index("pop")
    q = lax.axis_index("mp")
    mate = flip(q, 1)
    across = flip(q, 2)
    diagonal = flip(q, 3)
    blocks = (diagonal, across, mate, q)

    def remote(src, dst, ss, rs, pop, mp):
        return pltpu.make_async_remote_copy(
            src_ref=src, dst_ref=dst, send_sem=ss, recv_sem=rs,
            device_id=(pop, mp), device_id_type=pl.DeviceIdType.MESH,
        )

    def signal(sem, pop, mp):
        pl.semaphore_signal(sem, inc=1, device_id=(pop, mp), device_id_type=pl.DeviceIdType.MESH)

    def w_copy(s, k):
        start = pl.multiple_of(blocks[s] * width + k * BLK, BLK)
        sem = near_sem if s == 3 else w_sem.at[s, k % 3]
        return pltpu.make_async_copy(w_h.at[:, pl.ds(start, BLK)], w_v.at[s, k], sem)

    def w_half(h):
        start = pl.multiple_of(blocks[0] * width + h * LANES, LANES)
        cols = pl.ds(h * LANES, LANES)
        return pltpu.make_async_copy(w_h.at[:, pl.ds(start, LANES)], w_v.at[0, 0, :, cols], half_sem.at[h])

    my_cols = pl.ds(pl.multiple_of(q * width, BLK), width)
    my_rows = pl.ds(pl.multiple_of(p * rows, LANES), rows)
    locals_ = [
        pltpu.make_async_copy(ctx_h, ctx, loc_sem.at[0]),
        pltpu.make_async_copy(res_h, res, loc_sem.at[1]),
        pltpu.make_async_copy(tgt_h, tgt, loc_sem.at[2]),
        pltpu.make_async_copy(left_h.at[:, my_cols], lcols, loc_sem.at[3]),
        pltpu.make_async_copy(left_h.at[:, my_rows], lall.at[0], loc_sem.at[4]),
        pltpu.make_async_copy(right_h.at[:, my_cols], rall.at[0], loc_sem.at[5]),
        pltpu.make_async_copy(gain_h, gain, loc_sem.at[6]),
        pltpu.make_async_copy(right_h, right, loc_sem.at[7]),
        pltpu.make_async_copy(ranks_h, ranks, loc_sem.at[8]),
    ]
    w_half(0).start()
    locals_[0].start()
    w_half(1).start()
    w_copy(1, 0).start()

    barrier = pltpu.get_barrier_semaphore()
    for peer in (mate, across, diagonal):
        signal(barrier, p, peer)
    for bit in (1, 2, 4):
        signal(barrier, flip(p, bit), q)

    def copy_a(first, count, n):
        cols = pl.ds(first, count)
        return remote(send.at[0, cols], recv.at[0, cols], sent, r_a.at[n], p, mate)

    def copy_y(u):
        return remote(send.at[1, u], recv.at[1, u], sent, r_y.at[u], p, across)

    def copy_b(k):
        cols = pl.ds(2 * k, 2)
        return remote(send.at[2, cols], recv.at[2, cols], sent, r_b, p, mate)

    def copy_l(d):
        peer = flip(p, d)
        cols = pl.ds(pl.multiple_of(peer * rows, LANES), rows)
        return remote(left_h.at[:, cols], lall.at[d], s_l, r_l, peer, q)

    def copy_r(d):
        return remote(right_h.at[:, my_cols], rall.at[d], s_r, r_r, flip(p, d), q)

    def copy_f(n):
        return remote(fits.at[0], fits.at[n], s_f, r_f, flip(p, n // n_mp), flip(q, n % n_mp))

    def copy_lin(i):
        return remote(lin.at[(mate, diagonal)[i]], lin_in.at[i], s_lin, r_lin, p, mate)

    def copy_post(d):
        return remote(post.at[0], post_in.at[d - 1], s_post, r_post, p, flip(q, d))

    def split_store(which, k, value):
        send[which, 2 * k] = value[:, :LANES]
        send[which, 2 * k + 1] = value[:, LANES:]

    def product(s, k):
        return jnp.dot(ctx[...], w_v[s, k], preferred_element_type=F32)

    def half(s, h):
        return jnp.dot(ctx[...], w_v[s, 0, :, h * LANES:(h + 1) * LANES], preferred_element_type=F32)

    locals_[0].wait()
    w_half(0).wait()
    w_copy(0, 1).start()
    w_copy(2, 0).start()
    w_copy(1, 1).start()
    send[0, 0] = half(0, 0).astype(BF)
    with jax.named_scope("barrier"):
        pl.semaphore_wait(barrier, 6)
    copy_a(0, 1, 0).start()
    signal(rounds.at[0], flip(p, 1), q)
    w_half(1).wait()
    send[0, 1] = half(0, 1).astype(BF)
    copy_a(1, 1, 1).start()
    w_copy(2, 1).start()
    for s in range(3):
        w_copy(s, 2).start()
    w_copy(1, 0).wait()
    first = half(1, 0)
    second = half(1, 1)
    with jax.named_scope("wait_a0"):
        copy_a(0, 1, 0).wait_recv()
    send[1, 0] = (first + recv[0, 0].astype(F32)).astype(BF)
    copy_y(0).start()
    copy_a(1, 1, 1).wait_recv()
    send[1, 1] = (second + recv[0, 1].astype(F32)).astype(BF)
    copy_y(1).start()
    w_copy(0, 1).wait()
    split_store(0, 1, product(0, 1).astype(BF))
    copy_a(2, 2, 2).start()
    w_copy(3, 0).start()
    w_copy(2, 0).wait()
    split_store(2, 0, product(2, 0).astype(BF))
    copy_b(0).start()

    def far(k, carry):
        @pl.when(k + 2 < chunks)
        def _():
            for s in range(3):
                w_copy(s, k + 2).start()

        w_copy(3, k).start()

        @pl.when(k == 1)
        def _():
            for item in locals_[1:]:
                item.start()
            pl.semaphore_wait(rounds.at[0], 1)
            signal(rounds.at[1], flip(p, 2), q)

        @pl.when(k == 2)
        def _():
            pl.semaphore_wait(rounds.at[1], 1)
            signal(rounds.at[2], flip(p, 4), q)

        @pl.when(k == 3)
        def _():
            pl.semaphore_wait(rounds.at[2], 1)
            for d in range(1, n_pop):
                copy_r(n_pop - d).start()
                copy_l(n_pop - d).start()

        w_copy(1, k).wait()
        mine = product(1, k)

        @pl.when(k + 1 < chunks)
        def _():
            w_copy(0, k + 1).wait()
            split_store(0, k + 1, product(0, k + 1).astype(BF))
            copy_a(2 * k + 2, 2, k + 2).start()

        with jax.named_scope("wait_a"):
            copy_a(2 * k, 2, k + 1).wait_recv()
        send[1, 2 * k] = (mine[:, :LANES] + recv[0, 2 * k].astype(F32)).astype(BF)
        copy_y(2 * k).start()
        send[1, 2 * k + 1] = (mine[:, LANES:] + recv[0, 2 * k + 1].astype(F32)).astype(BF)

        @pl.when(k + 1 < chunks)
        def _():
            copy_y(2 * k + 1).start()

        w_copy(2, k).wait()
        split_store(2, k, product(2, k).astype(BF))
        copy_b(k).start()
        return carry

    with jax.named_scope("far"):
        lax.fori_loop(1, chunks, far, 0)

    for item in locals_[1:]:
        item.wait()
    pltpu.make_async_copy(w_v.at[3], w_v.at[3], near_sem).wait()

    def near(k, carry):
        cols = pl.ds(pl.multiple_of(k * BLK, BLK), BLK)
        base[:, cols] = product(3, k) + res[:, cols].astype(F32)
        return carry

    with jax.named_scope("near"):
        lax.fori_loop(0, chunks, near, 0)

    with jax.named_scope("early"):
        r_mine = rall[0].astype(F32)
        gr_hi, gr_lo = split_two(r_mine * gain[:, my_cols])
        projected = nt_dot(lcols[...], ctx[...])
        cross_t = nt_dot(gr_hi, tgt[...]) + nt_dot(gr_lo, tgt[...])
        for j in range(n_mp):
            lin[j, 0:per, :] = projected[j * per:(j + 1) * per]
            lin[j, per:2 * per, :] = cross_t[j * per:(j + 1) * per]
        r_full = right[...].astype(F32)
        gr_full = r_full * gain[...]
        norm_r = jnp.sum(r_full * r_full, axis=1, keepdims=True)
        norm_gr = jnp.sum(gr_full * gr_full, axis=1, keepdims=True)
        sq_s[...] = jnp.zeros_like(sq_s)
        sq_a[...] = jnp.zeros_like(sq_a)
        sq_e[...] = jnp.zeros_like(sq_e)
        sq_t[...] = jnp.zeros_like(sq_t)

    def mixed(block, k):
        cols = pl.ds(pl.multiple_of(block * width + k * BLK, BLK), BLK)
        r = right[:, cols]
        g = gain[:, cols]
        hi, low = split_two(r.astype(F32) * (g * g))
        return jnp.concatenate([r, hi, low], axis=0)

    def linear(k, carry):
        crossed, crossed_g = carry
        near_rows = mixed(q, k)
        far_rows = mixed(across, k)
        for h in range(2):
            cols = pl.ds(pl.multiple_of(k * BLK + h * LANES, LANES), LANES)
            part = slice(h * LANES, (h + 1) * LANES)
            u = 2 * k + h
            s = base[:, cols] + recv[2, u].astype(F32)
            base[:, cols] = s
            hi, low = split_two(s)
            both = nt_dot(near_rows[:, part], hi) + nt_dot(near_rows[:, part], low) + nt_dot(far_rows[:, part], send[1, u])
            crossed = crossed + both[0:mem]
            crossed_g = crossed_g + both[mem:2 * mem] + both[2 * mem:3 * mem]
            wide = tgt[:, cols].astype(F32)
            sq_t[...] += wide * wide
        return crossed, crossed_g

    with jax.named_scope("wait_b"):
        pltpu.make_async_copy(send.at[2], recv.at[2], r_b).wait()
    with jax.named_scope("linear"):
        empty = jnp.zeros((mem, tok), F32)
        crossed, crossed_g = lax.fori_loop(0, chunks, linear, (empty, empty))
        for j in range(n_mp):
            lin[j, 2 * per:3 * per, :] = crossed[j * per:(j + 1) * per]
            lin[j, 3 * per:4 * per, :] = crossed_g[j * per:(j + 1) * per]
        copy_lin(1).start()
        copy_lin(0).start()

    def arrived(u):
        cols = pl.ds(pl.multiple_of(u * LANES, LANES), LANES)
        gain_u = gain[:, pl.ds(pl.multiple_of(q * width + u * LANES, LANES), LANES)]
        s = base[:, cols] + recv[1, u].astype(F32)
        base[:, cols] = s
        gs = s * gain_u
        return s * s, gs * gs, gs * tgt[:, cols].astype(F32)

    def settle(u, carry):
        with jax.named_scope("wait_y"):
            copy_y(u).wait_recv()
        for acc, item in zip((sq_s, sq_a, sq_e), arrived(u)):
            acc[...] += item
        return carry

    with jax.named_scope("settle0"):
        lax.fori_loop(0, 3, settle, 0)
    with jax.named_scope("wait_lin"):
        pltpu.make_async_copy(lin_in, lin_in, r_lin).wait()
    lin_out[...] = lin[across] + lin_in[1]
    copy_far = remote(lin_out, lin_far, s_far, r_far, p, across)
    copy_far.start()
    copy_y(units - 1).start()
    own = lin[q] + lin_in[0]
    with jax.named_scope("settle1"):
        lax.fori_loop(3, units - 1, settle, 0)
    before = nt_dot(row_picker(4), halves((sq_s[...], sq_a[...], sq_e[...], sq_t[...])))
    with jax.named_scope("wait_far"):
        copy_far.wait_recv()
    own = own + lin_far[...]

    def my_members(column):
        total = jnp.zeros((per, 1), F32)
        for j in range(n_mp):
            total = total + jnp.where(q == j, 1.0, 0.0) * column[j * per:(j + 1) * per]
        return total

    lifted = own[0:per] * (SIGMA / math.sqrt(full))
    square = lifted * lifted
    extra_s = 2.0 * lifted * own[2 * per:3 * per] + square * my_members(norm_r)
    extra_a = 2.0 * lifted * own[3 * per:4 * per] + square * my_members(norm_gr)
    extra_e = lifted * own[per:2 * per]
    lane = lax.broadcasted_iota(jnp.int32, (1, mem), 1)
    mine_lane = lane // per == q
    ceiling = math.log(members / 2 + 1)
    whole = sum(max(0.0, ceiling - math.log(i + 1.0)) for i in range(members))
    shaped = jnp.maximum(0.0, ceiling - jnp.log(ranks[...].astype(F32) + 1.0)) / whole - 1.0 / members
    with jax.named_scope("wait_last"):
        copy_y(units - 1).wait_recv()
    with jax.named_scope("last"):
        after = nt_dot(row_picker(3), halves(arrived(units - 1)))
        post[0] = (before + after)[0:4]
        for d in (2, 3, 1):
            copy_post(d).start()
    with jax.named_scope("wait_post"):
        pltpu.make_async_copy(post_in, post_in, r_post).wait()
    with jax.named_scope("errors"):
        late = post[0] + post_in[0] + post_in[1] + post_in[2]
        meansq = (late[0:1] + extra_s) / full
        inverse = lax.rsqrt(meansq + EPSILON)
        errors = inverse * inverse * (late[1:2] + extra_a) - 2.0 * inverse * (late[2:3] + extra_e) + late[3:4]
        summed = jnp.sum(errors, axis=1, keepdims=True)
        stacked = jnp.concatenate([summed] * n_mp, axis=0)
        square16 = (mem, mem)
        eye = lax.broadcasted_iota(jnp.int32, square16, 0) == lax.broadcasted_iota(jnp.int32, square16, 1)
        total_row = jnp.sum(jnp.where(eye, stacked, 0.0), axis=0, keepdims=True)
        fits[0, 0:1] = jnp.where(mine_lane, total_row, 0.0)
        fits[0, 1:2] = jnp.where(mine_lane, shaped, 0.0)
        for n in range(n_pop * n_mp - 1, 0, -1):
            copy_f(n).start()
    with jax.named_scope("wait_lr"):
        pltpu.make_async_copy(lall.at[pl.ds(1, n_pop - 1)], lall.at[pl.ds(1, n_pop - 1)], r_l).wait()
        pltpu.make_async_copy(rall.at[pl.ds(1, n_pop - 1)], rall.at[pl.ds(1, n_pop - 1)], r_r).wait()
    for d in range(n_pop):
        right_all[d * mem:(d + 1) * mem, :] = rall[d]
    with jax.named_scope("drain"):
        pltpu.make_async_copy(send, send, sent).wait()
        pltpu.make_async_copy(lin_in, lin_in, s_lin).wait()
        copy_far.wait_send()
        pltpu.make_async_copy(post_in, post_in, s_post).wait()
        pltpu.make_async_copy(lall.at[pl.ds(1, n_pop - 1)], lall.at[pl.ds(1, n_pop - 1)], s_l).wait()
        pltpu.make_async_copy(rall.at[pl.ds(1, n_pop - 1)], rall.at[pl.ds(1, n_pop - 1)], s_r).wait()
    others = fits.at[pl.ds(1, n_pop * n_mp - 1)]
    with jax.named_scope("wait_f"):
        pltpu.make_async_copy(others, others, r_f).wait()
    with jax.named_scope("weights"):
        rows_of = []
        for d in range(n_pop):
            total = fits[d * n_mp]
            for j in range(1, n_mp):
                total = total + fits[d * n_mp + j]
            rows_of.append(total)
        all_fit = jnp.concatenate([row[0:1] for row in rows_of], axis=0) * (-1.0 / (tok * full))
        all_shaped = jnp.concatenate([row[1:2] for row in rows_of], axis=0)
        fit_out[...] = all_fit[0:1]
        average = jnp.sum(jnp.sum(all_fit, axis=0, keepdims=True), axis=1, keepdims=True) / members
        centre = all_fit - average
        spread = jnp.sqrt(jnp.sum(jnp.sum(centre * centre, axis=0, keepdims=True), axis=1, keepdims=True) / members + 1e-05)
        weight = all_shaped + centre / spread / members
        for d in range(n_pop):
            upright = jnp.sum(jnp.where(eye, weight[d:d + 1], 0.0), axis=1, keepdims=True)
            weighted[d * mem:(d + 1) * mem, :] = (upright * lall[d].astype(F32)).astype(BF)
        pltpu.make_async_copy(others, others, s_f).wait()


def in_hbm(x):
    return pltpu.with_memory_space_constraint(x, pltpu.HBM)


def fused_shards(
    n_pop, n_mp, context, out_weight, residual, target, norm_gain, left_factors, right_factors, member_ranks
):
    tok, width = context.shape
    full = out_weight.shape[1]
    mem = left_factors.shape[0]
    rows = full // n_pop
    chunks = width // BLK
    units = width // LANES
    ranks = member_ranks.reshape(1, mem)
    anywhere = pl.BlockSpec(memory_space=pltpu.HBM)
    vmem = pl.BlockSpec(memory_space=pltpu.VMEM)
    dma = pltpu.SemaphoreType.DMA
    acc = pltpu.VMEM((tok, LANES), F32)
    group = (4 * mem // n_mp, tok)
    base, weighted, right_all, fitness = pl.pallas_call(
        functools.partial(kernel, n_pop, n_mp),
        name="es_step",
        out_shape=(
            jax.ShapeDtypeStruct((tok, width), F32),
            jax.ShapeDtypeStruct((n_pop * mem, rows), BF),
            jax.ShapeDtypeStruct((n_pop * mem, width), BF),
            jax.ShapeDtypeStruct((1, mem), F32),
        ),
        in_specs=[anywhere] * 8,
        out_specs=[vmem] * 4,
        scratch_shapes=[
            pltpu.VMEM((4, chunks, width, BLK), BF),
            pltpu.VMEM((tok, width), BF),
            pltpu.VMEM((tok, width), BF),
            pltpu.VMEM((tok, width), BF),
            pltpu.VMEM((mem, width), BF),
            pltpu.VMEM((1, full), F32),
            pltpu.VMEM((mem, full), BF),
            pltpu.VMEM((1, mem), jnp.int32),
            pltpu.VMEM((3, units, tok, LANES), BF),
            pltpu.VMEM((3, units, tok, LANES), BF),
            pltpu.VMEM((n_pop, mem, rows), BF),
            pltpu.VMEM((n_pop, mem, width), BF),
            acc, acc, acc, acc,
            pltpu.VMEM((n_mp,) + group, F32),
            pltpu.VMEM((2,) + group, F32),
            pltpu.VMEM(group, F32),
            pltpu.VMEM(group, F32),
            pltpu.VMEM((1, 4, tok), F32),
            pltpu.VMEM((n_mp - 1, 4, tok), F32),
            pltpu.VMEM((n_pop * n_mp, 2, mem), F32),
            dma((3, 3)),
            dma((2,)),
            dma,
            dma((9,)),
            dma,
            dma((chunks + 1,)),
            dma((units,)),
        ]
        + [dma] * 13
        + [pltpu.SemaphoreType.REGULAR((3,))],
        compiler_params=pltpu.CompilerParams(
            collective_id=0, has_side_effects=True, vmem_limit_bytes=48 * 1024 * 1024
        ),
    )(
        *map(in_hbm, (
            context, out_weight, residual, target, norm_gain.reshape(1, full), left_factors,
            right_factors, ranks,
        ))
    )
    count_all = n_pop * mem
    update, base, fitness = pl.pallas_call(
        functools.partial(finish, math.sqrt(count_all) / SIGMA),
        name="es_update",
        out_shape=(
            jax.ShapeDtypeStruct((rows, width), F32),
            jax.ShapeDtypeStruct((tok, width), F32),
            jax.ShapeDtypeStruct((1, mem), F32),
        ),
        in_specs=[vmem] * 4,
        out_specs=[anywhere] * 3,
        scratch_shapes=[pltpu.VMEM((rows, width), F32), dma((rows // 128 + 2,))],
        compiler_params=pltpu.CompilerParams(vmem_limit_bytes=16 * 1024 * 1024),
    )(weighted, right_all, base, fitness)
    return (update, fitness.reshape(mem), base)


def finish(scale, weighted, right_all, base_in, fit_in, update, base, fit, held, sems):
    steps = held.shape[0] // 128
    copies = [
        pltpu.make_async_copy(base_in, base, sems.at[steps]),
        pltpu.make_async_copy(fit_in, fit, sems.at[steps + 1]),
    ]
    copies[0].start()
    copies[1].start()
    for i in range(steps):
        part = slice(i * 128, (i + 1) * 128)
        held[part, :] = lax.dot_general(
            weighted[:, part], right_all[...], (((0,), (0,)), ((), ())), preferred_element_type=F32
        ) * scale
        copies.append(pltpu.make_async_copy(held.at[part], update.at[part], sems.at[i]))
        copies[-1].start()
    for item in copies:
        item.wait()


def chosen(n_pop, n_mp, context, out_weight, *rest):
    tok, width = context.shape
    mem = rest[3].shape[0]
    full = out_weight.shape[1]
    chunks = width // BLK
    if n_mp == 4 and n_pop == 8 and width % BLK == 0 and chunks > 3 and (full // n_pop) % 128 == 0 and tok % 128 == 0 and mem == 16:
        return fused_shards(n_pop, n_mp, context, out_weight, *rest)
    return shards(context, out_weight, *rest)


def solution(mesh):
    in_specs = (
        P("pop", "mp"),
        P("mp", None),
        P("pop", "mp"),
        P("pop", "mp"),
        P(),
        P("pop", None),
        P("pop", None),
        P("pop"),
    )
    out_specs = (P("pop", "mp"), P("pop"), P("pop", "mp"))
    return jax.shard_map(
        functools.partial(chosen, mesh.shape["pop"], mesh.shape["mp"]), mesh=mesh, in_specs=in_specs, out_specs=out_specs, check_vma=False)
```

```python
import functools
import math

import jax
import jax.numpy as jnp
from jax import lax
from jax.experimental import pallas as pl
from jax.experimental.pallas import tpu as pltpu
from jax.sharding import PartitionSpec as P

SIGMA = 1.0
EPSILON = 1e-06


def error_sums(stream, lifted, right_rows, gain_part, target_rows, inverse):
    hidden = stream[:, None, :] + lifted[:, :, None] * right_rows[None, :, :]
    differ = gain_part * hidden * inverse[:, :, None] - target_rows[:, None, :]
    return jnp.sum(differ * differ, axis=(0, 2))


def utility(member_ranks, count_all):
    levels = jnp.arange(count_all).astype(jnp.float32)
    ceiling = math.log(count_all / 2 + 1)
    baseline = jnp.maximum(0.0, ceiling - jnp.log(levels + 1.0))
    shaped = jnp.maximum(0.0, ceiling - jnp.log(member_ranks.astype(jnp.float32) + 1.0))
    return shaped / jnp.sum(baseline) - 1.0 / count_all


def shards(
    context, out_weight, residual, target, norm_gain, left_factors, right_factors, member_ranks
):
    tok_count = context.shape[0]
    shard_width = context.shape[1]
    full_width = out_weight.shape[1]
    factor = SIGMA / math.sqrt(full_width)
    offset = lax.axis_index("mp") * shard_width
    left_cols = lax.dynamic_slice_in_dim(left_factors, offset, shard_width, 1)
    right_cols = lax.dynamic_slice_in_dim(right_factors, offset, shard_width, 1)
    partial_value = jnp.dot(context, out_weight, preferred_element_type=jnp.float32)
    projected = lax.dot_general(
        context, left_cols, (((1,), (1,)), ((), ())), preferred_element_type=jnp.float32
    )
    summed = lax.psum_scatter(
        partial_value.astype(jnp.bfloat16), "mp", scatter_dimension=1, tiled=True
    ).astype(jnp.float32)
    stream = residual.astype(jnp.float32) + summed
    gain_part = lax.dynamic_slice_in_dim(norm_gain, offset, shard_width, 0)
    factor_f = right_cols.astype(jnp.float32)
    crossed = jnp.dot(stream, factor_f.T, precision=lax.Precision.HIGHEST)
    per_token = jnp.sum(stream * stream, axis=1)
    per_member = jnp.sum(factor_f * factor_f, axis=1)
    projected, crossed, per_token, per_member = lax.psum(
        (projected, crossed, per_token, per_member), "mp"
    )
    lifted = factor * projected
    meansq = (
        per_token[:, None] + 2.0 * lifted * crossed + lifted * lifted * per_member[None, :]
    ) / full_width
    inverse = lax.rsqrt(meansq + EPSILON)
    local_error = error_sums(
        stream, lifted, factor_f, gain_part, target.astype(jnp.float32), inverse
    )
    member_total = lax.psum(local_error, "mp")
    fitness = -member_total / (tok_count * full_width)
    everyone = lax.all_gather(fitness, "pop", axis=0, tiled=True)
    count_all = everyone.shape[0]
    average = jnp.mean(everyone)
    centre = everyone - average
    spread = jnp.sqrt(jnp.mean(centre * centre) + 1e-05)
    weight = utility(member_ranks, count_all) + (fitness - average) / spread / count_all
    weighted = (weight[:, None] * left_factors.astype(jnp.float32)).astype(jnp.bfloat16)
    weighted_rows = lax.all_to_all(weighted, "pop", split_axis=1, concat_axis=0, tiled=True)
    right_all = lax.all_gather(right_cols, "pop", axis=0, tiled=True)
    update = lax.dot_general(
        weighted_rows, right_all, (((0,), (0,)), ((), ())), preferred_element_type=jnp.float32
    ) * (math.sqrt(count_all) / SIGMA)
    return (update, fitness, stream)


BLK = 256
LANES = 128
F32 = jnp.float32
BF = jnp.bfloat16


def nt_dot(a, b):
    return lax.dot_general(a, b, (((1,), (1,)), ((), ())), preferred_element_type=F32)


def split_two(x):
    hi = x.astype(BF)
    return hi, (x - hi.astype(F32)).astype(BF)


def halves(parts):
    return jnp.concatenate([piece for part in parts for piece in split_two(part)], axis=1)


def row_picker(count):
    shape = (8, count * 2 * LANES)
    owner = lax.broadcasted_iota(jnp.int32, shape, 1) // (2 * LANES)
    return jnp.where(owner == lax.broadcasted_iota(jnp.int32, shape, 0), 1.0, 0.0).astype(BF)


def flip(index, bits):
    for bit in (1, 2, 4):
        if bits & bit:
            index = index + bit - 2 * bit * ((index // bit) % 2)
    return index


def kernel(
    n_pop, n_mp, ctx_h, w_h, res_h, tgt_h, gain_h, left_h, right_h, ranks_h,
    base, weighted, right_all, fit_out,
    w_v, w_top, ctx, res, tgt, lcols, gain, right, ranks, send, recv, first_v, direct, lall, rall,
    sq_s, sq_a, sq_e, sq_t, lin, lin_in, lin_out, lin_far, post, post_in, fits,
    w_sem, top_sem, near_sem, loc_sem, sent, r_a, r_y, r_b, s_top, r_top, s_a0,
    s_lin, r_lin, s_far, r_far, s_post, r_post, s_l, r_l, s_r, r_r, s_f, r_f, rounds,
):
    tok, width = ctx.shape
    mem = right.shape[0]
    full = right.shape[1]
    rows = full // n_pop
    chunks = width // BLK
    units = width // LANES
    last = units - 1
    pieces = tok // LANES
    upper = tok - 64
    per = mem // 2
    members = mem * n_pop
    p = lax.axis_index("pop")
    q = lax.axis_index("mp")
    y = q // 2
    c = q % 2
    mate = flip(q, 1)
    across = flip(q, 2)
    diagonal = flip(q, 3)
    blocks = (diagonal, across, mate, q)
    other = 2 - 2 * y

    def remote(src, dst, ss, rs, pop, mp):
        return pltpu.make_async_remote_copy(
            src_ref=src, dst_ref=dst, send_sem=ss, recv_sem=rs,
            device_id=(pop, mp), device_id_type=pl.DeviceIdType.MESH,
        )

    def signal(sem, pop, mp):
        pl.semaphore_signal(sem, inc=1, device_id=(pop, mp), device_id_type=pl.DeviceIdType.MESH)

    def wait_for(ref, sem):
        pltpu.make_async_copy(ref, ref, sem).wait()

    def w_copy(s, k):
        start = pl.multiple_of(blocks[s] * width + k * BLK, BLK)
        sem = near_sem if s == 3 else w_sem.at[s, k % 3]
        return pltpu.make_async_copy(w_h.at[:, pl.ds(start, BLK)], w_v.at[s, k], sem)

    def w_first(n):
        block = (other, other + 1, diagonal, across)[n]
        start = pl.multiple_of(block * width + (n // 2) * LANES, LANES)
        return pltpu.make_async_copy(w_h.at[:, pl.ds(start, LANES)], w_top.at[n], top_sem.at[n])

    my_cols = pl.ds(pl.multiple_of(q * width, BLK), width)
    my_rows = pl.ds(pl.multiple_of(p * rows, LANES), rows)
    locals_ = [
        pltpu.make_async_copy(ctx_h.at[0:upper], ctx.at[0:upper], loc_sem.at[0]),
        pltpu.make_async_copy(ctx_h.at[upper:tok], ctx.at[upper:tok], loc_sem.at[1]),
        pltpu.make_async_copy(res_h, res, loc_sem.at[2]),
        pltpu.make_async_copy(tgt_h, tgt, loc_sem.at[3]),
        pltpu.make_async_copy(left_h.at[:, my_cols], lcols, loc_sem.at[4]),
        pltpu.make_async_copy(left_h.at[:, my_rows], lall.at[0], loc_sem.at[5]),
        pltpu.make_async_copy(right_h.at[:, my_cols], rall.at[0], loc_sem.at[6]),
        pltpu.make_async_copy(gain_h, gain, loc_sem.at[7]),
        pltpu.make_async_copy(right_h, right, loc_sem.at[8]),
        pltpu.make_async_copy(ranks_h, ranks, loc_sem.at[9]),
    ]
    w_first(0).start()
    locals_[0].start()
    locals_[1].start()
    w_first(1).start()

    barrier = pltpu.get_barrier_semaphore()
    for peer in (mate, across, diagonal):
        signal(barrier, p, peer)
    for bit in (1, 2, 4):
        signal(barrier, flip(p, bit), q)

    def copy_top():
        return remote(first_v.at[0:upper], direct.at[c], s_top, r_top, p, other)

    def copy_a(first, count, n):
        cols = pl.ds(first, count)
        return remote(send.at[0, cols], recv.at[0, cols], sent, r_a.at[n], p, mate)

    def copy_a0(core):
        if core == 1:
            return remote(first_v.at[upper:tok], recv.at[0, 0, upper:tok], s_a0, r_a.at[0], p, mate)
        return remote(send.at[0, 0], recv.at[0, 0], s_a0, r_a.at[0], p, mate)

    def copy_y0(core):
        part = slice(0 if core == 1 else upper, tok)
        return remote(send.at[1, 0, part], recv.at[1, 0, part], s_a0, r_y.at[0], p, across)

    def copy_y(first, count, n):
        cols = pl.ds(first, count)
        return remote(send.at[1, cols], recv.at[1, cols], sent, r_y.at[n], p, across)

    def copy_end(i):
        part = slice(i * LANES, (i + 1) * LANES)
        return remote(send.at[1, last, part], recv.at[1, last, part], sent, r_y.at[chunks + 1 + i], p, across)

    def copy_b(k):
        cols = pl.ds(2 * k, 2)
        return remote(send.at[2, cols], recv.at[2, cols], sent, r_b, p, mate)

    def copy_l(d):
        peer = flip(p, d)
        cols = pl.ds(pl.multiple_of(peer * rows, LANES), rows)
        return remote(left_h.at[:, cols], lall.at[d], s_l, r_l, peer, q)

    def copy_r(d):
        return remote(right_h.at[:, my_cols], rall.at[d], s_r, r_r, flip(p, d), q)

    def copy_f(n, core):
        target = flip(q, 2 * (n % 2)) - c + core
        return remote(fits.at[0], fits.at[n], s_f.at[core], r_f, flip(p, n // 2), target)

    copy_lin = remote(lin, lin_in, s_lin, r_lin, p, mate)
    copy_far = remote(lin_out, lin_far, s_far, r_far, p, across)

    def copy_post(i, d):
        return remote(post.at[i], post_in.at[d - 1, i], s_post, r_post, p, flip(q, d))

    def split_store(which, k, value):
        send[which, 2 * k] = value[:, :LANES]
        send[which, 2 * k + 1] = value[:, LANES:]

    def product(s, k):
        return jnp.dot(ctx[...], w_v[s, k], preferred_element_type=F32)

    def narrow(n, part):
        return jnp.dot(ctx[part, :], w_top[n], preferred_element_type=F32)

    everything = slice(0, tok)
    with jax.named_scope("load0"):
        locals_[0].wait()
        w_first(0).wait()
    w_first(2).start()
    w_first(3).start()
    first_v[0:upper] = narrow(0, slice(0, upper)).astype(BF)
    with jax.named_scope("barrier"):
        pl.semaphore_wait(barrier, 6)
    copy_top().start()
    signal(rounds.at[0], flip(p, 1), q)
    locals_[1].wait()
    w_first(1).wait()
    second = narrow(1, everything)

    @pl.when(c == 0)
    def _():
        send[0, 0] = second.astype(BF)
        copy_a0(0).start()

    low_rows = narrow(0, slice(upper, tok))
    first_v[upper:tok] = low_rows.astype(BF)

    @pl.when(c == 1)
    def _():
        copy_a0(1).start()

    w_copy(0, 1).start()
    w_copy(1, 1).start()

    for k in (0, 1):
        w_copy(2, k).start()
    for s in range(3):
        w_copy(s, 2).start()
    w_copy(3, 0).start()
    w_first(2).wait()
    send[0, 1] = narrow(2, everything).astype(BF)
    copy_a(1, 1, 1).start()
    w_first(3).wait()
    third = narrow(3, everything)

    with jax.named_scope("wait_a0"):
        @pl.when(c == 0)
        def _():
            copy_a0(1).wait_recv()
            send[1, 0, 0:upper] = first_v[0:upper]
            send[1, 0, upper:tok] = (low_rows + recv[0, 0, upper:tok].astype(F32)).astype(BF)
            copy_y0(0).start()

        @pl.when(c == 1)
        def _():
            copy_a0(0).wait_recv()
            send[1, 0] = (second + recv[0, 0].astype(F32)).astype(BF)
            copy_y0(1).start()

    w_copy(0, 1).wait()
    split_store(0, 1, product(0, 1).astype(BF))
    copy_a(2, 2, 2).start()
    with jax.named_scope("wait_a1"):
        copy_a(1, 1, 1).wait_recv()
    send[1, 1] = (third + recv[0, 1].astype(F32)).astype(BF)
    copy_y(1, 1, 1).start()
    w_copy(2, 0).wait()

    def far(k, carry):
        w_copy(1, k).wait()
        mine = product(1, k)
        with jax.named_scope("wait_a"):
            copy_a(2 * k, 2, k + 1).wait_recv()
        send[1, 2 * k] = (mine[:, :LANES] + recv[0, 2 * k].astype(F32)).astype(BF)
        send[1, 2 * k + 1] = (mine[:, LANES:] + recv[0, 2 * k + 1].astype(F32)).astype(BF)

        @pl.when(k + 1 < chunks)
        def _():
            copy_y(2 * k, 2, k + 1).start()

        @pl.when(k + 1 == chunks)
        def _():
            copy_y(2 * k, 1, k + 1).start()

        @pl.when(k + 2 < chunks)
        def _():
            for s in range(3):
                w_copy(s, k + 2).start()

        w_copy(3, k).start()

        @pl.when(k == 1)
        def _():
            for item in locals_[2:]:
                item.start()
            pl.semaphore_wait(rounds.at[0], 1)
            signal(rounds.at[1], flip(p, 2), q)

        @pl.when(k == 2)
        def _():
            pl.semaphore_wait(rounds.at[1], 1)
            signal(rounds.at[2], flip(p, 4), q)

        @pl.when(k == 3)
        def _():
            pl.semaphore_wait(rounds.at[2], 1)
            for d in range(1, n_pop):
                copy_r(n_pop - d).start()
                copy_l(n_pop - d).start()

        @pl.when(k + 1 < chunks)
        def _():
            w_copy(0, k + 1).wait()
            split_store(0, k + 1, product(0, k + 1).astype(BF))
            copy_a(2 * k + 2, 2, k + 2).start()

        @pl.when(k == 1)
        def _():
            split_store(2, 0, product(2, 0).astype(BF))
            copy_b(0).start()

        w_copy(2, k).wait()
        split_store(2, k, product(2, k).astype(BF))
        copy_b(k).start()
        return carry

    with jax.named_scope("far"):
        lax.fori_loop(1, chunks, far, 0)

    for item in locals_[2:]:
        item.wait()
    wait_for(w_v.at[3], near_sem)

    def near(k, carry):
        cols = pl.ds(pl.multiple_of(k * BLK, BLK), BLK)
        base[:, cols] = product(3, k) + res[:, cols].astype(F32)
        return carry

    with jax.named_scope("near"):
        lax.fori_loop(0, chunks, near, 0)

    def spread(slot, value):
        for j in range(2):
            lin[j, slot * per:(slot + 1) * per, :] = value[j * per:(j + 1) * per]

    with jax.named_scope("early"):
        r_mine = rall[0].astype(F32)
        gr_hi, gr_lo = split_two(r_mine * gain[:, my_cols])
        spread(0, nt_dot(lcols[...], ctx[...]))
        spread(1, nt_dot(gr_hi, tgt[...]) + nt_dot(gr_lo, tgt[...]))
        r_full = right[...].astype(F32)
        gr_full = r_full * gain[...]
        norm_r = jnp.sum(r_full * r_full, axis=1, keepdims=True)
        norm_gr = jnp.sum(gr_full * gr_full, axis=1, keepdims=True)
        for acc in (sq_s, sq_a, sq_e, sq_t):
            acc[...] = jnp.zeros_like(acc)

    def mixed(block, start, size):
        cols = pl.ds(pl.multiple_of(block * width + start, LANES), size)
        r = right[:, cols]
        g = gain[:, cols]
        hi, low = split_two(r.astype(F32) * (g * g))
        return jnp.concatenate([r, hi, low], axis=0)

    def linear(k, carry):
        crossed, crossed_g = carry
        near_rows = mixed(q, k * BLK, BLK)
        far_rows = mixed(across, k * BLK, BLK)
        for h in range(2):
            cols = pl.ds(pl.multiple_of(k * BLK + h * LANES, LANES), LANES)
            part = slice(h * LANES, (h + 1) * LANES)
            u = 2 * k + h
            s = base[:, cols] + recv[2, u].astype(F32)
            base[:, cols] = s
            hi, low = split_two(s)
            both = nt_dot(near_rows[:, part], hi) + nt_dot(near_rows[:, part], low) + nt_dot(far_rows[:, part], send[1, u])
            crossed = crossed + both[0:mem]
            crossed_g = crossed_g + both[mem:2 * mem] + both[2 * mem:3 * mem]
            wide = tgt[:, cols].astype(F32)
            sq_t[...] += wide * wide
        return crossed, crossed_g

    with jax.named_scope("wait_b"):
        wait_for(recv.at[2], r_b)
    with jax.named_scope("linear"):
        top = nt_dot(mixed(other, 0, LANES), first_v[0:upper]) * jnp.where(c == 1, 1.0, 0.0)
        top = jnp.concatenate([top, jnp.zeros((3 * mem, tok - upper), F32)], axis=1)
        carry = (top[0:mem], top[mem:2 * mem] + top[2 * mem:3 * mem])
        crossed, crossed_g = lax.fori_loop(0, chunks, linear, carry)
        spread(2, crossed)
        spread(3, crossed_g)

    @pl.when(c == 0)
    def _():
        copy_lin.start()
        for i in range(pieces):
            copy_end(i).start()

    def arrived(u, part):
        cols = pl.ds(pl.multiple_of(u * LANES, LANES), LANES)
        gain_u = gain[:, pl.ds(pl.multiple_of(q * width + u * LANES, LANES), LANES)]
        s = base[part, cols] + recv[1, u, part].astype(F32)
        base[part, cols] = s
        gs = s * gain_u
        return s * s, gs * gs, gs * tgt[part, cols].astype(F32)

    def settle(u, carry):
        for acc, item in zip((sq_s, sq_a, sq_e), arrived(u, everything)):
            acc[...] += item
        return carry

    with jax.named_scope("wait_y0"):
        @pl.when(c == 0)
        def _():
            wait_for(direct, r_top)
            copy_y0(0).wait_recv()
            recv[1, 0, 0:upper] = jnp.zeros((upper, LANES), BF)
            base[0:upper, 0:LANES] += direct[0].astype(F32) + direct[1].astype(F32)

        @pl.when(c == 1)
        def _():
            copy_y0(1).wait_recv()

    settle(0, 0)
    copy_y(1, 1, 1).wait_recv()
    settle(1, 0)

    @pl.when(c == 1)
    def _():
        with jax.named_scope("wait_lin"):
            copy_lin.wait_recv()
        lin_out[...] = lin[1 - y] + lin_in[1 - y]
        copy_far.start()
        for i in range(pieces):
            copy_end(i).start()

    def settle_chunk(k, carry):
        with jax.named_scope("wait_y"):
            copy_y(2 * k, 2, k + 1).wait_recv()
        settle(2 * k, 0)
        settle(2 * k + 1, 0)
        return carry

    with jax.named_scope("settle"):
        lax.fori_loop(1, chunks - 1, settle_chunk, 0)
    with jax.named_scope("wait_y8"):
        copy_y(last - 1, 1, chunks).wait_recv()
    settle(last - 1, 0)
    before = nt_dot(row_picker(4), halves((sq_s[...], sq_a[...], sq_e[...], sq_t[...])))
    lane = lax.broadcasted_iota(jnp.int32, (1, mem), 1)
    mine_lane = lane // per == y
    ceiling = math.log(members / 2 + 1)
    whole = sum(max(0.0, ceiling - math.log(i + 1.0)) for i in range(members))
    shaped = jnp.maximum(0.0, ceiling - jnp.log(ranks[...].astype(F32) + 1.0)) / whole - 1.0 / members
    picker = row_picker(3)
    for i in range(pieces):
        part = slice(i * LANES, (i + 1) * LANES)
        with jax.named_scope("wait_end"):
            copy_end(i).wait_recv()
        with jax.named_scope("end"):
            post[i] = (before[:, part] + nt_dot(picker, halves(arrived(last, part))))[0:4]

            @pl.when(c == 0)
            def _():
                copy_post(i, 3).start()
                copy_post(i, 1).start()

            @pl.when(c == 1)
            def _():
                copy_post(i, 2).start()

    square = (mem, mem)
    eye = lax.broadcasted_iota(jnp.int32, square, 0) == lax.broadcasted_iota(jnp.int32, square, 1)
    half_of = slice(1, n_pop)
    others = fits.at[pl.ds(1, 2 * n_pop - 1)]

    @pl.when(c == 1)
    def _():
        with jax.named_scope("wait_far"):
            copy_far.wait_recv()
        own = lin[y] + lin_in[y] + lin_far[...]
        mine = jnp.where(y == 1, 1.0, 0.0)

        def my_members(column):
            return column[0:per] + mine * (column[per:mem] - column[0:per])

        lifted = own[0:per] * (SIGMA / math.sqrt(full))
        lifted2 = lifted * lifted
        extra_s = 2.0 * lifted * own[2 * per:3 * per] + lifted2 * my_members(norm_r)
        extra_a = 2.0 * lifted * own[3 * per:4 * per] + lifted2 * my_members(norm_gr)
        extra_e = lifted * own[per:2 * per]
        with jax.named_scope("wait_post"):
            wait_for(post_in, r_post)
        with jax.named_scope("errors"):
            late = jnp.concatenate([post[i] + post_in[0, i] + post_in[1, i] + post_in[2, i] for i in range(pieces)], axis=1)
            meansq = (late[0:1] + extra_s) / full
            inverse = lax.rsqrt(meansq + EPSILON)
            errors = inverse * inverse * (late[1:2] + extra_a) - 2.0 * inverse * (late[2:3] + extra_e) + late[3:4]
            summed = jnp.sum(errors, axis=1, keepdims=True)
            stacked = jnp.concatenate([summed, summed], axis=0)
            total_row = jnp.sum(jnp.where(eye, stacked, 0.0), axis=0, keepdims=True)
            fits[0, 0:1] = jnp.where(mine_lane, total_row, 0.0)
            fits[0, 1:2] = jnp.where(mine_lane, shaped, 0.0)
            for n in range(2 * n_pop - 1, -1, -1):
                copy_f(n, 0).start()
                if n > 0:
                    copy_f(n, 1).start()

    with jax.named_scope("wait_lr"):
        wait_for(lall.at[half_of], r_l)
        wait_for(rall.at[half_of], r_r)
    for d in range(n_pop):
        right_all[d * mem:(d + 1) * mem, :] = rall[d]
    with jax.named_scope("drain"):
        for which in range(3):
            wait_for(send.at[which, 1:units], sent)
        wait_for(send.at[2, 0], sent)
        wait_for(first_v.at[0:upper], s_top)
        wait_for(lall.at[half_of], s_l)
        wait_for(rall.at[half_of], s_r)

        @pl.when(c == 0)
        def _():
            copy_a0(0).wait_send()
            copy_y0(0).wait_send()
            copy_lin.wait_send()
            wait_for(post_in.at[0:2], s_post)
            with jax.named_scope("wait_f"):
                wait_for(fits, r_f)

        @pl.when(c == 1)
        def _():
            copy_a0(1).wait_send()
            copy_y0(1).wait_send()
            copy_far.wait_send()
            wait_for(post_in.at[0], s_post)
            with jax.named_scope("wait_f"):
                wait_for(others, r_f)
            wait_for(fits, s_f.at[0])
            wait_for(others, s_f.at[1])

    with jax.named_scope("weights"):
        rows_of = [fits[2 * d] + fits[2 * d + 1] for d in range(n_pop)]
        all_fit = jnp.concatenate([row[0:1] for row in rows_of], axis=0) * (-1.0 / (tok * full))
        all_shaped = jnp.concatenate([row[1:2] for row in rows_of], axis=0)
        fit_out[...] = all_fit[0:1]
        average = jnp.sum(jnp.sum(all_fit, axis=0, keepdims=True), axis=1, keepdims=True) / members
        centre = all_fit - average
        deviation = jnp.sqrt(jnp.sum(jnp.sum(centre * centre, axis=0, keepdims=True), axis=1, keepdims=True) / members + 1e-05)
        weight = all_shaped + centre / deviation / members
        for d in range(n_pop):
            upright = jnp.sum(jnp.where(eye, weight[d:d + 1], 0.0), axis=1, keepdims=True)
            weighted[d * mem:(d + 1) * mem, :] = (upright * lall[d].astype(F32)).astype(BF)


def in_hbm(x):
    return pltpu.with_memory_space_constraint(x, pltpu.HBM)


def fused_shards(
    n_pop, n_mp, context, out_weight, residual, target, norm_gain, left_factors, right_factors, member_ranks
):
    tok, width = context.shape
    full = out_weight.shape[1]
    mem = left_factors.shape[0]
    rows = full // n_pop
    chunks = width // BLK
    units = width // LANES
    pieces = tok // LANES
    ranks = member_ranks.reshape(1, mem)
    anywhere = pl.BlockSpec(memory_space=pltpu.HBM)
    vmem = pl.BlockSpec(memory_space=pltpu.VMEM)
    dma = pltpu.SemaphoreType.DMA
    acc = pltpu.VMEM((tok, LANES), F32)
    group = (2 * mem, tok)
    base, weighted, right_all, fitness = pl.pallas_call(
        functools.partial(kernel, n_pop, n_mp),
        name="es_step",
        out_shape=(
            jax.ShapeDtypeStruct((tok, width), F32),
            jax.ShapeDtypeStruct((n_pop * mem, rows), BF),
            jax.ShapeDtypeStruct((n_pop * mem, width), BF),
            jax.ShapeDtypeStruct((1, mem), F32),
        ),
        in_specs=[anywhere] * 8,
        out_specs=[vmem] * 4,
        scratch_shapes=[
            pltpu.VMEM((4, chunks, width, BLK), BF),
            pltpu.VMEM((4, width, LANES), BF),
            pltpu.VMEM((tok, width), BF),
            pltpu.VMEM((tok, width), BF),
            pltpu.VMEM((tok, width), BF),
            pltpu.VMEM((mem, width), BF),
            pltpu.VMEM((1, full), F32),
            pltpu.VMEM((mem, full), BF),
            pltpu.VMEM((1, mem), jnp.int32),
            pltpu.VMEM((3, units, tok, LANES), BF),
            pltpu.VMEM((3, units, tok, LANES), BF),
            pltpu.VMEM((tok, LANES), BF),
            pltpu.VMEM((2, tok - 64, LANES), BF),
            pltpu.VMEM((n_pop, mem, rows), BF),
            pltpu.VMEM((n_pop, mem, width), BF),
            acc, acc, acc, acc,
            pltpu.VMEM((2,) + group, F32),
            pltpu.VMEM((2,) + group, F32),
            pltpu.VMEM(group, F32),
            pltpu.VMEM(group, F32),
            pltpu.VMEM((pieces, 4, LANES), F32),
            pltpu.VMEM((n_mp - 1, pieces, 4, LANES), F32),
            pltpu.VMEM((2 * n_pop, 2, mem), F32),
            dma((3, 3)),
            dma((4,)),
            dma,
            dma((10,)),
            dma,
            dma((chunks + 1,)),
            dma((chunks + 1 + pieces,)),
        ]
        + [dma] * 14
        + [dma((2,)), dma]
        + [pltpu.SemaphoreType.REGULAR((3,))],
        compiler_params=pltpu.CompilerParams(
            collective_id=0, has_side_effects=True, vmem_limit_bytes=48 * 1024 * 1024
        ),
    )(
        *map(in_hbm, (
            context, out_weight, residual, target, norm_gain.reshape(1, full), left_factors,
            right_factors, ranks,
        ))
    )
    count_all = n_pop * mem
    update, base, fitness = pl.pallas_call(
        functools.partial(finish, math.sqrt(count_all) / SIGMA),
        name="es_update",
        out_shape=(
            jax.ShapeDtypeStruct((rows, width), F32),
            jax.ShapeDtypeStruct((tok, width), F32),
            jax.ShapeDtypeStruct((1, mem), F32),
        ),
        in_specs=[vmem] * 4,
        out_specs=[anywhere] * 3,
        scratch_shapes=[pltpu.VMEM((rows, width), F32), dma((rows // 128 + 2,))],
        compiler_params=pltpu.CompilerParams(vmem_limit_bytes=16 * 1024 * 1024),
    )(weighted, right_all, base, fitness)
    return (update, fitness.reshape(mem), base)


def finish(scale, weighted, right_all, base_in, fit_in, update, base, fit, held, sems):
    steps = held.shape[0] // 128
    copies = [
        pltpu.make_async_copy(base_in, base, sems.at[steps]),
        pltpu.make_async_copy(fit_in, fit, sems.at[steps + 1]),
    ]
    copies[0].start()
    copies[1].start()
    for i in range(steps):
        part = slice(i * 128, (i + 1) * 128)
        held[part, :] = lax.dot_general(
            weighted[:, part], right_all[...], (((0,), (0,)), ((), ())), preferred_element_type=F32
        ) * scale
        copies.append(pltpu.make_async_copy(held.at[part], update.at[part], sems.at[i]))
        copies[-1].start()
    for item in copies:
        item.wait()


def chosen(n_pop, n_mp, context, out_weight, *rest):
    tok, width = context.shape
    mem = rest[3].shape[0]
    full = out_weight.shape[1]
    chunks = width // BLK
    if n_mp == 4 and n_pop == 8 and width % BLK == 0 and chunks > 3 and (full // n_pop) % 128 == 0 and tok % 128 == 0 and mem == 16:
        return fused_shards(n_pop, n_mp, context, out_weight, *rest)
    return shards(context, out_weight, *rest)


def solution(mesh):
    in_specs = (
        P("pop", "mp"),
        P("mp", None),
        P("pop", "mp"),
        P("pop", "mp"),
        P(),
        P("pop", None),
        P("pop", None),
        P("pop"),
    )
    out_specs = (P("pop", "mp"), P("pop"), P("pop", "mp"))
    return jax.shard_map(
        functools.partial(chosen, mesh.shape["pop"], mesh.shape["mp"]), mesh=mesh, in_specs=in_specs, out_specs=out_specs, check_vma=False)
```

```python
import functools
import math

import jax
import jax.numpy as jnp
from jax import lax
from jax.experimental import pallas as pl
from jax.experimental.pallas import tpu as pltpu
from jax.sharding import PartitionSpec as P

SIGMA = 1.0
EPSILON = 1e-06


def error_sums(stream, lifted, right_rows, gain_part, target_rows, inverse):
    hidden = stream[:, None, :] + lifted[:, :, None] * right_rows[None, :, :]
    differ = gain_part * hidden * inverse[:, :, None] - target_rows[:, None, :]
    return jnp.sum(differ * differ, axis=(0, 2))


def utility(member_ranks, count_all):
    levels = jnp.arange(count_all).astype(jnp.float32)
    ceiling = math.log(count_all / 2 + 1)
    baseline = jnp.maximum(0.0, ceiling - jnp.log(levels + 1.0))
    shaped = jnp.maximum(0.0, ceiling - jnp.log(member_ranks.astype(jnp.float32) + 1.0))
    return shaped / jnp.sum(baseline) - 1.0 / count_all


def shards(
    context, out_weight, residual, target, norm_gain, left_factors, right_factors, member_ranks
):
    tok_count = context.shape[0]
    shard_width = context.shape[1]
    full_width = out_weight.shape[1]
    factor = SIGMA / math.sqrt(full_width)
    offset = lax.axis_index("mp") * shard_width
    left_cols = lax.dynamic_slice_in_dim(left_factors, offset, shard_width, 1)
    right_cols = lax.dynamic_slice_in_dim(right_factors, offset, shard_width, 1)
    partial_value = jnp.dot(context, out_weight, preferred_element_type=jnp.float32)
    projected = lax.dot_general(
        context, left_cols, (((1,), (1,)), ((), ())), preferred_element_type=jnp.float32
    )
    summed = lax.psum_scatter(
        partial_value.astype(jnp.bfloat16), "mp", scatter_dimension=1, tiled=True
    ).astype(jnp.float32)
    stream = residual.astype(jnp.float32) + summed
    gain_part = lax.dynamic_slice_in_dim(norm_gain, offset, shard_width, 0)
    factor_f = right_cols.astype(jnp.float32)
    crossed = jnp.dot(stream, factor_f.T, precision=lax.Precision.HIGHEST)
    per_token = jnp.sum(stream * stream, axis=1)
    per_member = jnp.sum(factor_f * factor_f, axis=1)
    projected, crossed, per_token, per_member = lax.psum(
        (projected, crossed, per_token, per_member), "mp"
    )
    lifted = factor * projected
    meansq = (
        per_token[:, None] + 2.0 * lifted * crossed + lifted * lifted * per_member[None, :]
    ) / full_width
    inverse = lax.rsqrt(meansq + EPSILON)
    local_error = error_sums(
        stream, lifted, factor_f, gain_part, target.astype(jnp.float32), inverse
    )
    member_total = lax.psum(local_error, "mp")
    fitness = -member_total / (tok_count * full_width)
    everyone = lax.all_gather(fitness, "pop", axis=0, tiled=True)
    count_all = everyone.shape[0]
    average = jnp.mean(everyone)
    centre = everyone - average
    spread = jnp.sqrt(jnp.mean(centre * centre) + 1e-05)
    weight = utility(member_ranks, count_all) + (fitness - average) / spread / count_all
    weighted = (weight[:, None] * left_factors.astype(jnp.float32)).astype(jnp.bfloat16)
    weighted_rows = lax.all_to_all(weighted, "pop", split_axis=1, concat_axis=0, tiled=True)
    right_all = lax.all_gather(right_cols, "pop", axis=0, tiled=True)
    update = lax.dot_general(
        weighted_rows, right_all, (((0,), (0,)), ((), ())), preferred_element_type=jnp.float32
    ) * (math.sqrt(count_all) / SIGMA)
    return (update, fitness, stream)


BLK = 256
LANES = 128
F32 = jnp.float32
BF = jnp.bfloat16


def nt_dot(a, b):
    return lax.dot_general(a, b, (((1,), (1,)), ((), ())), preferred_element_type=F32)


def split_two(x):
    hi = x.astype(BF)
    return hi, (x - hi.astype(F32)).astype(BF)


def halves(parts):
    return jnp.concatenate([piece for part in parts for piece in split_two(part)], axis=1)


def row_picker(count):
    shape = (8, count * 2 * LANES)
    owner = lax.broadcasted_iota(jnp.int32, shape, 1) // (2 * LANES)
    return jnp.where(owner == lax.broadcasted_iota(jnp.int32, shape, 0), 1.0, 0.0).astype(BF)


def flip(index, bits):
    for bit in (1, 2, 4):
        if bits & bit:
            index = index + bit - 2 * bit * ((index // bit) % 2)
    return index


def kernel(
    n_pop, n_mp, ctx_h, w_h, res_h, tgt_h, gain_h, left_h, right_h, ranks_h,
    base, weighted, right_all, fit_out,
    w_v, ctx, res, tgt, lcols, gain, right, ranks, send, recv, first_v, direct, lall, rall,
    sq_s, sq_a, sq_e, sq_t, lin, lin_in, lin_out, lin_far, post, post_in, fits,
    w_sem, top_sem, near_sem, loc_sem, sent, r_a, r_y, r_b, r_top, r_lin, r_far, r_post, r_l, r_r, r_f, rounds,
):
    tok, width = ctx.shape
    mem = right.shape[0]
    full = right.shape[1]
    rows = full // n_pop
    chunks = width // BLK
    units = width // LANES
    last = units - 1
    pieces = tok // LANES
    upper = LANES
    per = mem // 2
    members = mem * n_pop
    p = lax.axis_index("pop")
    q = lax.axis_index("mp")
    y = q // 2
    c = q % 2
    mate = flip(q, 1)
    across = flip(q, 2)
    diagonal = flip(q, 3)
    blocks = (diagonal, across, mate, q)
    other = 2 - 2 * y

    def remote(src, dst, ss, rs, pop, mp):
        return pltpu.make_async_remote_copy(
            src_ref=src, dst_ref=dst, send_sem=ss, recv_sem=rs,
            device_id=(pop, mp), device_id_type=pl.DeviceIdType.MESH,
        )

    def signal(sem, pop, mp):
        pl.semaphore_signal(sem, inc=1, device_id=(pop, mp), device_id_type=pl.DeviceIdType.MESH)

    def wait_for(ref, sem):
        pltpu.make_async_copy(ref, ref, sem).wait()

    def w_copy(s, k, sem):
        start = pl.multiple_of(blocks[s] * width + k * BLK, BLK)
        return pltpu.make_async_copy(w_h.at[:, pl.ds(start, BLK)], w_v.at[s, k], sem)

    def w_first(n):
        start = pl.multiple_of((other + n) * width, BLK)
        slot = 1 - c if n == 0 else c
        return pltpu.make_async_copy(w_h.at[:, pl.ds(start, BLK)], w_v.at[slot, 0], top_sem.at[n])

    def near_copy(k):
        return w_copy(3, k, near_sem)

    def w_step(k, more):
        steps = [(1, k), (2, k)] if isinstance(k, jax.Array) or k > 0 else [(2, k)]
        if more:
            steps.append((0, k + 1))
        return [w_copy(s, i, w_sem.at[k % 2]) for s, i in steps]

    my_cols = pl.ds(pl.multiple_of(q * width, BLK), width)
    my_rows = pl.ds(pl.multiple_of(p * rows, LANES), rows)
    locals_ = [
        pltpu.make_async_copy(ctx_h.at[0:upper], ctx.at[0:upper], loc_sem.at[0]),
        pltpu.make_async_copy(ctx_h.at[upper:tok], ctx.at[upper:tok], loc_sem.at[1]),
        pltpu.make_async_copy(res_h, res, loc_sem.at[2]),
        pltpu.make_async_copy(tgt_h, tgt, loc_sem.at[2]),
        pltpu.make_async_copy(left_h.at[:, my_cols], lcols, loc_sem.at[2]),
        pltpu.make_async_copy(left_h.at[:, my_rows], lall.at[0], loc_sem.at[2]),
        pltpu.make_async_copy(right_h.at[:, my_cols], rall.at[0], loc_sem.at[2]),
        pltpu.make_async_copy(gain_h, gain, loc_sem.at[2]),
        pltpu.make_async_copy(right_h, right, loc_sem.at[2]),
        pltpu.make_async_copy(ranks_h, ranks, loc_sem.at[2]),
    ]
    locals_[0].start()
    w_first(0).start()
    locals_[1].start()
    w_first(1).start()

    barrier = pltpu.get_barrier_semaphore()
    for peer in (mate, across, diagonal):
        signal(barrier, p, peer)
    for bit in (1, 2, 4):
        signal(barrier, flip(p, bit), q)

    copy_top = remote(first_v, direct.at[c], sent, r_top, p, other)

    def copy_a(k):
        cols = pl.ds(2 * k, 2)
        return remote(send.at[0, cols], recv.at[0, cols], sent, r_a.at[pieces + k - 1], p, mate)

    def strip(i):
        return pl.ds(i * LANES, LANES)

    def copy_a0(i):
        return remote(send.at[0, 0:2, strip(i)], recv.at[0, 0:2, strip(i)], sent, r_a.at[i], p, mate)

    def copy_y0(i):
        return remote(send.at[1, 0:2, strip(i)], recv.at[1, 0:2, strip(i)], sent, r_y.at[i], p, across)

    def copy_y(k, count=2):
        cols = pl.ds(2 * k, count)
        return remote(send.at[1, cols], recv.at[1, cols], sent, r_y.at[pieces + k - 1], p, across)

    def copy_end(i):
        part = slice(i * LANES, (i + 1) * LANES)
        return remote(send.at[1, last, part], recv.at[1, last, part], sent, r_y.at[pieces + chunks - 1 + i], p, across)

    def copy_b(k):
        cols = pl.ds(2 * k, 2)
        return remote(send.at[2, cols], recv.at[2, cols], sent, r_b, p, mate)

    def copy_l(d):
        peer = flip(p, d)
        cols = pl.ds(pl.multiple_of(peer * rows, LANES), rows)
        return remote(left_h.at[:, cols], lall.at[d], sent, r_l, peer, q)

    def copy_r(d):
        return remote(right_h.at[:, my_cols], rall.at[d], sent, r_r, flip(p, d), q)

    def copy_f(n, core):
        target = flip(q, 2 * (n % 2)) - c + core
        return remote(fits.at[0], fits.at[n], sent, r_f, flip(p, n // 2), target)

    copy_lin = remote(lin, lin_in, sent, r_lin, p, mate)
    copy_far = remote(lin_out, lin_far, sent, r_far, p, across)

    def copy_post(i, d):
        return remote(post.at[i], post_in.at[d - 1, i], sent, r_post, p, flip(q, d))

    def split_store(which, k, value):
        send[which, 2 * k] = value[:, :LANES]
        send[which, 2 * k + 1] = value[:, LANES:]

    def product(s, k):
        return jnp.dot(ctx[...], w_v[s, k], preferred_element_type=F32)

    everything = slice(0, tok)
    with jax.named_scope("load0"):
        locals_[0].wait()
        w_first(0).wait()
    top = jnp.dot(ctx[0:upper, :], w_v[1 - c, 0], preferred_element_type=F32).astype(BF)
    first_v[0] = top[:, :LANES]
    first_v[1] = top[:, LANES:]
    with jax.named_scope("barrier"):
        pl.semaphore_wait(barrier, 6)
    copy_top.start()
    signal(rounds.at[0], flip(p, 1), q)
    for item in w_step(0, True):
        item.start()
    locals_[1].wait()
    w_first(1).wait()

    def strip_product(s, i):
        rows_i = slice(i * LANES, (i + 1) * LANES)
        return jnp.dot(ctx[rows_i, :], w_v[s, 0], preferred_element_type=F32)

    def give(i):
        value = strip_product(0, i).astype(BF)
        send[0, 0, strip(i)] = value[:, :LANES]
        send[0, 1, strip(i)] = value[:, LANES:]
        copy_a0(i).start()

    def pass_on(i, value):
        send[1, 0, strip(i)] = (value[:, :LANES] + recv[0, 0, strip(i)].astype(F32)).astype(BF)
        send[1, 1, strip(i)] = (value[:, LANES:] + recv[0, 1, strip(i)].astype(F32)).astype(BF)
        copy_y0(i).start()

    for i in range(1, pieces):
        give(i)

    @pl.when(c == 0)
    def _():
        give(0)
        send[1, 0, strip(0)] = first_v[0]
        send[1, 1, strip(0)] = first_v[1]

    for item in w_step(1, True):
        item.start()
    near_copy(0).start()
    mine = [strip_product(1, i) for i in range(1, pieces)]
    with jax.named_scope("wait_a0"):
        for i in range(1, pieces):
            copy_a0(i).wait_recv()
            pass_on(i, mine[i - 1])

    @pl.when(c == 1)
    def _():
        value = strip_product(1, 0)
        copy_a0(0).wait_recv()
        pass_on(0, value)

    for item in w_step(0, True):
        item.wait()
    split_store(0, 1, product(0, 1).astype(BF))
    copy_a(1).start()
    for item in w_step(2, True):
        item.start()

    def far(k, carry):
        for item in w_step(k, False):
            item.wait()

        @pl.when(k + 1 < chunks)
        def _():
            w_copy(0, k + 1, w_sem.at[k % 2]).wait()

        mine = product(1, k)
        with jax.named_scope("wait_a"):
            copy_a(k).wait_recv()
        send[1, 2 * k] = (mine[:, :LANES] + recv[0, 2 * k].astype(F32)).astype(BF)
        send[1, 2 * k + 1] = (mine[:, LANES:] + recv[0, 2 * k + 1].astype(F32)).astype(BF)

        @pl.when(k + 1 < chunks)
        def _():
            copy_y(k).start()

        @pl.when(k + 1 == chunks)
        def _():
            copy_y(k, 1).start()

        @pl.when(k + 2 < chunks)
        def _():
            for item in w_step(k + 2, False):
                item.start()

        @pl.when(k + 3 < chunks)
        def _():
            w_copy(0, k + 3, w_sem.at[k % 2]).start()

        near_copy(k).start()

        @pl.when(k == 1)
        def _():
            for item in locals_[2:]:
                item.start()
            pl.semaphore_wait(rounds.at[0], 1)
            signal(rounds.at[1], flip(p, 2), q)

        @pl.when(k == 2)
        def _():
            pl.semaphore_wait(rounds.at[1], 1)
            signal(rounds.at[2], flip(p, 4), q)

        @pl.when(k == 3)
        def _():
            pl.semaphore_wait(rounds.at[2], 1)
            for d in range(1, n_pop):
                copy_r(n_pop - d).start()
                copy_l(n_pop - d).start()

        @pl.when(k + 1 < chunks)
        def _():
            split_store(0, k + 1, product(0, k + 1).astype(BF))
            copy_a(k + 1).start()

        @pl.when(k == 1)
        def _():
            split_store(2, 0, product(2, 0).astype(BF))
            copy_b(0).start()

        split_store(2, k, product(2, k).astype(BF))
        copy_b(k).start()
        return carry

    with jax.named_scope("far"):
        lax.fori_loop(1, chunks, far, 0)

    for item in locals_[2:]:
        item.wait()
    wait_for(w_v.at[3], near_sem)

    def near(k, carry):
        cols = pl.ds(pl.multiple_of(k * BLK, BLK), BLK)
        base[:, cols] = product(3, k) + res[:, cols].astype(F32)
        return carry

    with jax.named_scope("near"):
        lax.fori_loop(0, chunks, near, 0)

    def spread(slot, value):
        for j in range(2):
            lin[j, slot * per:(slot + 1) * per, :] = value[j * per:(j + 1) * per]

    with jax.named_scope("early"):
        r_mine = rall[0].astype(F32)
        gr_hi, gr_lo = split_two(r_mine * gain[:, my_cols])
        spread(0, nt_dot(lcols[...], ctx[...]))
        spread(1, nt_dot(gr_hi, tgt[...]) + nt_dot(gr_lo, tgt[...]))
        r_full = right[...].astype(F32)
        gr_full = r_full * gain[...]
        norm_r = jnp.sum(r_full * r_full, axis=1, keepdims=True)
        norm_gr = jnp.sum(gr_full * gr_full, axis=1, keepdims=True)
        for acc in (sq_s, sq_a, sq_e, sq_t):
            acc[...] = jnp.zeros_like(acc)

    def mixed(block, start, size):
        cols = pl.ds(pl.multiple_of(block * width + start, LANES), size)
        r = right[:, cols]
        g = gain[:, cols]
        hi, low = split_two(r.astype(F32) * (g * g))
        return jnp.concatenate([r, hi, low], axis=0)

    def linear(k, carry):
        crossed, crossed_g = carry
        near_rows = mixed(q, k * BLK, BLK)
        far_rows = mixed(across, k * BLK, BLK)
        for h in range(2):
            cols = pl.ds(pl.multiple_of(k * BLK + h * LANES, LANES), LANES)
            part = slice(h * LANES, (h + 1) * LANES)
            u = 2 * k + h
            s = base[:, cols] + recv[2, u].astype(F32)
            base[:, cols] = s
            hi, low = split_two(s)
            both = nt_dot(near_rows[:, part], hi) + nt_dot(near_rows[:, part], low) + nt_dot(far_rows[:, part], send[1, u])
            crossed = crossed + both[0:mem]
            crossed_g = crossed_g + both[mem:2 * mem] + both[2 * mem:3 * mem]
            wide = tgt[:, cols].astype(F32)
            sq_t[...] += wide * wide
        return crossed, crossed_g

    with jax.named_scope("wait_b"):
        wait_for(recv.at[2], r_b)
    with jax.named_scope("linear"):
        top_rows = mixed(other, 0, BLK)
        top = nt_dot(top_rows[:, :LANES], first_v[0]) + nt_dot(top_rows[:, LANES:], first_v[1])
        top = top * jnp.where(c == 1, 1.0, 0.0)
        top = jnp.concatenate([top, jnp.zeros((3 * mem, tok - upper), F32)], axis=1)
        carry = (top[0:mem], top[mem:2 * mem] + top[2 * mem:3 * mem])
        crossed, crossed_g = lax.fori_loop(0, chunks, linear, carry)
        spread(2, crossed)
        spread(3, crossed_g)

    @pl.when(c == 0)
    def _():
        copy_lin.start()
        for i in range(pieces):
            copy_end(i).start()

    def arrived(u, part):
        cols = pl.ds(pl.multiple_of(u * LANES, LANES), LANES)
        gain_u = gain[:, pl.ds(pl.multiple_of(q * width + u * LANES, LANES), LANES)]
        s = base[part, cols] + recv[1, u, part].astype(F32)
        base[part, cols] = s
        gs = s * gain_u
        return s * s, gs * gs, gs * tgt[part, cols].astype(F32)

    def settle(u, carry):
        for acc, item in zip((sq_s, sq_a, sq_e), arrived(u, everything)):
            acc[...] += item
        return carry

    with jax.named_scope("wait_y0"):
        for i in range(1, pieces):
            copy_y0(i).wait_recv()

        @pl.when(c == 0)
        def _():
            wait_for(direct, r_top)
            for u in range(2):
                recv[1, u, strip(0)] = jnp.zeros((upper, LANES), BF)
                base[0:upper, u * LANES:(u + 1) * LANES] += direct[0, u].astype(F32) + direct[1, u].astype(F32)

        @pl.when(c == 1)
        def _():
            copy_y0(0).wait_recv()

    lax.fori_loop(0, 2, settle, 0)

    @pl.when(c == 1)
    def _():
        with jax.named_scope("wait_lin"):
            copy_lin.wait_recv()
        lin_out[...] = lin[1 - y] + lin_in[1 - y]
        copy_far.start()
        for i in range(pieces):
            copy_end(i).start()

    def settle_chunk(k, carry):
        with jax.named_scope("wait_y"):
            copy_y(k).wait_recv()
        settle(2 * k, 0)
        settle(2 * k + 1, 0)
        return carry

    with jax.named_scope("settle"):
        lax.fori_loop(1, chunks - 1, settle_chunk, 0)
    with jax.named_scope("wait_y8"):
        copy_y(chunks - 1, 1).wait_recv()
    settle(last - 1, 0)
    before = nt_dot(row_picker(4), halves((sq_s[...], sq_a[...], sq_e[...], sq_t[...])))
    lane = lax.broadcasted_iota(jnp.int32, (1, mem), 1)
    mine_lane = lane // per == y
    ceiling = math.log(members / 2 + 1)
    whole = sum(max(0.0, ceiling - math.log(i + 1.0)) for i in range(members))
    shaped = jnp.maximum(0.0, ceiling - jnp.log(ranks[...].astype(F32) + 1.0)) / whole - 1.0 / members
    picker = row_picker(3)
    for i in range(pieces):
        part = slice(i * LANES, (i + 1) * LANES)
        with jax.named_scope("wait_end"):
            copy_end(i).wait_recv()
        with jax.named_scope("end"):
            post[i] = (before[:, part] + nt_dot(picker, halves(arrived(last, part))))[0:4]

            @pl.when(c == 0)
            def _():
                copy_post(i, 3).start()
                copy_post(i, 1).start()

            @pl.when(c == 1)
            def _():
                copy_post(i, 2).start()

    square = (mem, mem)
    eye = lax.broadcasted_iota(jnp.int32, square, 0) == lax.broadcasted_iota(jnp.int32, square, 1)
    half_of = slice(1, n_pop)
    others = fits.at[pl.ds(1, 2 * n_pop - 1)]

    @pl.when(c == 1)
    def _():
        with jax.named_scope("wait_far"):
            copy_far.wait_recv()
        own = lin[y] + lin_in[y] + lin_far[...]
        mine = jnp.where(y == 1, 1.0, 0.0)

        def my_members(column):
            return column[0:per] + mine * (column[per:mem] - column[0:per])

        lifted = own[0:per] * (SIGMA / math.sqrt(full))
        lifted2 = lifted * lifted
        extra_s = 2.0 * lifted * own[2 * per:3 * per] + lifted2 * my_members(norm_r)
        extra_a = 2.0 * lifted * own[3 * per:4 * per] + lifted2 * my_members(norm_gr)
        extra_e = lifted * own[per:2 * per]
        with jax.named_scope("wait_post"):
            wait_for(post_in, r_post)
        with jax.named_scope("errors"):
            late = jnp.concatenate([post[i] + post_in[0, i] + post_in[1, i] + post_in[2, i] for i in range(pieces)], axis=1)
            meansq = (late[0:1] + extra_s) / full
            inverse = lax.rsqrt(meansq + EPSILON)
            errors = inverse * inverse * (late[1:2] + extra_a) - 2.0 * inverse * (late[2:3] + extra_e) + late[3:4]
            summed = jnp.sum(errors, axis=1, keepdims=True)
            stacked = jnp.concatenate([summed, summed], axis=0)
            total_row = jnp.sum(jnp.where(eye, stacked, 0.0), axis=0, keepdims=True)
            fits[0, 0:1] = jnp.where(mine_lane, total_row, 0.0)
            fits[0, 1:2] = jnp.where(mine_lane, shaped, 0.0)
            for n in range(2 * n_pop - 1, -1, -1):
                copy_f(n, 0).start()
                if n > 0:
                    copy_f(n, 1).start()

    with jax.named_scope("wait_lr"):
        wait_for(lall.at[half_of], r_l)
        wait_for(rall.at[half_of], r_r)
    for d in range(n_pop):
        right_all[d * mem:(d + 1) * mem, :] = rall[d]

    @pl.when(c == 0)
    def _():
        with jax.named_scope("wait_f"):
            wait_for(fits, r_f)

    @pl.when(c == 1)
    def _():
        with jax.named_scope("wait_f"):
            wait_for(others, r_f)

    with jax.named_scope("weights"):
        rows_of = [fits[2 * d] + fits[2 * d + 1] for d in range(n_pop)]
        all_fit = jnp.concatenate([row[0:1] for row in rows_of], axis=0) * (-1.0 / (tok * full))
        all_shaped = jnp.concatenate([row[1:2] for row in rows_of], axis=0)
        fit_out[...] = all_fit[0:1]
        average = jnp.sum(jnp.sum(all_fit, axis=0, keepdims=True), axis=1, keepdims=True) / members
        centre = all_fit - average
        deviation = jnp.sqrt(jnp.sum(jnp.sum(centre * centre, axis=0, keepdims=True), axis=1, keepdims=True) / members + 1e-05)
        weight = all_shaped + centre / deviation / members
        for d in range(n_pop):
            upright = jnp.sum(jnp.where(eye, weight[d:d + 1], 0.0), axis=1, keepdims=True)
            weighted[d * mem:(d + 1) * mem, :] = (upright * lall[d].astype(F32)).astype(BF)

    for which in range(2):
        wait_for(send.at[which, 2:units], sent)
    wait_for(send.at[2], sent)
    wait_for(first_v, sent)
    wait_for(lall.at[half_of], sent)
    wait_for(rall.at[half_of], sent)
    for core in range(2):
        @pl.when(c == core)
        def _(core=core):
            for i in range(core, pieces):
                copy_a0(i).wait_send()
            for i in range(1 - core, pieces):
                copy_y0(i).wait_send()
            if core == 0:
                copy_lin.wait_send()
                wait_for(post_in.at[0:2], sent)
            else:
                copy_far.wait_send()
                wait_for(post_in.at[0], sent)
                wait_for(fits, sent)
                wait_for(others, sent)


def in_hbm(x):
    return pltpu.with_memory_space_constraint(x, pltpu.HBM)


def fused_shards(
    n_pop, n_mp, context, out_weight, residual, target, norm_gain, left_factors, right_factors, member_ranks
):
    tok, width = context.shape
    full = out_weight.shape[1]
    mem = left_factors.shape[0]
    rows = full // n_pop
    chunks = width // BLK
    units = width // LANES
    pieces = tok // LANES
    ranks = member_ranks.reshape(1, mem)
    anywhere = pl.BlockSpec(memory_space=pltpu.HBM)
    vmem = pl.BlockSpec(memory_space=pltpu.VMEM)
    dma = pltpu.SemaphoreType.DMA
    acc = pltpu.VMEM((tok, LANES), F32)
    group = (2 * mem, tok)
    base, weighted, right_all, fitness = pl.pallas_call(
        functools.partial(kernel, n_pop, n_mp),
        name="es_step",
        out_shape=(
            jax.ShapeDtypeStruct((tok, width), F32),
            jax.ShapeDtypeStruct((n_pop * mem, rows), BF),
            jax.ShapeDtypeStruct((n_pop * mem, width), BF),
            jax.ShapeDtypeStruct((1, mem), F32),
        ),
        in_specs=[anywhere] * 8,
        out_specs=[vmem] * 4,
        scratch_shapes=[
            pltpu.VMEM((4, chunks, width, BLK), BF),
            pltpu.VMEM((tok, width), BF),
            pltpu.VMEM((tok, width), BF),
            pltpu.VMEM((tok, width), BF),
            pltpu.VMEM((mem, width), BF),
            pltpu.VMEM((1, full), F32),
            pltpu.VMEM((mem, full), BF),
            pltpu.VMEM((1, mem), jnp.int32),
            pltpu.VMEM((3, units, tok, LANES), BF),
            pltpu.VMEM((3, units, tok, LANES), BF),
            pltpu.VMEM((2, LANES, LANES), BF),
            pltpu.VMEM((2, 2, LANES, LANES), BF),
            pltpu.VMEM((n_pop, mem, rows), BF),
            pltpu.VMEM((n_pop, mem, width), BF),
            acc, acc, acc, acc,
            pltpu.VMEM((2,) + group, F32),
            pltpu.VMEM((2,) + group, F32),
            pltpu.VMEM(group, F32),
            pltpu.VMEM(group, F32),
            pltpu.VMEM((pieces, 4, LANES), F32),
            pltpu.VMEM((n_mp - 1, pieces, 4, LANES), F32),
            pltpu.VMEM((2 * n_pop, 2, mem), F32),
            dma((2,)),
            dma((2,)),
            dma,
            dma((3,)),
            dma,
            dma((chunks - 1 + pieces,)),
            dma((chunks - 1 + 2 * pieces,)),
        ]
        + [dma] * 8
        + [pltpu.SemaphoreType.REGULAR((3,))],
        compiler_params=pltpu.CompilerParams(
            collective_id=0, has_side_effects=True, vmem_limit_bytes=48 * 1024 * 1024
        ),
    )(
        *map(in_hbm, (
            context, out_weight, residual, target, norm_gain.reshape(1, full), left_factors,
            right_factors, ranks,
        ))
    )
    count_all = n_pop * mem
    update, base, fitness = pl.pallas_call(
        functools.partial(finish, math.sqrt(count_all) / SIGMA),
        name="es_update",
        out_shape=(
            jax.ShapeDtypeStruct((rows, width), F32),
            jax.ShapeDtypeStruct((tok, width), F32),
            jax.ShapeDtypeStruct((1, mem), F32),
        ),
        in_specs=[vmem] * 4,
        out_specs=[anywhere] * 3,
        scratch_shapes=[pltpu.VMEM((rows, width), F32), dma((rows // 128 + 2,))],
        compiler_params=pltpu.CompilerParams(vmem_limit_bytes=16 * 1024 * 1024),
    )(weighted, right_all, base, fitness)
    return (update, fitness.reshape(mem), base)


def finish(scale, weighted, right_all, base_in, fit_in, update, base, fit, held, sems):
    steps = held.shape[0] // 128
    copies = [
        pltpu.make_async_copy(base_in, base, sems.at[steps]),
        pltpu.make_async_copy(fit_in, fit, sems.at[steps + 1]),
    ]
    copies[0].start()
    copies[1].start()
    for i in range(steps):
        part = slice(i * 128, (i + 1) * 128)
        held[part, :] = lax.dot_general(
            weighted[:, part], right_all[...], (((0,), (0,)), ((), ())), preferred_element_type=F32
        ) * scale
        copies.append(pltpu.make_async_copy(held.at[part], update.at[part], sems.at[i]))
        copies[-1].start()
    for item in copies:
        item.wait()


def chosen(n_pop, n_mp, context, out_weight, *rest):
    tok, width = context.shape
    mem = rest[3].shape[0]
    full = out_weight.shape[1]
    chunks = width // BLK
    if n_mp == 4 and n_pop == 8 and width % BLK == 0 and chunks > 3 and (full // n_pop) % 128 == 0 and tok % 128 == 0 and mem == 16:
        return fused_shards(n_pop, n_mp, context, out_weight, *rest)
    return shards(context, out_weight, *rest)


def solution(mesh):
    in_specs = (
        P("pop", "mp"),
        P("mp", None),
        P("pop", "mp"),
        P("pop", "mp"),
        P(),
        P("pop", None),
        P("pop", None),
        P("pop"),
    )
    out_specs = (P("pop", "mp"), P("pop"), P("pop", "mp"))
    return jax.shard_map(
        functools.partial(chosen, mesh.shape["pop"], mesh.shape["mp"]), mesh=mesh, in_specs=in_specs, out_specs=out_specs, check_vma=False)
```

```python
import functools
import math

import jax
import jax.numpy as jnp
from jax import lax
from jax.experimental import pallas as pl
from jax.experimental.pallas import tpu as pltpu
from jax.sharding import PartitionSpec as P

SIGMA = 1.0
EPSILON = 1e-06


def error_sums(stream, lifted, right_rows, gain_part, target_rows, inverse):
    hidden = stream[:, None, :] + lifted[:, :, None] * right_rows[None, :, :]
    differ = gain_part * hidden * inverse[:, :, None] - target_rows[:, None, :]
    return jnp.sum(differ * differ, axis=(0, 2))


def utility(member_ranks, count_all):
    levels = jnp.arange(count_all).astype(jnp.float32)
    ceiling = math.log(count_all / 2 + 1)
    baseline = jnp.maximum(0.0, ceiling - jnp.log(levels + 1.0))
    shaped = jnp.maximum(0.0, ceiling - jnp.log(member_ranks.astype(jnp.float32) + 1.0))
    return shaped / jnp.sum(baseline) - 1.0 / count_all


def shards(
    context, out_weight, residual, target, norm_gain, left_factors, right_factors, member_ranks
):
    tok_count = context.shape[0]
    shard_width = context.shape[1]
    full_width = out_weight.shape[1]
    factor = SIGMA / math.sqrt(full_width)
    offset = lax.axis_index("mp") * shard_width
    left_cols = lax.dynamic_slice_in_dim(left_factors, offset, shard_width, 1)
    right_cols = lax.dynamic_slice_in_dim(right_factors, offset, shard_width, 1)
    partial_value = jnp.dot(context, out_weight, preferred_element_type=jnp.float32)
    projected = lax.dot_general(
        context, left_cols, (((1,), (1,)), ((), ())), preferred_element_type=jnp.float32
    )
    summed = lax.psum_scatter(
        partial_value.astype(jnp.bfloat16), "mp", scatter_dimension=1, tiled=True
    ).astype(jnp.float32)
    stream = residual.astype(jnp.float32) + summed
    gain_part = lax.dynamic_slice_in_dim(norm_gain, offset, shard_width, 0)
    factor_f = right_cols.astype(jnp.float32)
    crossed = jnp.dot(stream, factor_f.T, precision=lax.Precision.HIGHEST)
    per_token = jnp.sum(stream * stream, axis=1)
    per_member = jnp.sum(factor_f * factor_f, axis=1)
    projected, crossed, per_token, per_member = lax.psum(
        (projected, crossed, per_token, per_member), "mp"
    )
    lifted = factor * projected
    meansq = (
        per_token[:, None] + 2.0 * lifted * crossed + lifted * lifted * per_member[None, :]
    ) / full_width
    inverse = lax.rsqrt(meansq + EPSILON)
    local_error = error_sums(
        stream, lifted, factor_f, gain_part, target.astype(jnp.float32), inverse
    )
    member_total = lax.psum(local_error, "mp")
    fitness = -member_total / (tok_count * full_width)
    everyone = lax.all_gather(fitness, "pop", axis=0, tiled=True)
    count_all = everyone.shape[0]
    average = jnp.mean(everyone)
    centre = everyone - average
    spread = jnp.sqrt(jnp.mean(centre * centre) + 1e-05)
    weight = utility(member_ranks, count_all) + (fitness - average) / spread / count_all
    weighted = (weight[:, None] * left_factors.astype(jnp.float32)).astype(jnp.bfloat16)
    weighted_rows = lax.all_to_all(weighted, "pop", split_axis=1, concat_axis=0, tiled=True)
    right_all = lax.all_gather(right_cols, "pop", axis=0, tiled=True)
    update = lax.dot_general(
        weighted_rows, right_all, (((0,), (0,)), ((), ())), preferred_element_type=jnp.float32
    ) * (math.sqrt(count_all) / SIGMA)
    return (update, fitness, stream)


BLK = 256
LANES = 128
F32 = jnp.float32
BF = jnp.bfloat16


def nt_dot(a, b):
    return lax.dot_general(a, b, (((1,), (1,)), ((), ())), preferred_element_type=F32)


def split_two(x):
    hi = x.astype(BF)
    return hi, (x - hi.astype(F32)).astype(BF)


def halves(parts):
    return jnp.concatenate([piece for part in parts for piece in split_two(part)], axis=1)


def row_picker(count):
    shape = (8, count * 2 * LANES)
    owner = lax.broadcasted_iota(jnp.int32, shape, 1) // (2 * LANES)
    return jnp.where(owner == lax.broadcasted_iota(jnp.int32, shape, 0), 1.0, 0.0).astype(BF)


def flip(index, bits):
    for bit in (1, 2, 4):
        if bits & bit:
            index = index + bit - 2 * bit * ((index // bit) % 2)
    return index


def kernel(
    n_pop, n_mp, ctx_h, w_h, res_h, tgt_h, gain_h, left_h, right_h, ranks_h,
    base, left_all, right_all, fits,
    w_v, ctx, res, tgt, lcols, gain, right, ranks, send, recv, first_v, direct, lall, rall,
    sq_s, sq_a, sq_e, sq_t, lin, lin_in, lin_out, lin_far, post, post_in, swap, swap_in, marks,
    w_sem, top_sem, near_sem, loc_sem, sent, r_a, r_y, r_b, r_top, r_lin, r_far, r_post, r_swap, r_l, r_r, r_f, rounds,
):
    tok, width = ctx.shape
    mem = right.shape[0]
    full = right.shape[1]
    rows = full // n_pop
    chunks = width // BLK
    units = width // LANES
    last = units - 1
    pieces = tok // LANES
    upper = LANES
    per = mem // 2
    members = mem * n_pop
    p = lax.axis_index("pop")
    q = lax.axis_index("mp")
    y = q // 2
    c = q % 2
    mate = flip(q, 1)
    across = flip(q, 2)
    diagonal = flip(q, 3)
    blocks = (diagonal, across, mate, q)
    other = 2 - 2 * y

    def remote(src, dst, ss, rs, pop, mp):
        return pltpu.make_async_remote_copy(
            src_ref=src, dst_ref=dst, send_sem=ss, recv_sem=rs,
            device_id=(pop, mp), device_id_type=pl.DeviceIdType.MESH,
        )

    def signal(sem, pop, mp):
        pl.semaphore_signal(sem, inc=1, device_id=(pop, mp), device_id_type=pl.DeviceIdType.MESH)

    def wait_for(ref, sem):
        pltpu.make_async_copy(ref, ref, sem).wait()

    def w_copy(s, k, sem):
        start = pl.multiple_of(blocks[s] * width + k * BLK, BLK)
        return pltpu.make_async_copy(w_h.at[:, pl.ds(start, BLK)], w_v.at[s, k], sem)

    def w_first(n):
        start = pl.multiple_of((other + n) * width, BLK)
        slot = 1 - c if n == 0 else c
        return pltpu.make_async_copy(w_h.at[:, pl.ds(start, BLK)], w_v.at[slot, 0], top_sem.at[n])

    def near_copy(k):
        return w_copy(3, k, near_sem)

    def w_step(k, more):
        steps = [(1, k), (2, k)] if isinstance(k, jax.Array) or k > 0 else [(2, k)]
        if more:
            steps.append((0, k + 1))
        return [w_copy(s, i, w_sem.at[k % 2]) for s, i in steps]

    my_cols = pl.ds(pl.multiple_of(q * width, BLK), width)
    my_rows = pl.ds(pl.multiple_of(p * rows, LANES), rows)
    locals_ = [
        pltpu.make_async_copy(ctx_h.at[0:upper], ctx.at[0:upper], loc_sem.at[0]),
        pltpu.make_async_copy(ctx_h.at[upper:tok], ctx.at[upper:tok], loc_sem.at[1]),
        pltpu.make_async_copy(res_h, res, loc_sem.at[2]),
        pltpu.make_async_copy(tgt_h, tgt, loc_sem.at[2]),
        pltpu.make_async_copy(left_h.at[:, my_cols], lcols, loc_sem.at[2]),
        pltpu.make_async_copy(left_h.at[:, my_rows], lall.at[0], loc_sem.at[2]),
        pltpu.make_async_copy(right_h.at[:, my_cols], rall.at[0], loc_sem.at[2]),
        pltpu.make_async_copy(gain_h, gain, loc_sem.at[2]),
        pltpu.make_async_copy(right_h, right, loc_sem.at[2]),
        pltpu.make_async_copy(ranks_h, ranks, loc_sem.at[2]),
    ]
    locals_[0].start()
    w_first(0).start()

    barrier = pltpu.get_barrier_semaphore()
    for peer in (mate, across, diagonal):
        signal(barrier, p, peer)
    locals_[1].start()
    for bit in (1, 2, 4):
        signal(barrier, flip(p, bit), q)

    copy_top = remote(first_v, direct.at[c], sent, r_top, p, other)

    def copy_a(k):
        cols = pl.ds(2 * k, 2)
        return remote(send.at[0, cols], recv.at[0, cols], sent, r_a.at[pieces + k - 1], p, mate)

    def strip(i):
        return pl.ds(i * LANES, LANES)

    def copy_a0(i):
        return remote(send.at[0, 0:2, strip(i)], recv.at[0, 0:2, strip(i)], sent, r_a.at[i], p, mate)

    def copy_y0(i):
        return remote(send.at[1, 0:2, strip(i)], recv.at[1, 0:2, strip(i)], sent, r_y.at[i], p, across)

    def copy_y(k, count=2):
        cols = pl.ds(2 * k, count)
        return remote(send.at[1, cols], recv.at[1, cols], sent, r_y.at[pieces + k - 1], p, across)

    def copy_end(i):
        part = slice(i * LANES, (i + 1) * LANES)
        return remote(send.at[1, last, part], recv.at[1, last, part], sent, r_y.at[pieces + chunks - 1 + i], p, across)

    copy_swap = remote(send.at[1, last, strip(0)], swap_in, sent, r_swap, p, mate)
    copy_swapped = remote(swap, recv.at[1, last, strip(0)], sent, r_y.at[pieces + chunks - 1], p, diagonal)

    def copy_b(k):
        cols = pl.ds(2 * k, 2)
        return remote(send.at[2, cols], recv.at[2, cols], sent, r_b, p, mate)

    def copy_l(d):
        peer = flip(p, d)
        cols = pl.ds(pl.multiple_of(peer * rows, LANES), rows)
        return remote(left_h.at[:, cols], lall.at[d], sent, r_l, peer, q)

    def copy_r(d):
        return remote(right_h.at[:, my_cols], rall.at[d], sent, r_r, flip(p, d), q)

    def copy_f(n, core):
        target = flip(q, 2 * (n % 2)) - c + core
        return remote(marks.at[0], marks.at[n], sent, r_f, flip(p, n // 2), target)

    copy_lin = remote(lin, lin_in, sent, r_lin, p, mate)
    copy_far = remote(lin_out, lin_far, sent, r_far, p, across)

    def copy_post(i, d):
        return remote(post.at[i], post_in.at[d - 1, i], sent, r_post, p, flip(q, d))

    def split_store(which, k, value):
        send[which, 2 * k] = value[:, :LANES]
        send[which, 2 * k + 1] = value[:, LANES:]

    def product(s, k):
        return jnp.dot(ctx[...], w_v[s, k], preferred_element_type=F32)

    everything = slice(0, tok)
    with jax.named_scope("load0"):
        locals_[0].wait()
        w_first(0).wait()
    w_first(1).start()
    top = jnp.dot(ctx[0:upper, :], w_v[1 - c, 0], preferred_element_type=F32).astype(BF)
    first_v[0] = top[:, :LANES]
    first_v[1] = top[:, LANES:]
    with jax.named_scope("barrier"):
        pl.semaphore_wait(barrier, 6)
    copy_top.start()
    signal(rounds.at[0], flip(p, 1), q)
    for item in w_step(0, True):
        item.start()
    locals_[1].wait()

    def strip_product(s, i):
        rows_i = slice(i * LANES, (i + 1) * LANES)
        return jnp.dot(ctx[rows_i, :], w_v[s, 0], preferred_element_type=F32)

    def give(i):
        value = strip_product(0, i).astype(BF)
        send[0, 0, strip(i)] = value[:, :LANES]
        send[0, 1, strip(i)] = value[:, LANES:]
        copy_a0(i).start()

    def pass_on(i, value):
        send[1, 0, strip(i)] = (value[:, :LANES] + recv[0, 0, strip(i)].astype(F32)).astype(BF)
        send[1, 1, strip(i)] = (value[:, LANES:] + recv[0, 1, strip(i)].astype(F32)).astype(BF)
        copy_y0(i).start()

    @pl.when(c == 0)
    def _():
        mine = [strip_product(1, i) for i in (1, 2)]
        copy_a0(1).wait_recv()
        pass_on(1, mine[0])
        w_first(1).wait()
        give(1)
        copy_a0(2).wait_recv()
        pass_on(2, mine[1])
        give(2)
        give(0)
        send[1, 0, strip(0)] = first_v[0]
        send[1, 1, strip(0)] = first_v[1]

    @pl.when(c == 1)
    def _():
        give(1)
        give(2)
        send[0, 0, strip(0)] = first_v[0]
        send[0, 1, strip(0)] = first_v[1]
        w_first(1).wait()

    for item in w_step(1, True):
        item.start()
    near_copy(0).start()
    for item in w_step(0, True):
        item.wait()
    split_store(0, 1, product(0, 1).astype(BF))
    copy_a(1).start()
    for item in w_step(2, True):
        item.start()

    @pl.when(c == 1)
    def _():
        mine = [strip_product(1, i) for i in (1, 2, 0)]
        with jax.named_scope("wait_a0"):
            for i in (1, 2, 0):
                copy_a0(i).wait_recv()
                pass_on(i, mine[i - 1])


    def far(k, carry):
        for item in w_step(k, False):
            item.wait()

        @pl.when(k + 1 < chunks)
        def _():
            w_copy(0, k + 1, w_sem.at[k % 2]).wait()

        mine = product(1, k)
        with jax.named_scope("wait_a"):
            copy_a(k).wait_recv()
        send[1, 2 * k] = (mine[:, :LANES] + recv[0, 2 * k].astype(F32)).astype(BF)
        send[1, 2 * k + 1] = (mine[:, LANES:] + recv[0, 2 * k + 1].astype(F32)).astype(BF)

        @pl.when(k + 1 < chunks)
        def _():
            copy_y(k).start()

        @pl.when(k + 1 == chunks)
        def _():
            copy_y(k, 1).start()

            @pl.when(c == 0)
            def _():
                send[1, last, strip(0)] = mine[0:LANES, LANES:].astype(BF)
                copy_swap.start()

        @pl.when(k + 2 < chunks)
        def _():
            for item in w_step(k + 2, False):
                item.start()

        @pl.when(k + 3 < chunks)
        def _():
            w_copy(0, k + 3, w_sem.at[k % 2]).start()

        near_copy(k).start()

        @pl.when(k == 1)
        def _():
            for item in locals_[2:]:
                item.start()
            pl.semaphore_wait(rounds.at[0], 1)
            signal(rounds.at[1], flip(p, 2), q)

        @pl.when(k == 2)
        def _():
            pl.semaphore_wait(rounds.at[1], 1)
            signal(rounds.at[2], flip(p, 4), q)

        @pl.when(k == 3)
        def _():
            pl.semaphore_wait(rounds.at[2], 1)
            for d in range(1, n_pop):
                copy_r(n_pop - d).start()
                copy_l(n_pop - d).start()

        @pl.when(k + 1 < chunks)
        def _():
            split_store(0, k + 1, product(0, k + 1).astype(BF))
            copy_a(k + 1).start()

        @pl.when(k == 1)
        def _():
            split_store(2, 0, product(2, 0).astype(BF))
            copy_b(0).start()

        split_store(2, k, product(2, k).astype(BF))
        copy_b(k).start()
        return carry

    with jax.named_scope("far"):
        lax.fori_loop(1, chunks, far, 0)

    for item in locals_[2:]:
        item.wait()
    wait_for(w_v.at[3], near_sem)

    def near(k, carry):
        cols = pl.ds(pl.multiple_of(k * BLK, BLK), BLK)
        base[:, cols] = product(3, k) + res[:, cols].astype(F32)
        return carry

    with jax.named_scope("near"):
        lax.fori_loop(0, chunks, near, 0)

    def spread(slot, value):
        for j in range(2):
            lin[j, slot * per:(slot + 1) * per, :] = value[j * per:(j + 1) * per]

    with jax.named_scope("early"):
        r_mine = rall[0].astype(F32)
        gr_hi, gr_lo = split_two(r_mine * gain[:, my_cols])
        spread(0, nt_dot(lcols[...], ctx[...]))
        spread(1, nt_dot(gr_hi, tgt[...]) + nt_dot(gr_lo, tgt[...]))
        r_full = right[...].astype(F32)
        gr_full = r_full * gain[...]
        norm_r = jnp.sum(r_full * r_full, axis=1, keepdims=True)
        norm_gr = jnp.sum(gr_full * gr_full, axis=1, keepdims=True)
        for acc in (sq_s, sq_a, sq_e, sq_t):
            acc[...] = jnp.zeros_like(acc)

    def mixed(block, start, size):
        cols = pl.ds(pl.multiple_of(block * width + start, LANES), size)
        r = right[:, cols]
        g = gain[:, cols]
        hi, low = split_two(r.astype(F32) * (g * g))
        return jnp.concatenate([r, hi, low], axis=0)

    def linear(k, carry):
        crossed, crossed_g = carry
        near_rows = mixed(q, k * BLK, BLK)
        far_rows = mixed(across, k * BLK, BLK)
        for h in range(2):
            cols = pl.ds(pl.multiple_of(k * BLK + h * LANES, LANES), LANES)
            part = slice(h * LANES, (h + 1) * LANES)
            u = 2 * k + h
            s = base[:, cols] + recv[2, u].astype(F32)
            base[:, cols] = s
            hi, low = split_two(s)
            both = nt_dot(near_rows[:, part], hi) + nt_dot(near_rows[:, part], low) + nt_dot(far_rows[:, part], send[1, u])
            crossed = crossed + both[0:mem]
            crossed_g = crossed_g + both[mem:2 * mem] + both[2 * mem:3 * mem]
            wide = tgt[:, cols].astype(F32)
            sq_t[...] += wide * wide
        return crossed, crossed_g

    with jax.named_scope("wait_b"):
        wait_for(recv.at[2], r_b)
    with jax.named_scope("linear"):
        top_rows = mixed(other, 0, BLK)
        top = nt_dot(top_rows[:, :LANES], first_v[0]) + nt_dot(top_rows[:, LANES:], first_v[1])
        top = top + nt_dot(mixed(other, last * LANES, LANES), send[0, last, strip(0)])
        top = top * jnp.where(c == 1, 1.0, 0.0)
        top = jnp.concatenate([top, jnp.zeros((3 * mem, tok - upper), F32)], axis=1)
        carry = (top[0:mem], top[mem:2 * mem] + top[2 * mem:3 * mem])
        crossed, crossed_g = lax.fori_loop(0, chunks, linear, carry)
        spread(2, crossed)
        spread(3, crossed_g)

    @pl.when(c == 0)
    def _():
        copy_lin.start()
        for i in range(1, pieces):
            copy_end(i).start()

    def arrived(u, part):
        cols = pl.ds(pl.multiple_of(u * LANES, LANES), LANES)
        gain_u = gain[:, pl.ds(pl.multiple_of(q * width + u * LANES, LANES), LANES)]
        s = base[part, cols] + recv[1, u, part].astype(F32)
        base[part, cols] = s
        gs = s * gain_u
        return s * s, gs * gs, gs * tgt[part, cols].astype(F32)

    def settle(u, carry):
        for acc, item in zip((sq_s, sq_a, sq_e), arrived(u, everything)):
            acc[...] += item
        return carry

    with jax.named_scope("wait_y0"):
        for i in range(1, pieces):
            copy_y0(i).wait_recv()

        @pl.when(c == 0)
        def _():
            wait_for(direct, r_top)
            for u in range(2):
                recv[1, u, strip(0)] = jnp.zeros((upper, LANES), BF)
                base[0:upper, u * LANES:(u + 1) * LANES] += direct[0, u].astype(F32) + direct[1, u].astype(F32)

        @pl.when(c == 1)
        def _():
            copy_y0(0).wait_recv()

    lax.fori_loop(0, 2, settle, 0)

    @pl.when(c == 1)
    def _():
        with jax.named_scope("wait_lin"):
            copy_lin.wait_recv()
        copy_swap.wait_recv()
        swap[...] = (send[0, last, strip(0)].astype(F32) + swap_in[...].astype(F32)).astype(BF)
        copy_swapped.start()
        lin_out[...] = lin[1 - y] + lin_in[1 - y]
        copy_far.start()
        for i in range(pieces):
            copy_end(i).start()

    def settle_chunk(k, carry):
        with jax.named_scope("wait_y"):
            copy_y(k).wait_recv()
        settle(2 * k, 0)
        settle(2 * k + 1, 0)
        return carry

    with jax.named_scope("settle"):
        lax.fori_loop(1, chunks - 1, settle_chunk, 0)
    with jax.named_scope("wait_y8"):
        copy_y(chunks - 1, 1).wait_recv()
    settle(last - 1, 0)
    before = nt_dot(row_picker(4), halves((sq_s[...], sq_a[...], sq_e[...], sq_t[...])))
    lane = lax.broadcasted_iota(jnp.int32, (1, mem), 1)
    mine_lane = lane // per == y
    ceiling = math.log(members / 2 + 1)
    whole = sum(max(0.0, ceiling - math.log(i + 1.0)) for i in range(members))
    shaped = jnp.maximum(0.0, ceiling - jnp.log(ranks[...].astype(F32) + 1.0)) / whole - 1.0 / members
    picker = row_picker(3)
    for i in range(pieces):
        part = slice(i * LANES, (i + 1) * LANES)
        with jax.named_scope("wait_end"):
            copy_end(i).wait_recv()
        with jax.named_scope("end"):
            post[i] = (before[:, part] + nt_dot(picker, halves(arrived(last, part))))[0:4]

            @pl.when(c == 0)
            def _():
                copy_post(i, 3).start()
                copy_post(i, 1).start()

            @pl.when(c == 1)
            def _():
                copy_post(i, 2).start()

    square = (mem, mem)
    eye = lax.broadcasted_iota(jnp.int32, square, 0) == lax.broadcasted_iota(jnp.int32, square, 1)
    half_of = slice(1, n_pop)
    others = marks.at[pl.ds(1, 2 * n_pop - 1)]

    @pl.when(c == 1)
    def _():
        with jax.named_scope("wait_far"):
            copy_far.wait_recv()
        own = lin[y] + lin_in[y] + lin_far[...]
        mine = jnp.where(y == 1, 1.0, 0.0)

        def my_members(column):
            return column[0:per] + mine * (column[per:mem] - column[0:per])

        lifted = own[0:per] * (SIGMA / math.sqrt(full))
        lifted2 = lifted * lifted
        extra_s = 2.0 * lifted * own[2 * per:3 * per] + lifted2 * my_members(norm_r)
        extra_a = 2.0 * lifted * own[3 * per:4 * per] + lifted2 * my_members(norm_gr)
        extra_e = lifted * own[per:2 * per]
        with jax.named_scope("wait_post"):
            wait_for(post_in, r_post)
        with jax.named_scope("errors"):
            late = jnp.concatenate([post[i] + post_in[0, i] + post_in[1, i] + post_in[2, i] for i in range(pieces)], axis=1)
            meansq = (late[0:1] + extra_s) / full
            inverse = lax.rsqrt(meansq + EPSILON)
            errors = inverse * inverse * (late[1:2] + extra_a) - 2.0 * inverse * (late[2:3] + extra_e) + late[3:4]
            summed = jnp.sum(errors, axis=1, keepdims=True)
            stacked = jnp.concatenate([summed, summed], axis=0)
            total_row = jnp.sum(jnp.where(eye, stacked, 0.0), axis=0, keepdims=True)
            marks[0, 0:1] = jnp.where(mine_lane, total_row, 0.0)
            marks[0, 1:2] = jnp.where(mine_lane, shaped, 0.0)
            for n in range(2 * n_pop - 1, -1, -1):
                copy_f(n, 0).start()
                if n > 0:
                    copy_f(n, 1).start()

    with jax.named_scope("wait_lr"):
        wait_for(lall.at[half_of], r_l)
        wait_for(rall.at[half_of], r_r)
    for d in range(n_pop):
        right_all[d * mem:(d + 1) * mem, :] = rall[d]
        left_all[d * mem:(d + 1) * mem, :] = lall[d]

    @pl.when(c == 0)
    def _():
        with jax.named_scope("wait_f"):
            wait_for(marks, r_f)

    @pl.when(c == 1)
    def _():
        with jax.named_scope("wait_f"):
            wait_for(others, r_f)

    fits[...] = marks[...]
    for which in range(2):
        wait_for(send.at[which, 2:units], sent)
    wait_for(send.at[2], sent)
    wait_for(first_v, sent)
    wait_for(lall.at[half_of], sent)
    wait_for(rall.at[half_of], sent)
    for core in range(2):
        @pl.when(c == core)
        def _(core=core):
            for i in range(core, pieces):
                copy_a0(i).wait_send()
            for i in range(1 - core, pieces):
                copy_y0(i).wait_send()
            if core == 1:
                copy_swapped.wait_send()
            if core == 0:
                copy_lin.wait_send()
                wait_for(post_in.at[0:2], sent)
            else:
                copy_far.wait_send()
                wait_for(post_in.at[0], sent)
                wait_for(marks, sent)
                wait_for(others, sent)


def in_hbm(x):
    return pltpu.with_memory_space_constraint(x, pltpu.HBM)


def fused_shards(
    n_pop, n_mp, context, out_weight, residual, target, norm_gain, left_factors, right_factors, member_ranks
):
    tok, width = context.shape
    full = out_weight.shape[1]
    mem = left_factors.shape[0]
    rows = full // n_pop
    chunks = width // BLK
    units = width // LANES
    pieces = tok // LANES
    ranks = member_ranks.reshape(1, mem)
    anywhere = pl.BlockSpec(memory_space=pltpu.HBM)
    vmem = pl.BlockSpec(memory_space=pltpu.VMEM)
    dma = pltpu.SemaphoreType.DMA
    acc = pltpu.VMEM((tok, LANES), F32)
    group = (2 * mem, tok)
    base, left_all, right_all, fits = pl.pallas_call(
        functools.partial(kernel, n_pop, n_mp),
        name="es_step",
        out_shape=(
            jax.ShapeDtypeStruct((tok, width), F32),
            jax.ShapeDtypeStruct((n_pop * mem, rows), BF),
            jax.ShapeDtypeStruct((n_pop * mem, width), BF),
            jax.ShapeDtypeStruct((2 * n_pop, 2, mem), F32),
        ),
        in_specs=[anywhere] * 8,
        out_specs=[vmem] * 4,
        scratch_shapes=[
            pltpu.VMEM((4, chunks, width, BLK), BF),
            pltpu.VMEM((tok, width), BF),
            pltpu.VMEM((tok, width), BF),
            pltpu.VMEM((tok, width), BF),
            pltpu.VMEM((mem, width), BF),
            pltpu.VMEM((1, full), F32),
            pltpu.VMEM((mem, full), BF),
            pltpu.VMEM((1, mem), jnp.int32),
            pltpu.VMEM((3, units, tok, LANES), BF),
            pltpu.VMEM((3, units, tok, LANES), BF),
            pltpu.VMEM((2, LANES, LANES), BF),
            pltpu.VMEM((2, 2, LANES, LANES), BF),
            pltpu.VMEM((n_pop, mem, rows), BF),
            pltpu.VMEM((n_pop, mem, width), BF),
            acc, acc, acc, acc,
            pltpu.VMEM((2,) + group, F32),
            pltpu.VMEM((2,) + group, F32),
            pltpu.VMEM(group, F32),
            pltpu.VMEM(group, F32),
            pltpu.VMEM((pieces, 4, LANES), F32),
            pltpu.VMEM((n_mp - 1, pieces, 4, LANES), F32),
            pltpu.VMEM((LANES, LANES), BF),
            pltpu.VMEM((LANES, LANES), BF),
            pltpu.VMEM((2 * n_pop, 2, mem), F32),
            dma((2,)),
            dma((2,)),
            dma,
            dma((3,)),
            dma,
            dma((chunks - 1 + pieces,)),
            dma((chunks - 1 + 2 * pieces,)),
        ]
        + [dma] * 9
        + [pltpu.SemaphoreType.REGULAR((3,))],
        compiler_params=pltpu.CompilerParams(
            collective_id=0, has_side_effects=True, vmem_limit_bytes=48 * 1024 * 1024
        ),
    )(
        *map(in_hbm, (
            context, out_weight, residual, target, norm_gain.reshape(1, full), left_factors,
            right_factors, ranks,
        ))
    )
    count_all = n_pop * mem
    update, base, fitness = pl.pallas_call(
        functools.partial(finish, math.sqrt(count_all) / SIGMA, tok * full),
        name="es_update",
        out_shape=(
            jax.ShapeDtypeStruct((rows, width), F32),
            jax.ShapeDtypeStruct((tok, width), F32),
            jax.ShapeDtypeStruct((1, mem), F32),
        ),
        in_specs=[vmem] * 4,
        out_specs=[anywhere] * 3,
        scratch_shapes=[
            pltpu.VMEM((rows, width), F32),
            pltpu.VMEM((n_pop * mem, rows), BF),
            pltpu.VMEM((1, mem), F32),
            dma((rows // 128 + 2,)),
        ],
        compiler_params=pltpu.CompilerParams(vmem_limit_bytes=16 * 1024 * 1024),
    )(left_all, right_all, base, fits)
    return (update, fitness.reshape(mem), base)


def finish(scale, count, left_all, right_all, base_in, fits, update, base, fit, held, weighted, fit_v, sems):
    steps = held.shape[0] // 128
    mem = fit_v.shape[1]
    n_pop = left_all.shape[0] // mem
    members = n_pop * mem
    copies = [
        pltpu.make_async_copy(base_in, base, sems.at[steps]),
        pltpu.make_async_copy(fit_v, fit, sems.at[steps + 1]),
    ]
    copies[0].start()
    rows_of = [fits[2 * d] + fits[2 * d + 1] for d in range(n_pop)]
    all_fit = jnp.concatenate([row[0:1] for row in rows_of], axis=0) * (-1.0 / count)
    all_shaped = jnp.concatenate([row[1:2] for row in rows_of], axis=0)
    fit_v[...] = all_fit[0:1]
    copies[1].start()
    average = jnp.sum(jnp.sum(all_fit, axis=0, keepdims=True), axis=1, keepdims=True) / members
    centre = all_fit - average
    deviation = jnp.sqrt(jnp.sum(jnp.sum(centre * centre, axis=0, keepdims=True), axis=1, keepdims=True) / members + 1e-05)
    weight = all_shaped + centre / deviation / members
    square = (mem, mem)
    eye = lax.broadcasted_iota(jnp.int32, square, 0) == lax.broadcasted_iota(jnp.int32, square, 1)
    for d in range(n_pop):
        part = slice(d * mem, (d + 1) * mem)
        upright = jnp.sum(jnp.where(eye, weight[d:d + 1], 0.0), axis=1, keepdims=True)
        weighted[part, :] = (upright * left_all[part, :].astype(F32)).astype(BF)
    for i in range(steps):
        part = slice(i * 128, (i + 1) * 128)
        held[part, :] = lax.dot_general(
            weighted[:, part], right_all[...], (((0,), (0,)), ((), ())), preferred_element_type=F32
        ) * scale
        copies.append(pltpu.make_async_copy(held.at[part], update.at[part], sems.at[i]))
        copies[-1].start()
    for item in copies:
        item.wait()


def chosen(n_pop, n_mp, context, out_weight, *rest):
    tok, width = context.shape
    mem = rest[3].shape[0]
    full = out_weight.shape[1]
    chunks = width // BLK
    if n_mp == 4 and n_pop == 8 and width % BLK == 0 and chunks > 3 and (full // n_pop) % 128 == 0 and tok % 128 == 0 and mem == 16:
        return fused_shards(n_pop, n_mp, context, out_weight, *rest)
    return shards(context, out_weight, *rest)


def solution(mesh):
    in_specs = (
        P("pop", "mp"),
        P("mp", None),
        P("pop", "mp"),
        P("pop", "mp"),
        P(),
        P("pop", None),
        P("pop", None),
        P("pop"),
    )
    out_specs = (P("pop", "mp"), P("pop"), P("pop", "mp"))
    return jax.shard_map(
        functools.partial(chosen, mesh.shape["pop"], mesh.shape["mp"]), mesh=mesh, in_specs=in_specs, out_specs=out_specs, check_vma=False)
```

```python
import functools
import math

import jax
import jax.numpy as jnp
from jax import lax
from jax.experimental import pallas as pl
from jax.experimental.pallas import tpu as pltpu
from jax.sharding import PartitionSpec as P

SIGMA = 1.0
EPSILON = 1e-06


def error_sums(stream, lifted, right_rows, gain_part, target_rows, inverse):
    hidden = stream[:, None, :] + lifted[:, :, None] * right_rows[None, :, :]
    differ = gain_part * hidden * inverse[:, :, None] - target_rows[:, None, :]
    return jnp.sum(differ * differ, axis=(0, 2))


def utility(member_ranks, count_all):
    levels = jnp.arange(count_all).astype(jnp.float32)
    ceiling = math.log(count_all / 2 + 1)
    baseline = jnp.maximum(0.0, ceiling - jnp.log(levels + 1.0))
    shaped = jnp.maximum(0.0, ceiling - jnp.log(member_ranks.astype(jnp.float32) + 1.0))
    return shaped / jnp.sum(baseline) - 1.0 / count_all


def shards(
    context, out_weight, residual, target, norm_gain, left_factors, right_factors, member_ranks
):
    tok_count = context.shape[0]
    shard_width = context.shape[1]
    full_width = out_weight.shape[1]
    factor = SIGMA / math.sqrt(full_width)
    offset = lax.axis_index("mp") * shard_width
    left_cols = lax.dynamic_slice_in_dim(left_factors, offset, shard_width, 1)
    right_cols = lax.dynamic_slice_in_dim(right_factors, offset, shard_width, 1)
    partial_value = jnp.dot(context, out_weight, preferred_element_type=jnp.float32)
    projected = lax.dot_general(
        context, left_cols, (((1,), (1,)), ((), ())), preferred_element_type=jnp.float32
    )
    summed = lax.psum_scatter(
        partial_value.astype(jnp.bfloat16), "mp", scatter_dimension=1, tiled=True
    ).astype(jnp.float32)
    stream = residual.astype(jnp.float32) + summed
    gain_part = lax.dynamic_slice_in_dim(norm_gain, offset, shard_width, 0)
    factor_f = right_cols.astype(jnp.float32)
    crossed = jnp.dot(stream, factor_f.T, precision=lax.Precision.HIGHEST)
    per_token = jnp.sum(stream * stream, axis=1)
    per_member = jnp.sum(factor_f * factor_f, axis=1)
    projected, crossed, per_token, per_member = lax.psum(
        (projected, crossed, per_token, per_member), "mp"
    )
    lifted = factor * projected
    meansq = (
        per_token[:, None] + 2.0 * lifted * crossed + lifted * lifted * per_member[None, :]
    ) / full_width
    inverse = lax.rsqrt(meansq + EPSILON)
    local_error = error_sums(
        stream, lifted, factor_f, gain_part, target.astype(jnp.float32), inverse
    )
    member_total = lax.psum(local_error, "mp")
    fitness = -member_total / (tok_count * full_width)
    everyone = lax.all_gather(fitness, "pop", axis=0, tiled=True)
    count_all = everyone.shape[0]
    average = jnp.mean(everyone)
    centre = everyone - average
    spread = jnp.sqrt(jnp.mean(centre * centre) + 1e-05)
    weight = utility(member_ranks, count_all) + (fitness - average) / spread / count_all
    weighted = (weight[:, None] * left_factors.astype(jnp.float32)).astype(jnp.bfloat16)
    weighted_rows = lax.all_to_all(weighted, "pop", split_axis=1, concat_axis=0, tiled=True)
    right_all = lax.all_gather(right_cols, "pop", axis=0, tiled=True)
    update = lax.dot_general(
        weighted_rows, right_all, (((0,), (0,)), ((), ())), preferred_element_type=jnp.float32
    ) * (math.sqrt(count_all) / SIGMA)
    return (update, fitness, stream)


BLK = 256
LANES = 128
F32 = jnp.float32
BF = jnp.bfloat16


def nt_dot(a, b):
    return lax.dot_general(a, b, (((1,), (1,)), ((), ())), preferred_element_type=F32)


def split_two(x):
    hi = x.astype(BF)
    return hi, (x - hi.astype(F32)).astype(BF)


def halves(parts):
    return jnp.concatenate([piece for part in parts for piece in split_two(part)], axis=1)


def row_picker(count):
    shape = (8, count * 2 * LANES)
    owner = lax.broadcasted_iota(jnp.int32, shape, 1) // (2 * LANES)
    return jnp.where(owner == lax.broadcasted_iota(jnp.int32, shape, 0), 1.0, 0.0).astype(BF)


def flip(index, bits):
    for bit in (1, 2, 4):
        if bits & bit:
            index = index + bit - 2 * bit * ((index // bit) % 2)
    return index


def kernel(
    n_pop, n_mp, ctx_h, w_h, res_h, tgt_h, gain_h, left_h, right_h, ranks_h,
    base, left_t, right_all, fits,
    w_v, ctx, res, tgt, lcols, gain, right, ranks, send, recv, first_v, direct, lall, rall,
    sq_s, sq_a, sq_e, sq_t, lin, lin_in, lin_out, lin_far, post, post_in, swap, swap_in, marks, left_v, ranked,
    w_sem, top_sem, near_sem, loc_sem, sent, r_a, r_y, r_b, r_top, r_lin, r_far, r_post, r_swap, r_l, r_r, r_u, r_f, rounds,
):
    tok, width = ctx.shape
    mem = right.shape[0]
    full = right.shape[1]
    rows = full // n_pop
    chunks = width // BLK
    units = width // LANES
    last = units - 1
    pieces = tok // LANES
    upper = LANES
    per = mem // 2
    members = mem * n_pop
    p = lax.axis_index("pop")
    q = lax.axis_index("mp")
    y = q // 2
    c = q % 2
    mate = flip(q, 1)
    across = flip(q, 2)
    diagonal = flip(q, 3)
    blocks = (diagonal, across, mate, q)
    other = 2 - 2 * y

    def remote(src, dst, ss, rs, pop, mp):
        return pltpu.make_async_remote_copy(
            src_ref=src, dst_ref=dst, send_sem=ss, recv_sem=rs,
            device_id=(pop, mp), device_id_type=pl.DeviceIdType.MESH,
        )

    def signal(sem, pop, mp):
        pl.semaphore_signal(sem, inc=1, device_id=(pop, mp), device_id_type=pl.DeviceIdType.MESH)

    def wait_for(ref, sem):
        pltpu.make_async_copy(ref, ref, sem).wait()

    def w_copy(s, k, sem):
        start = pl.multiple_of(blocks[s] * width + k * BLK, BLK)
        return pltpu.make_async_copy(w_h.at[:, pl.ds(start, BLK)], w_v.at[s, k], sem)

    def w_first(n):
        start = pl.multiple_of((other + n) * width, BLK)
        slot = 1 - c if n == 0 else c
        return pltpu.make_async_copy(w_h.at[:, pl.ds(start, BLK)], w_v.at[slot, 0], top_sem.at[n])

    def near_copy(k):
        return w_copy(3, k, near_sem)

    def w_step(k, more):
        steps = [(1, k), (2, k)] if isinstance(k, jax.Array) or k > 0 else [(2, k)]
        if more:
            steps.append((0, k + 1))
        return [w_copy(s, i, w_sem.at[k % 2]) for s, i in steps]

    my_cols = pl.ds(pl.multiple_of(q * width, BLK), width)
    my_rows = pl.ds(pl.multiple_of(p * rows, LANES), rows)
    locals_ = [
        pltpu.make_async_copy(ctx_h.at[0:upper], ctx.at[0:upper], loc_sem.at[0]),
        pltpu.make_async_copy(ctx_h.at[upper:tok], ctx.at[upper:tok], loc_sem.at[1]),
        pltpu.make_async_copy(res_h, res, loc_sem.at[2]),
        pltpu.make_async_copy(tgt_h, tgt, loc_sem.at[2]),
        pltpu.make_async_copy(left_h.at[:, my_cols], lcols, loc_sem.at[2]),
        pltpu.make_async_copy(left_h.at[:, my_rows], lall.at[0], loc_sem.at[2]),
        pltpu.make_async_copy(right_h.at[:, my_cols], rall.at[0], loc_sem.at[2]),
        pltpu.make_async_copy(gain_h, gain, loc_sem.at[2]),
        pltpu.make_async_copy(right_h, right, loc_sem.at[2]),
        pltpu.make_async_copy(ranks_h, ranks, loc_sem.at[2]),
    ]
    locals_[0].start()
    w_first(0).start()

    barrier = pltpu.get_barrier_semaphore()
    for peer in (mate, across, diagonal):
        signal(barrier, p, peer)
    locals_[1].start()
    for bit in (1, 2, 4):
        signal(barrier, flip(p, bit), q)

    copy_top = remote(first_v, direct.at[c], sent, r_top, p, other)

    def copy_a(k):
        cols = pl.ds(2 * k, 2)
        return remote(send.at[0, cols], recv.at[0, cols], sent, r_a.at[pieces + k - 1], p, mate)

    def strip(i):
        return pl.ds(i * LANES, LANES)

    def copy_a0(i):
        return remote(send.at[0, 0:2, strip(i)], recv.at[0, 0:2, strip(i)], sent, r_a.at[i], p, mate)

    def copy_y0(i):
        return remote(send.at[1, 0:2, strip(i)], recv.at[1, 0:2, strip(i)], sent, r_y.at[i], p, across)

    def copy_y(k, count=2):
        cols = pl.ds(2 * k, count)
        return remote(send.at[1, cols], recv.at[1, cols], sent, r_y.at[pieces + k - 1], p, across)

    def copy_end(i):
        part = slice(i * LANES, (i + 1) * LANES)
        return remote(send.at[1, last, part], recv.at[1, last, part], sent, r_y.at[pieces + chunks - 1 + i], p, across)

    copy_swap = remote(send.at[1, last, strip(0)], swap_in, sent, r_swap, p, mate)
    copy_swapped = remote(swap, recv.at[1, last, strip(0)], sent, r_y.at[pieces + chunks - 1], p, diagonal)

    def copy_b(k):
        cols = pl.ds(2 * k, 2)
        return remote(send.at[2, cols], recv.at[2, cols], sent, r_b, p, mate)

    def copy_l(d):
        peer = flip(p, d)
        cols = pl.ds(pl.multiple_of(peer * rows, LANES), rows)
        return remote(left_h.at[:, cols], lall.at[d], sent, r_l, peer, q)

    def copy_r(d):
        return remote(right_h.at[:, my_cols], rall.at[d], sent, r_r, flip(p, d), q)

    def copy_u(d):
        return remote(ranked.at[0], ranked.at[d], sent, r_u, flip(p, d), q)

    def copy_f(n, core):
        target = flip(q, 2 * (n % 2)) - c + core
        return remote(marks.at[0], marks.at[n], sent, r_f, flip(p, n // 2), target)

    copy_lin = remote(lin, lin_in, sent, r_lin, p, mate)
    copy_far = remote(lin_out, lin_far, sent, r_far, p, across)

    def copy_post(i, d):
        return remote(post.at[i], post_in.at[d - 1, i], sent, r_post, p, flip(q, d))

    def split_store(which, k, value):
        send[which, 2 * k] = value[:, :LANES]
        send[which, 2 * k + 1] = value[:, LANES:]

    def product(s, k):
        return jnp.dot(ctx[...], w_v[s, k], preferred_element_type=F32)

    everything = slice(0, tok)
    order = [*range(1, pieces), 0]
    with jax.named_scope("load0"):
        locals_[0].wait()
        w_first(0).wait()
    w_first(1).start()
    top = jnp.dot(ctx[0:upper, :], w_v[1 - c, 0], preferred_element_type=F32).astype(BF)
    first_v[0] = top[:, :LANES]
    first_v[1] = top[:, LANES:]
    with jax.named_scope("barrier"):
        pl.semaphore_wait(barrier, 6)
    copy_top.start()
    signal(rounds.at[0], flip(p, 1), q)
    for item in w_step(0, True):
        item.start()
    locals_[1].wait()

    def strip_product(s, i):
        rows_i = slice(i * LANES, (i + 1) * LANES)
        return jnp.dot(ctx[rows_i, :], w_v[s, 0], preferred_element_type=F32)

    def give(i):
        value = strip_product(0, i).astype(BF)
        send[0, 0, strip(i)] = value[:, :LANES]
        send[0, 1, strip(i)] = value[:, LANES:]
        copy_a0(i).start()

    def pass_on(i, value):
        send[1, 0, strip(i)] = (value[:, :LANES] + recv[0, 0, strip(i)].astype(F32)).astype(BF)
        send[1, 1, strip(i)] = (value[:, LANES:] + recv[0, 1, strip(i)].astype(F32)).astype(BF)
        copy_y0(i).start()

    @pl.when(c == 0)
    def _():
        mine = [strip_product(1, i) for i in (1, 2)]
        copy_a0(1).wait_recv()
        pass_on(1, mine[0])
        w_first(1).wait()
        give(1)
        copy_a0(2).wait_recv()
        pass_on(2, mine[1])
        give(2)
        give(0)
        send[1, 0, strip(0)] = first_v[0]
        send[1, 1, strip(0)] = first_v[1]

    @pl.when(c == 1)
    def _():
        give(1)
        give(2)
        send[0, 0, strip(0)] = first_v[0]
        send[0, 1, strip(0)] = first_v[1]
        w_first(1).wait()

    for item in w_step(1, True):
        item.start()
    near_copy(0).start()
    for item in w_step(0, True):
        item.wait()
    split_store(0, 1, product(0, 1).astype(BF))
    copy_a(1).start()
    for item in w_step(2, True):
        item.start()

    @pl.when(c == 1)
    def _():
        mine = [strip_product(1, i) for i in (1, 2, 0)]
        with jax.named_scope("wait_a0"):
            for i in (1, 2, 0):
                copy_a0(i).wait_recv()
                pass_on(i, mine[i - 1])


    def far(k, carry):
        for item in w_step(k, False):
            item.wait()

        @pl.when(k + 1 < chunks)
        def _():
            w_copy(0, k + 1, w_sem.at[k % 2]).wait()

        mine = product(1, k)
        with jax.named_scope("wait_a"):
            copy_a(k).wait_recv()
        send[1, 2 * k] = (mine[:, :LANES] + recv[0, 2 * k].astype(F32)).astype(BF)
        send[1, 2 * k + 1] = (mine[:, LANES:] + recv[0, 2 * k + 1].astype(F32)).astype(BF)

        @pl.when(k + 1 < chunks)
        def _():
            copy_y(k).start()

        @pl.when((k + 1 == chunks) & (c == 0))
        def _():
            send[1, last, strip(0)] = mine[0:LANES, LANES:].astype(BF)
            copy_swap.start()

        @pl.when(k + 2 < chunks)
        def _():
            for item in w_step(k + 2, False):
                item.start()

        @pl.when(k + 3 < chunks)
        def _():
            w_copy(0, k + 3, w_sem.at[k % 2]).start()

        near_copy(k).start()

        @pl.when(k == 1)
        def _():
            for item in locals_[2:]:
                item.start()
            pl.semaphore_wait(rounds.at[0], 1)
            signal(rounds.at[1], flip(p, 2), q)

        @pl.when(k == 2)
        def _():
            pl.semaphore_wait(rounds.at[1], 1)
            signal(rounds.at[2], flip(p, 4), q)

        @pl.when(k == 3)
        def _():
            pl.semaphore_wait(rounds.at[2], 1)
            for d in range(1, n_pop):
                copy_r(n_pop - d).start()
                copy_l(n_pop - d).start()

        @pl.when(k + 1 < chunks)
        def _():
            split_store(0, k + 1, product(0, k + 1).astype(BF))
            copy_a(k + 1).start()

        @pl.when(k == 1)
        def _():
            split_store(2, 0, product(2, 0).astype(BF))
            copy_b(0).start()

        split_store(2, k, product(2, k).astype(BF))
        copy_b(k).start()
        return carry

    with jax.named_scope("far"):
        lax.fori_loop(1, chunks, far, 0)

    for item in locals_[2:]:
        item.wait()
    wait_for(w_v.at[3], near_sem)

    lane = lax.broadcasted_iota(jnp.int32, (1, LANES), 1)
    ceiling = math.log(members / 2 + 1)
    whole = sum(max(0.0, ceiling - math.log(i + 1.0)) for i in range(members))
    shaped = jnp.maximum(0.0, ceiling - jnp.log(ranks[...].astype(F32) + 1.0)) / whole - 1.0 / members
    ranked[0] = jnp.where(lane // mem == p, jnp.concatenate([shaped] * n_pop, axis=1), 0.0)
    for d in range(1, n_pop):
        copy_u(d).start()

    def near(k, carry):
        cols = pl.ds(pl.multiple_of(k * BLK, BLK), BLK)
        base[:, cols] = product(3, k) + res[:, cols].astype(F32)
        return carry

    with jax.named_scope("near"):
        lax.fori_loop(0, chunks, near, 0)

    @pl.when(c == 1)
    def _():
        copy_swap.wait_recv()
        swap[...] = (send[0, last, strip(0)].astype(F32) + swap_in[...].astype(F32)).astype(BF)
        copy_swapped.start()

    copy_y(chunks - 1, 1).start()

    def spread(slot, value):
        for j in range(2):
            lin[j, slot * per:(slot + 1) * per, :] = value[j * per:(j + 1) * per]

    with jax.named_scope("early"):
        r_mine = rall[0].astype(F32)
        gr_hi, gr_lo = split_two(r_mine * gain[:, my_cols])
        spread(0, nt_dot(lcols[...], ctx[...]))
        spread(1, nt_dot(gr_hi, tgt[...]) + nt_dot(gr_lo, tgt[...]))
        r_full = right[...].astype(F32)
        gr_full = r_full * gain[...]
        norm_r = jnp.sum(r_full * r_full, axis=1, keepdims=True)
        norm_gr = jnp.sum(gr_full * gr_full, axis=1, keepdims=True)
        for acc in (sq_s, sq_a, sq_e, sq_t):
            acc[...] = jnp.zeros_like(acc)

    def mixed(block, start, size):
        cols = pl.ds(pl.multiple_of(block * width + start, LANES), size)
        r = right[:, cols]
        g = gain[:, cols]
        hi, low = split_two(r.astype(F32) * (g * g))
        return jnp.concatenate([r, hi, low], axis=0)

    def linear(k, carry):
        crossed, crossed_g = carry
        near_rows = mixed(q, k * BLK, BLK)
        far_rows = mixed(across, k * BLK, BLK)
        for h in range(2):
            cols = pl.ds(pl.multiple_of(k * BLK + h * LANES, LANES), LANES)
            part = slice(h * LANES, (h + 1) * LANES)
            u = 2 * k + h
            s = base[:, cols] + recv[2, u].astype(F32)
            base[:, cols] = s
            hi, low = split_two(s)
            both = nt_dot(near_rows[:, part], hi) + nt_dot(near_rows[:, part], low) + nt_dot(far_rows[:, part], send[1, u])
            crossed = crossed + both[0:mem]
            crossed_g = crossed_g + both[mem:2 * mem] + both[2 * mem:3 * mem]
            wide = tgt[:, cols].astype(F32)
            sq_t[...] += wide * wide
        return crossed, crossed_g

    with jax.named_scope("wait_b"):
        wait_for(recv.at[2], r_b)
    with jax.named_scope("linear"):
        top_rows = mixed(other, 0, BLK)
        top = nt_dot(top_rows[:, :LANES], first_v[0]) + nt_dot(top_rows[:, LANES:], first_v[1])
        top = top + nt_dot(mixed(other, last * LANES, LANES), send[0, last, strip(0)])
        top = top * jnp.where(c == 1, 1.0, 0.0)
        top = jnp.concatenate([top, jnp.zeros((3 * mem, tok - upper), F32)], axis=1)
        carry = (top[0:mem], top[mem:2 * mem] + top[2 * mem:3 * mem])
        crossed, crossed_g = lax.fori_loop(0, chunks, linear, carry)
        spread(2, crossed)
        spread(3, crossed_g)

    @pl.when(c == 0)
    def _():
        copy_lin.start()
        for i in order[:-1]:
            copy_end(i).start()

    def arrived(u, part):
        cols = pl.ds(pl.multiple_of(u * LANES, LANES), LANES)
        gain_u = gain[:, pl.ds(pl.multiple_of(q * width + u * LANES, LANES), LANES)]
        s = base[part, cols] + recv[1, u, part].astype(F32)
        base[part, cols] = s
        gs = s * gain_u
        return s * s, gs * gs, gs * tgt[part, cols].astype(F32)

    def settle(u, carry):
        for acc, item in zip((sq_s, sq_a, sq_e), arrived(u, everything)):
            acc[...] += item
        return carry

    with jax.named_scope("wait_y0"):
        for i in range(1, pieces):
            copy_y0(i).wait_recv()

        @pl.when(c == 0)
        def _():
            wait_for(direct, r_top)
            for u in range(2):
                recv[1, u, strip(0)] = jnp.zeros((upper, LANES), BF)
                base[0:upper, u * LANES:(u + 1) * LANES] += direct[0, u].astype(F32) + direct[1, u].astype(F32)

        @pl.when(c == 1)
        def _():
            copy_y0(0).wait_recv()

    lax.fori_loop(0, 2, settle, 0)

    @pl.when(c == 1)
    def _():
        for i in order:
            copy_end(i).start()
        with jax.named_scope("wait_lin"):
            copy_lin.wait_recv()
        lin_out[...] = lin[1 - y] + lin_in[1 - y]
        copy_far.start()

    def settle_chunk(k, carry):
        with jax.named_scope("wait_y"):
            copy_y(k).wait_recv()
        settle(2 * k, 0)
        settle(2 * k + 1, 0)
        return carry

    with jax.named_scope("settle"):
        lax.fori_loop(1, chunks - 1, settle_chunk, 0)
    half_of = slice(1, n_pop)
    with jax.named_scope("wait_lr"):
        wait_for(lall.at[half_of], r_l)
        wait_for(rall.at[half_of], r_r)
        wait_for(ranked.at[half_of], r_u)
    with jax.named_scope("turn"):
        for d in range(n_pop):
            place = pl.ds(pl.multiple_of(flip(p, d) * mem, mem), mem)
            right_all[place, :] = rall[d]
            left_v[place, :] = lall[d].astype(F32)
        left_t[...] = left_v[...].T
    with jax.named_scope("wait_y8"):
        copy_y(chunks - 1, 1).wait_recv()
    settle(last - 1, 0)
    before = nt_dot(row_picker(4), halves((sq_s[...], sq_a[...], sq_e[...], sq_t[...])))
    picker = row_picker(3)
    for i in order:
        part = slice(i * LANES, (i + 1) * LANES)
        with jax.named_scope("wait_end"):
            copy_end(i).wait_recv()
        with jax.named_scope("end"):
            post[i] = (before[:, part] + nt_dot(picker, halves(arrived(last, part))))[0:4]

            @pl.when(c == 0)
            def _():
                copy_post(i, 3).start()
                copy_post(i, 1).start()

            @pl.when(c == 1)
            def _():
                copy_post(i, 2).start()

    others = marks.at[pl.ds(1, 2 * n_pop - 1)]

    @pl.when(c == 1)
    def _():
        with jax.named_scope("wait_far"):
            copy_far.wait_recv()
        own = lin[y] + lin_in[y] + lin_far[...]
        mine = jnp.where(y == 1, 1.0, 0.0)

        def my_members(column):
            return column[0:per] + mine * (column[per:mem] - column[0:per])

        lifted = own[0:per] * (SIGMA / math.sqrt(full))
        lifted2 = lifted * lifted
        extra_s = 2.0 * lifted * own[2 * per:3 * per] + lifted2 * my_members(norm_r)
        extra_a = 2.0 * lifted * own[3 * per:4 * per] + lifted2 * my_members(norm_gr)
        extra_e = lifted * own[per:2 * per]
        with jax.named_scope("wait_post"):
            wait_for(post_in, r_post)
        with jax.named_scope("errors"):
            late = jnp.concatenate([post[i] + post_in[0, i] + post_in[1, i] + post_in[2, i] for i in range(pieces)], axis=1)
            meansq = (late[0:1] + extra_s) / full
            inverse = lax.rsqrt(meansq + EPSILON)
            errors = inverse * inverse * (late[1:2] + extra_a) - 2.0 * inverse * (late[2:3] + extra_e) + late[3:4]
            summed = jnp.sum(errors, axis=1, keepdims=True)
            spot = lax.broadcasted_iota(jnp.int32, (per, LANES), 0) + (p * mem + y * per)
            here = lax.broadcasted_iota(jnp.int32, (per, LANES), 1) == spot
            marks[0] = jnp.sum(jnp.where(here, summed, 0.0), axis=0, keepdims=True)
            for n in range(2 * n_pop - 1, -1, -1):
                copy_f(n, 0).start()
                if n > 0:
                    copy_f(n, 1).start()

    @pl.when(c == 0)
    def _():
        with jax.named_scope("wait_f"):
            wait_for(marks, r_f)

    @pl.when(c == 1)
    def _():
        with jax.named_scope("wait_f"):
            wait_for(others, r_f)

    fits[0:1] = sum((marks[n] for n in range(1, 2 * n_pop)), marks[0])
    fits[1:2] = sum((ranked[d] for d in range(1, n_pop)), ranked[0])
    for which in range(2):
        wait_for(send.at[which, 2:units], sent)
    wait_for(send.at[2], sent)
    wait_for(first_v, sent)
    wait_for(lall.at[half_of], sent)
    wait_for(rall.at[half_of], sent)
    wait_for(ranked.at[half_of], sent)
    for core in range(2):
        @pl.when(c == core)
        def _(core=core):
            for i in range(core, pieces):
                copy_a0(i).wait_send()
            for i in range(1 - core, pieces):
                copy_y0(i).wait_send()
            if core == 1:
                copy_swapped.wait_send()
            if core == 0:
                copy_lin.wait_send()
                wait_for(post_in.at[0:2], sent)
            else:
                copy_far.wait_send()
                wait_for(post_in.at[0], sent)
                wait_for(marks, sent)
                wait_for(others, sent)


def in_hbm(x):
    return pltpu.with_memory_space_constraint(x, pltpu.HBM)


def fused_shards(
    n_pop, n_mp, context, out_weight, residual, target, norm_gain, left_factors, right_factors, member_ranks
):
    tok, width = context.shape
    full = out_weight.shape[1]
    mem = left_factors.shape[0]
    rows = full // n_pop
    chunks = width // BLK
    units = width // LANES
    pieces = tok // LANES
    ranks = member_ranks.reshape(1, mem)
    anywhere = pl.BlockSpec(memory_space=pltpu.HBM)
    vmem = pl.BlockSpec(memory_space=pltpu.VMEM)
    dma = pltpu.SemaphoreType.DMA
    acc = pltpu.VMEM((tok, LANES), F32)
    group = (2 * mem, tok)
    base, left_t, right_all, fits = pl.pallas_call(
        functools.partial(kernel, n_pop, n_mp),
        name="es_step",
        out_shape=(
            jax.ShapeDtypeStruct((tok, width), F32),
            jax.ShapeDtypeStruct((rows, n_pop * mem), F32),
            jax.ShapeDtypeStruct((n_pop * mem, width), BF),
            jax.ShapeDtypeStruct((2, n_pop * mem), F32),
        ),
        in_specs=[anywhere] * 8,
        out_specs=[vmem] * 4,
        scratch_shapes=[
            pltpu.VMEM((4, chunks, width, BLK), BF),
            pltpu.VMEM((tok, width), BF),
            pltpu.VMEM((tok, width), BF),
            pltpu.VMEM((tok, width), BF),
            pltpu.VMEM((mem, width), BF),
            pltpu.VMEM((1, full), F32),
            pltpu.VMEM((mem, full), BF),
            pltpu.VMEM((1, mem), jnp.int32),
            pltpu.VMEM((3, units, tok, LANES), BF),
            pltpu.VMEM((3, units, tok, LANES), BF),
            pltpu.VMEM((2, LANES, LANES), BF),
            pltpu.VMEM((2, 2, LANES, LANES), BF),
            pltpu.VMEM((n_pop, mem, rows), BF),
            pltpu.VMEM((n_pop, mem, width), BF),
            acc, acc, acc, acc,
            pltpu.VMEM((2,) + group, F32),
            pltpu.VMEM((2,) + group, F32),
            pltpu.VMEM(group, F32),
            pltpu.VMEM(group, F32),
            pltpu.VMEM((pieces, 4, LANES), F32),
            pltpu.VMEM((n_mp - 1, pieces, 4, LANES), F32),
            pltpu.VMEM((LANES, LANES), BF),
            pltpu.VMEM((LANES, LANES), BF),
            pltpu.VMEM((2 * n_pop, 1, LANES), F32),
            pltpu.VMEM((n_pop * mem, rows), F32),
            pltpu.VMEM((n_pop, 1, LANES), F32),
            dma((2,)),
            dma((2,)),
            dma,
            dma((3,)),
            dma,
            dma((chunks - 1 + pieces,)),
            dma((chunks - 1 + 2 * pieces,)),
        ]
        + [dma] * 10
        + [pltpu.SemaphoreType.REGULAR((3,))],
        compiler_params=pltpu.CompilerParams(
            collective_id=0, has_side_effects=True, vmem_limit_bytes=48 * 1024 * 1024
        ),
    )(
        *map(in_hbm, (
            context, out_weight, residual, target, norm_gain.reshape(1, full), left_factors,
            right_factors, ranks,
        ))
    )
    count_all = n_pop * mem
    update, base, fitness = pl.pallas_call(
        functools.partial(finish, n_pop, math.sqrt(count_all) / SIGMA, tok * full),
        name="es_update",
        out_shape=(
            jax.ShapeDtypeStruct((rows, width), F32),
            jax.ShapeDtypeStruct((tok, width), F32),
            jax.ShapeDtypeStruct((1, mem), F32),
        ),
        in_specs=[vmem] * 4,
        out_specs=[anywhere] * 3,
        scratch_shapes=[
            pltpu.VMEM((rows, width), F32),
            pltpu.VMEM((1, mem), F32),
            dma((rows // 128 + 2,)),
        ],
        compiler_params=pltpu.CompilerParams(vmem_limit_bytes=16 * 1024 * 1024),
    )(left_t, right_all, base, fits)
    return (update, fitness.reshape(mem), base)


def finish(n_pop, scale, count, left_t, right_all, base_in, fits, update, base, fit, held, fit_v, sems):
    steps = held.shape[0] // 128
    mem = fit_v.shape[1]
    members = n_pop * mem
    copies = [
        pltpu.make_async_copy(base_in, base, sems.at[steps]),
        pltpu.make_async_copy(fit_v, fit, sems.at[steps + 1]),
    ]
    copies[0].start()
    all_fit = fits[0:1] * (-1.0 / count)
    centre = all_fit - jnp.sum(all_fit, axis=1, keepdims=True) / members
    deviation = jnp.sqrt(jnp.sum(centre * centre, axis=1, keepdims=True) / members + 1e-05)
    weight = fits[1:2] + centre / deviation / members
    for i in range(steps):
        part = slice(i * 128, (i + 1) * 128)
        weighted = (left_t[part, :] * weight).astype(BF)
        held[part, :] = jnp.dot(weighted, right_all[...], preferred_element_type=F32) * scale
        copies.append(pltpu.make_async_copy(held.at[part], update.at[part], sems.at[i]))
        copies[-1].start()
    p = lax.axis_index("pop")
    mine = jnp.zeros((1, mem), F32)
    for d in range(n_pop):
        mine = mine + jnp.where(p == d, 1.0, 0.0) * all_fit[:, d * mem:(d + 1) * mem]
    fit_v[...] = mine
    copies[1].start()
    for item in copies:
        item.wait()


def chosen(n_pop, n_mp, context, out_weight, *rest):
    tok, width = context.shape
    mem = rest[3].shape[0]
    full = out_weight.shape[1]
    chunks = width // BLK
    if n_mp == 4 and n_pop == 8 and width % BLK == 0 and chunks > 3 and (full // n_pop) % 128 == 0 and tok % 128 == 0 and mem == 16:
        return fused_shards(n_pop, n_mp, context, out_weight, *rest)
    return shards(context, out_weight, *rest)


def solution(mesh):
    in_specs = (
        P("pop", "mp"),
        P("mp", None),
        P("pop", "mp"),
        P("pop", "mp"),
        P(),
        P("pop", None),
        P("pop", None),
        P("pop"),
    )
    out_specs = (P("pop", "mp"), P("pop"), P("pop", "mp"))
    return jax.shard_map(
        functools.partial(chosen, mesh.shape["pop"], mesh.shape["mp"]), mesh=mesh, in_specs=in_specs, out_specs=out_specs, check_vma=False)
```

```python
import functools
import math

import jax
import jax.numpy as jnp
from jax import lax
from jax.experimental import pallas as pl
from jax.experimental.pallas import tpu as pltpu
from jax.sharding import PartitionSpec as P

SIGMA = 1.0
EPSILON = 1e-06


def error_sums(stream, lifted, right_rows, gain_part, target_rows, inverse):
    hidden = stream[:, None, :] + lifted[:, :, None] * right_rows[None, :, :]
    differ = gain_part * hidden * inverse[:, :, None] - target_rows[:, None, :]
    return jnp.sum(differ * differ, axis=(0, 2))


def utility(member_ranks, count_all):
    levels = jnp.arange(count_all).astype(jnp.float32)
    ceiling = math.log(count_all / 2 + 1)
    baseline = jnp.maximum(0.0, ceiling - jnp.log(levels + 1.0))
    shaped = jnp.maximum(0.0, ceiling - jnp.log(member_ranks.astype(jnp.float32) + 1.0))
    return shaped / jnp.sum(baseline) - 1.0 / count_all


def shards(
    context, out_weight, residual, target, norm_gain, left_factors, right_factors, member_ranks
):
    tok_count = context.shape[0]
    shard_width = context.shape[1]
    full_width = out_weight.shape[1]
    factor = SIGMA / math.sqrt(full_width)
    offset = lax.axis_index("mp") * shard_width
    left_cols = lax.dynamic_slice_in_dim(left_factors, offset, shard_width, 1)
    right_cols = lax.dynamic_slice_in_dim(right_factors, offset, shard_width, 1)
    partial_value = jnp.dot(context, out_weight, preferred_element_type=jnp.float32)
    projected = lax.dot_general(
        context, left_cols, (((1,), (1,)), ((), ())), preferred_element_type=jnp.float32
    )
    summed = lax.psum_scatter(
        partial_value.astype(jnp.bfloat16), "mp", scatter_dimension=1, tiled=True
    ).astype(jnp.float32)
    stream = residual.astype(jnp.float32) + summed
    gain_part = lax.dynamic_slice_in_dim(norm_gain, offset, shard_width, 0)
    factor_f = right_cols.astype(jnp.float32)
    crossed = jnp.dot(stream, factor_f.T, precision=lax.Precision.HIGHEST)
    per_token = jnp.sum(stream * stream, axis=1)
    per_member = jnp.sum(factor_f * factor_f, axis=1)
    projected, crossed, per_token, per_member = lax.psum(
        (projected, crossed, per_token, per_member), "mp"
    )
    lifted = factor * projected
    meansq = (
        per_token[:, None] + 2.0 * lifted * crossed + lifted * lifted * per_member[None, :]
    ) / full_width
    inverse = lax.rsqrt(meansq + EPSILON)
    local_error = error_sums(
        stream, lifted, factor_f, gain_part, target.astype(jnp.float32), inverse
    )
    member_total = lax.psum(local_error, "mp")
    fitness = -member_total / (tok_count * full_width)
    everyone = lax.all_gather(fitness, "pop", axis=0, tiled=True)
    count_all = everyone.shape[0]
    average = jnp.mean(everyone)
    centre = everyone - average
    spread = jnp.sqrt(jnp.mean(centre * centre) + 1e-05)
    weight = utility(member_ranks, count_all) + (fitness - average) / spread / count_all
    weighted = (weight[:, None] * left_factors.astype(jnp.float32)).astype(jnp.bfloat16)
    weighted_rows = lax.all_to_all(weighted, "pop", split_axis=1, concat_axis=0, tiled=True)
    right_all = lax.all_gather(right_cols, "pop", axis=0, tiled=True)
    update = lax.dot_general(
        weighted_rows, right_all, (((0,), (0,)), ((), ())), preferred_element_type=jnp.float32
    ) * (math.sqrt(count_all) / SIGMA)
    return (update, fitness, stream)


BLK = 256
LANES = 128
F32 = jnp.float32
BF = jnp.bfloat16


def nt_dot(a, b):
    return lax.dot_general(a, b, (((1,), (1,)), ((), ())), preferred_element_type=F32)


def split_two(x):
    hi = x.astype(BF)
    return hi, (x - hi.astype(F32)).astype(BF)


def halves(parts):
    return jnp.concatenate([piece for part in parts for piece in split_two(part)], axis=1)


def row_picker(count):
    shape = (8, count * 2 * LANES)
    owner = lax.broadcasted_iota(jnp.int32, shape, 1) // (2 * LANES)
    return jnp.where(owner == lax.broadcasted_iota(jnp.int32, shape, 0), 1.0, 0.0).astype(BF)


def flip(index, bits):
    for bit in (1, 2, 4):
        if bits & bit:
            index = index + bit - 2 * bit * ((index // bit) % 2)
    return index


def kernel(
    n_pop, n_mp, ctx_h, w_h, res_h, tgt_h, gain_h, left_h, right_h, ranks_h,
    base, left_t, right_all, fits,
    w_v, ctx, res, tgt, lcols, gain, right, ranks, send, recv, first_v, direct, lall, rall,
    sq_s, sq_a, sq_e, sq_t, lin, lin_in, lin_out, lin_far, post, post_in, swap, swap_in, marks, left_v, ranked,
    w_sem, top_sem, near_sem, loc_sem, sent, r_a, r_y, r_b, r_top, r_lin, r_far, r_post, r_swap, r_l, r_r, r_u, r_f, rounds,
):
    tok, width = ctx.shape
    mem = right.shape[0]
    full = right.shape[1]
    rows = full // n_pop
    chunks = width // BLK
    units = width // LANES
    last = units - 1
    pieces = tok // LANES
    upper = LANES
    members = mem * n_pop
    p = lax.axis_index("pop")
    q = lax.axis_index("mp")
    y = q // 2
    c = q % 2
    mate = flip(q, 1)
    across = flip(q, 2)
    diagonal = flip(q, 3)
    blocks = (diagonal, across, mate, q)
    other = 2 - 2 * y

    def remote(src, dst, ss, rs, pop, mp):
        return pltpu.make_async_remote_copy(
            src_ref=src, dst_ref=dst, send_sem=ss, recv_sem=rs,
            device_id=(pop, mp), device_id_type=pl.DeviceIdType.MESH,
        )

    def signal(sem, pop, mp):
        pl.semaphore_signal(sem, inc=1, device_id=(pop, mp), device_id_type=pl.DeviceIdType.MESH)

    def wait_for(ref, sem):
        pltpu.make_async_copy(ref, ref, sem).wait()

    def w_copy(s, k, sem):
        start = pl.multiple_of(blocks[s] * width + k * BLK, BLK)
        return pltpu.make_async_copy(w_h.at[:, pl.ds(start, BLK)], w_v.at[s, k], sem)

    def w_first(n):
        start = pl.multiple_of((other + n) * width, BLK)
        slot = 1 - c if n == 0 else c
        return pltpu.make_async_copy(w_h.at[:, pl.ds(start, BLK)], w_v.at[slot, 0], top_sem.at[n])

    def near_copy(k):
        return w_copy(3, k, near_sem)

    def w_step(k, more):
        steps = [(1, k), (2, k)] if isinstance(k, jax.Array) or k > 0 else [(2, k)]
        if more:
            steps.append((0, k + 1))
        return [w_copy(s, i, w_sem.at[k % 2]) for s, i in steps]

    my_cols = pl.ds(pl.multiple_of(q * width, BLK), width)
    my_rows = pl.ds(pl.multiple_of(p * rows, LANES), rows)
    locals_ = [
        pltpu.make_async_copy(ctx_h.at[0:upper], ctx.at[0:upper], loc_sem.at[0]),
        pltpu.make_async_copy(ctx_h.at[upper:tok], ctx.at[upper:tok], loc_sem.at[1]),
        pltpu.make_async_copy(res_h, res, loc_sem.at[2]),
        pltpu.make_async_copy(tgt_h, tgt, loc_sem.at[2]),
        pltpu.make_async_copy(left_h.at[:, my_cols], lcols, loc_sem.at[2]),
        pltpu.make_async_copy(left_h.at[:, my_rows], lall.at[0], loc_sem.at[2]),
        pltpu.make_async_copy(right_h.at[:, my_cols], rall.at[0], loc_sem.at[2]),
        pltpu.make_async_copy(gain_h, gain, loc_sem.at[2]),
        pltpu.make_async_copy(right_h, right, loc_sem.at[2]),
        pltpu.make_async_copy(ranks_h, ranks, loc_sem.at[2]),
    ]
    locals_[0].start()
    w_first(0).start()

    barrier = pltpu.get_barrier_semaphore()
    for peer in (mate, across, diagonal):
        signal(barrier, p, peer)
    locals_[1].start()
    for bit in (1, 2, 4):
        signal(barrier, flip(p, bit), q)

    copy_top = remote(first_v, direct.at[c], sent, r_top, p, other)

    def copy_a(k):
        cols = pl.ds(2 * k, 2)
        return remote(send.at[0, cols], recv.at[0, cols], sent, r_a.at[pieces + k - 1], p, mate)

    def strip(i):
        return pl.ds(i * LANES, LANES)

    def copy_a0(i):
        return remote(send.at[0, 0:2, strip(i)], recv.at[0, 0:2, strip(i)], sent, r_a.at[i], p, mate)

    def copy_y0(i):
        return remote(send.at[1, 0:2, strip(i)], recv.at[1, 0:2, strip(i)], sent, r_y.at[i], p, across)

    def copy_y(k, count=2):
        cols = pl.ds(2 * k, count)
        return remote(send.at[1, cols], recv.at[1, cols], sent, r_y.at[pieces + k - 1], p, across)

    def copy_end(i):
        part = slice(i * LANES, (i + 1) * LANES)
        return remote(send.at[1, last, part], recv.at[1, last, part], sent, r_y.at[pieces + chunks - 1 + i], p, across)

    copy_swap = remote(send.at[1, last, strip(0)], swap_in, sent, r_swap, p, mate)
    copy_swapped = remote(swap, recv.at[1, last, strip(0)], sent, r_y.at[pieces + chunks - 1], p, diagonal)

    def copy_b(k):
        cols = pl.ds(2 * k, 2)
        return remote(send.at[2, cols], recv.at[2, cols], sent, r_b, p, mate)

    def copy_l(d):
        peer = flip(p, d)
        cols = pl.ds(pl.multiple_of(peer * rows, LANES), rows)
        return remote(left_h.at[:, cols], lall.at[d], sent, r_l, peer, q)

    def copy_r(d):
        return remote(right_h.at[:, my_cols], rall.at[d], sent, r_r, flip(p, d), q)

    def copy_u(d):
        return remote(ranked.at[0], ranked.at[d], sent, r_u, flip(p, d), q)

    def copy_f(d, core):
        return remote(marks.at[0], marks.at[d], sent, r_f, flip(p, d), 2 * y + core)

    copy_lin = remote(lin, lin_in, sent, r_lin, p, mate)
    copy_far = remote(lin_out, lin_far, sent, r_far, p, across)

    def copy_post(i, d):
        return remote(post.at[i], post_in.at[d - 1, i], sent, r_post, p, flip(q, d))

    def split_store(which, k, value):
        send[which, 2 * k] = value[:, :LANES]
        send[which, 2 * k + 1] = value[:, LANES:]

    def product(s, k):
        return jnp.dot(ctx[...], w_v[s, k], preferred_element_type=F32)

    everything = slice(0, tok)
    order = [*range(1, pieces), 0]
    with jax.named_scope("load0"):
        locals_[0].wait()
        w_first(0).wait()
    w_first(1).start()
    top = jnp.dot(ctx[0:upper, :], w_v[1 - c, 0], preferred_element_type=F32).astype(BF)
    first_v[0] = top[:, :LANES]
    first_v[1] = top[:, LANES:]
    with jax.named_scope("barrier"):
        pl.semaphore_wait(barrier, 6)
    copy_top.start()
    signal(rounds.at[0], flip(p, 1), q)
    for item in w_step(0, True):
        item.start()
    locals_[1].wait()

    def strip_product(s, i):
        rows_i = slice(i * LANES, (i + 1) * LANES)
        return jnp.dot(ctx[rows_i, :], w_v[s, 0], preferred_element_type=F32)

    def give(i):
        value = strip_product(0, i).astype(BF)
        send[0, 0, strip(i)] = value[:, :LANES]
        send[0, 1, strip(i)] = value[:, LANES:]
        copy_a0(i).start()

    def pass_on(i, value):
        send[1, 0, strip(i)] = (value[:, :LANES] + recv[0, 0, strip(i)].astype(F32)).astype(BF)
        send[1, 1, strip(i)] = (value[:, LANES:] + recv[0, 1, strip(i)].astype(F32)).astype(BF)
        copy_y0(i).start()

    @pl.when(c == 0)
    def _():
        mine = [strip_product(1, i) for i in (1, 2)]
        copy_a0(1).wait_recv()
        pass_on(1, mine[0])
        w_first(1).wait()
        give(1)
        copy_a0(2).wait_recv()
        pass_on(2, mine[1])
        give(2)
        give(0)
        send[1, 0, strip(0)] = first_v[0]
        send[1, 1, strip(0)] = first_v[1]

    @pl.when(c == 1)
    def _():
        give(1)
        give(2)
        send[0, 0, strip(0)] = first_v[0]
        send[0, 1, strip(0)] = first_v[1]
        w_first(1).wait()

    for item in w_step(1, True):
        item.start()
    near_copy(0).start()
    for item in w_step(0, True):
        item.wait()
    split_store(0, 1, product(0, 1).astype(BF))
    copy_a(1).start()
    for item in w_step(2, True):
        item.start()

    @pl.when(c == 1)
    def _():
        mine = [strip_product(1, i) for i in (1, 2, 0)]
        with jax.named_scope("wait_a0"):
            for i in (1, 2, 0):
                copy_a0(i).wait_recv()
                pass_on(i, mine[i - 1])


    def far(k, carry):
        for item in w_step(k, False):
            item.wait()

        @pl.when(k + 1 < chunks)
        def _():
            w_copy(0, k + 1, w_sem.at[k % 2]).wait()

        mine = product(1, k)
        with jax.named_scope("wait_a"):
            copy_a(k).wait_recv()
        send[1, 2 * k] = (mine[:, :LANES] + recv[0, 2 * k].astype(F32)).astype(BF)
        send[1, 2 * k + 1] = (mine[:, LANES:] + recv[0, 2 * k + 1].astype(F32)).astype(BF)

        @pl.when(k + 1 < chunks)
        def _():
            copy_y(k).start()

        @pl.when((k + 1 == chunks) & (c == 0))
        def _():
            send[1, last, strip(0)] = mine[0:LANES, LANES:].astype(BF)
            copy_swap.start()

        @pl.when(k + 2 < chunks)
        def _():
            for item in w_step(k + 2, False):
                item.start()

        @pl.when(k + 3 < chunks)
        def _():
            w_copy(0, k + 3, w_sem.at[k % 2]).start()

        near_copy(k).start()

        @pl.when(k == 1)
        def _():
            for item in locals_[2:]:
                item.start()
            pl.semaphore_wait(rounds.at[0], 1)
            signal(rounds.at[1], flip(p, 2), q)

        @pl.when(k == 2)
        def _():
            pl.semaphore_wait(rounds.at[1], 1)
            signal(rounds.at[2], flip(p, 4), q)

        @pl.when(k == 3)
        def _():
            pl.semaphore_wait(rounds.at[2], 1)
            for d in range(1, n_pop):
                copy_r(n_pop - d).start()
                copy_l(n_pop - d).start()

        @pl.when(k + 1 < chunks)
        def _():
            split_store(0, k + 1, product(0, k + 1).astype(BF))
            copy_a(k + 1).start()

        @pl.when(k == 1)
        def _():
            split_store(2, 0, product(2, 0).astype(BF))
            copy_b(0).start()

        split_store(2, k, product(2, k).astype(BF))
        copy_b(k).start()
        return carry

    with jax.named_scope("far"):
        lax.fori_loop(1, chunks, far, 0)

    for item in locals_[2:]:
        item.wait()
    wait_for(w_v.at[3], near_sem)

    lane = lax.broadcasted_iota(jnp.int32, (1, LANES), 1)
    ceiling = math.log(members / 2 + 1)
    whole = sum(max(0.0, ceiling - math.log(i + 1.0)) for i in range(members))
    shaped = jnp.maximum(0.0, ceiling - jnp.log(ranks[...].astype(F32) + 1.0)) / whole - 1.0 / members
    ranked[0] = jnp.where(lane // mem == p, jnp.concatenate([shaped] * n_pop, axis=1), 0.0)
    for d in range(1, n_pop):
        copy_u(d).start()

    def near(k, carry):
        cols = pl.ds(pl.multiple_of(k * BLK, BLK), BLK)
        base[:, cols] = product(3, k) + res[:, cols].astype(F32)
        return carry

    with jax.named_scope("near"):
        lax.fori_loop(0, chunks, near, 0)

    @pl.when(c == 1)
    def _():
        copy_swap.wait_recv()
        swap[...] = (send[0, last, strip(0)].astype(F32) + swap_in[...].astype(F32)).astype(BF)
        copy_swapped.start()

    copy_y(chunks - 1, 1).start()

    def spread(slot, value):
        lin[slot * mem:(slot + 1) * mem, :] = value

    with jax.named_scope("early"):
        r_mine = rall[0].astype(F32)
        gr_hi, gr_lo = split_two(r_mine * gain[:, my_cols])
        spread(0, nt_dot(lcols[...], ctx[...]))
        spread(1, nt_dot(gr_hi, tgt[...]) + nt_dot(gr_lo, tgt[...]))
        r_full = right[...].astype(F32)
        gr_full = r_full * gain[...]
        norm_r = jnp.sum(r_full * r_full, axis=1, keepdims=True)
        norm_gr = jnp.sum(gr_full * gr_full, axis=1, keepdims=True)
        for acc in (sq_s, sq_a, sq_e, sq_t):
            acc[...] = jnp.zeros_like(acc)

    def mixed(block, start, size):
        cols = pl.ds(pl.multiple_of(block * width + start, LANES), size)
        r = right[:, cols]
        g = gain[:, cols]
        hi, low = split_two(r.astype(F32) * (g * g))
        return jnp.concatenate([r, hi, low], axis=0)

    def linear(k, carry):
        crossed, crossed_g = carry
        near_rows = mixed(q, k * BLK, BLK)
        far_rows = mixed(across, k * BLK, BLK)
        for h in range(2):
            cols = pl.ds(pl.multiple_of(k * BLK + h * LANES, LANES), LANES)
            part = slice(h * LANES, (h + 1) * LANES)
            u = 2 * k + h
            s = base[:, cols] + recv[2, u].astype(F32)
            base[:, cols] = s
            hi, low = split_two(s)
            both = nt_dot(near_rows[:, part], hi) + nt_dot(near_rows[:, part], low) + nt_dot(far_rows[:, part], send[1, u])
            crossed = crossed + both[0:mem]
            crossed_g = crossed_g + both[mem:2 * mem] + both[2 * mem:3 * mem]
            wide = tgt[:, cols].astype(F32)
            sq_t[...] += wide * wide
        return crossed, crossed_g

    with jax.named_scope("wait_b"):
        wait_for(recv.at[2], r_b)
    with jax.named_scope("linear"):
        top_rows = mixed(other, 0, BLK)
        top = nt_dot(top_rows[:, :LANES], first_v[0]) + nt_dot(top_rows[:, LANES:], first_v[1])
        top = top + nt_dot(mixed(other, last * LANES, LANES), send[0, last, strip(0)])
        top = top * jnp.where(c == 1, 1.0, 0.0)
        top = jnp.concatenate([top, jnp.zeros((3 * mem, tok - upper), F32)], axis=1)
        carry = (top[0:mem], top[mem:2 * mem] + top[2 * mem:3 * mem])
        crossed, crossed_g = lax.fori_loop(0, chunks, linear, carry)
        spread(2, crossed)
        spread(3, crossed_g)

    @pl.when(c == 0)
    def _():
        copy_lin.start()
        for i in order[:-1]:
            copy_end(i).start()

    def arrived(u, part):
        cols = pl.ds(pl.multiple_of(u * LANES, LANES), LANES)
        gain_u = gain[:, pl.ds(pl.multiple_of(q * width + u * LANES, LANES), LANES)]
        s = base[part, cols] + recv[1, u, part].astype(F32)
        base[part, cols] = s
        gs = s * gain_u
        return s * s, gs * gs, gs * tgt[part, cols].astype(F32)

    def settle(u, carry):
        for acc, item in zip((sq_s, sq_a, sq_e), arrived(u, everything)):
            acc[...] += item
        return carry

    with jax.named_scope("wait_y0"):
        for i in range(1, pieces):
            copy_y0(i).wait_recv()

        @pl.when(c == 0)
        def _():
            wait_for(direct, r_top)
            for u in range(2):
                recv[1, u, strip(0)] = jnp.zeros((upper, LANES), BF)
                base[0:upper, u * LANES:(u + 1) * LANES] += direct[0, u].astype(F32) + direct[1, u].astype(F32)

        @pl.when(c == 1)
        def _():
            copy_y0(0).wait_recv()

    lax.fori_loop(0, 2, settle, 0)

    @pl.when(c == 1)
    def _():
        for i in order:
            copy_end(i).start()
        with jax.named_scope("wait_lin"):
            copy_lin.wait_recv()
        lin_out[...] = lin[...] + lin_in[...]
        copy_far.start()

    def settle_chunk(k, carry):
        with jax.named_scope("wait_y"):
            copy_y(k).wait_recv()
        settle(2 * k, 0)
        settle(2 * k + 1, 0)
        return carry

    with jax.named_scope("settle"):
        lax.fori_loop(1, chunks - 1, settle_chunk, 0)
    half_of = slice(1, n_pop)
    with jax.named_scope("wait_lr"):
        wait_for(lall.at[half_of], r_l)
        wait_for(rall.at[half_of], r_r)
        wait_for(ranked.at[half_of], r_u)
    with jax.named_scope("turn"):
        for d in range(n_pop):
            place = pl.ds(pl.multiple_of(flip(p, d) * mem, mem), mem)
            right_all[place, :] = rall[d]
            left_v[place, :] = lall[d].astype(F32)
        left_t[...] = left_v[...].T
    with jax.named_scope("wait_y8"):
        copy_y(chunks - 1, 1).wait_recv()
    settle(last - 1, 0)
    before = nt_dot(row_picker(4), halves((sq_s[...], sq_a[...], sq_e[...], sq_t[...])))
    picker = row_picker(3)
    for i in order:
        part = slice(i * LANES, (i + 1) * LANES)
        with jax.named_scope("wait_end"):
            copy_end(i).wait_recv()
        with jax.named_scope("end"):
            post[i] = (before[:, part] + nt_dot(picker, halves(arrived(last, part))))[0:4]

            @pl.when(c == 0)
            def _():
                copy_post(i, 3).start()
                copy_post(i, 1).start()

            @pl.when(c == 1)
            def _():
                copy_post(i, 2).start()

    others = marks.at[half_of]

    @pl.when(c == 1)
    def _():
        with jax.named_scope("wait_far"):
            copy_far.wait_recv()
        own = lin_out[...] + lin_far[...]
        lifted = own[0:mem] * (SIGMA / math.sqrt(full))
        lifted2 = lifted * lifted
        extra_s = 2.0 * lifted * own[2 * mem:3 * mem] + lifted2 * norm_r
        extra_a = 2.0 * lifted * own[3 * mem:4 * mem] + lifted2 * norm_gr
        extra_e = lifted * own[mem:2 * mem]
        with jax.named_scope("wait_post"):
            wait_for(post_in, r_post)
        with jax.named_scope("errors"):
            late = jnp.concatenate([post[i] + post_in[0, i] + post_in[1, i] + post_in[2, i] for i in range(pieces)], axis=1)
            meansq = (late[0:1] + extra_s) / full
            inverse = lax.rsqrt(meansq + EPSILON)
            errors = inverse * inverse * (late[1:2] + extra_a) - 2.0 * inverse * (late[2:3] + extra_e) + late[3:4]
            summed = jnp.sum(errors, axis=1, keepdims=True)
            spot = lax.broadcasted_iota(jnp.int32, (mem, LANES), 0) + p * mem
            here = lax.broadcasted_iota(jnp.int32, (mem, LANES), 1) == spot
            marks[0] = jnp.sum(jnp.where(here, summed, 0.0), axis=0, keepdims=True)
            for d in range(n_pop - 1, -1, -1):
                copy_f(d, 0).start()
                if d > 0:
                    copy_f(d, 1).start()

    @pl.when(c == 0)
    def _():
        with jax.named_scope("wait_f"):
            wait_for(marks, r_f)

    @pl.when(c == 1)
    def _():
        with jax.named_scope("wait_f"):
            wait_for(others, r_f)

    fits[0:1] = sum((marks[d] for d in range(1, n_pop)), marks[0])
    fits[1:2] = sum((ranked[d] for d in range(1, n_pop)), ranked[0])
    for which in range(2):
        wait_for(send.at[which, 2:units], sent)
    wait_for(send.at[2], sent)
    wait_for(first_v, sent)
    wait_for(lall.at[half_of], sent)
    wait_for(rall.at[half_of], sent)
    wait_for(ranked.at[half_of], sent)
    for core in range(2):
        @pl.when(c == core)
        def _(core=core):
            for i in range(core, pieces):
                copy_a0(i).wait_send()
            for i in range(1 - core, pieces):
                copy_y0(i).wait_send()
            if core == 1:
                copy_swapped.wait_send()
            if core == 0:
                copy_lin.wait_send()
                wait_for(post_in.at[0:2], sent)
            else:
                copy_far.wait_send()
                wait_for(post_in.at[0], sent)
                wait_for(marks, sent)
                wait_for(others, sent)


def in_hbm(x):
    return pltpu.with_memory_space_constraint(x, pltpu.HBM)


def fused_shards(
    n_pop, n_mp, context, out_weight, residual, target, norm_gain, left_factors, right_factors, member_ranks
):
    tok, width = context.shape
    full = out_weight.shape[1]
    mem = left_factors.shape[0]
    rows = full // n_pop
    chunks = width // BLK
    units = width // LANES
    pieces = tok // LANES
    ranks = member_ranks.reshape(1, mem)
    anywhere = pl.BlockSpec(memory_space=pltpu.HBM)
    vmem = pl.BlockSpec(memory_space=pltpu.VMEM)
    dma = pltpu.SemaphoreType.DMA
    acc = pltpu.VMEM((tok, LANES), F32)
    group = pltpu.VMEM((4 * mem, tok), F32)
    base, left_t, right_all, fits = pl.pallas_call(
        functools.partial(kernel, n_pop, n_mp),
        name="es_step",
        out_shape=(
            jax.ShapeDtypeStruct((tok, width), F32),
            jax.ShapeDtypeStruct((rows, n_pop * mem), F32),
            jax.ShapeDtypeStruct((n_pop * mem, width), BF),
            jax.ShapeDtypeStruct((2, n_pop * mem), F32),
        ),
        in_specs=[anywhere] * 8,
        out_specs=[vmem] * 4,
        scratch_shapes=[
            pltpu.VMEM((4, chunks, width, BLK), BF),
            pltpu.VMEM((tok, width), BF),
            pltpu.VMEM((tok, width), BF),
            pltpu.VMEM((tok, width), BF),
            pltpu.VMEM((mem, width), BF),
            pltpu.VMEM((1, full), F32),
            pltpu.VMEM((mem, full), BF),
            pltpu.VMEM((1, mem), jnp.int32),
            pltpu.VMEM((3, units, tok, LANES), BF),
            pltpu.VMEM((3, units, tok, LANES), BF),
            pltpu.VMEM((2, LANES, LANES), BF),
            pltpu.VMEM((2, 2, LANES, LANES), BF),
            pltpu.VMEM((n_pop, mem, rows), BF),
            pltpu.VMEM((n_pop, mem, width), BF),
            acc, acc, acc, acc,
            group, group, group, group,
            pltpu.VMEM((pieces, 4, LANES), F32),
            pltpu.VMEM((n_mp - 1, pieces, 4, LANES), F32),
            pltpu.VMEM((LANES, LANES), BF),
            pltpu.VMEM((LANES, LANES), BF),
            pltpu.VMEM((n_pop, 1, LANES), F32),
            pltpu.VMEM((n_pop * mem, rows), F32),
            pltpu.VMEM((n_pop, 1, LANES), F32),
            dma((2,)),
            dma((2,)),
            dma,
            dma((3,)),
            dma,
            dma((chunks - 1 + pieces,)),
            dma((chunks - 1 + 2 * pieces,)),
        ]
        + [dma] * 10
        + [pltpu.SemaphoreType.REGULAR((3,))],
        compiler_params=pltpu.CompilerParams(
            collective_id=0, has_side_effects=True, vmem_limit_bytes=48 * 1024 * 1024
        ),
    )(
        *map(in_hbm, (
            context, out_weight, residual, target, norm_gain.reshape(1, full), left_factors,
            right_factors, ranks,
        ))
    )
    count_all = n_pop * mem
    update, base, fitness = pl.pallas_call(
        functools.partial(finish, n_pop, math.sqrt(count_all) / SIGMA, tok * full),
        name="es_update",
        out_shape=(
            jax.ShapeDtypeStruct((rows, width), F32),
            jax.ShapeDtypeStruct((tok, width), F32),
            jax.ShapeDtypeStruct((1, mem), F32),
        ),
        in_specs=[vmem] * 4,
        out_specs=[anywhere] * 3,
        scratch_shapes=[
            pltpu.VMEM((rows, width), F32),
            pltpu.VMEM((1, mem), F32),
            dma((rows // 128 + 2,)),
        ],
        compiler_params=pltpu.CompilerParams(vmem_limit_bytes=16 * 1024 * 1024),
    )(left_t, right_all, base, fits)
    return (update, fitness.reshape(mem), base)


def finish(n_pop, scale, count, left_t, right_all, base_in, fits, update, base, fit, held, fit_v, sems):
    steps = held.shape[0] // 128
    mem = fit_v.shape[1]
    members = n_pop * mem
    copies = [
        pltpu.make_async_copy(base_in, base, sems.at[steps]),
        pltpu.make_async_copy(fit_v, fit, sems.at[steps + 1]),
    ]
    copies[0].start()
    all_fit = fits[0:1] * (-1.0 / count)
    centre = all_fit - jnp.sum(all_fit, axis=1, keepdims=True) / members
    deviation = jnp.sqrt(jnp.sum(centre * centre, axis=1, keepdims=True) / members + 1e-05)
    weight = fits[1:2] + centre / deviation / members
    for i in range(steps):
        part = slice(i * 128, (i + 1) * 128)
        weighted = (left_t[part, :] * weight).astype(BF)
        held[part, :] = jnp.dot(weighted, right_all[...], preferred_element_type=F32) * scale
        copies.append(pltpu.make_async_copy(held.at[part], update.at[part], sems.at[i]))
        copies[-1].start()
    p = lax.axis_index("pop")
    mine = jnp.zeros((1, mem), F32)
    for d in range(n_pop):
        mine = mine + jnp.where(p == d, 1.0, 0.0) * all_fit[:, d * mem:(d + 1) * mem]
    fit_v[...] = mine
    copies[1].start()
    for item in copies:
        item.wait()


def chosen(n_pop, n_mp, context, out_weight, *rest):
    tok, width = context.shape
    mem = rest[3].shape[0]
    full = out_weight.shape[1]
    chunks = width // BLK
    if n_mp == 4 and n_pop == 8 and width % BLK == 0 and chunks > 3 and (full // n_pop) % 128 == 0 and tok % 128 == 0 and mem == 16:
        return fused_shards(n_pop, n_mp, context, out_weight, *rest)
    return shards(context, out_weight, *rest)


def solution(mesh):
    in_specs = (
        P("pop", "mp"),
        P("mp", None),
        P("pop", "mp"),
        P("pop", "mp"),
        P(),
        P("pop", None),
        P("pop", None),
        P("pop"),
    )
    out_specs = (P("pop", "mp"), P("pop"), P("pop", "mp"))
    return jax.shard_map(
        functools.partial(chosen, mesh.shape["pop"], mesh.shape["mp"]), mesh=mesh, in_specs=in_specs, out_specs=out_specs, check_vma=False)
```

```python
import functools
import math

import jax
import jax.numpy as jnp
from jax import lax
from jax.experimental import pallas as pl
from jax.experimental.pallas import tpu as pltpu
from jax.sharding import PartitionSpec as P

SIGMA = 1.0
EPSILON = 1e-06


def error_sums(stream, lifted, right_rows, gain_part, target_rows, inverse):
    hidden = stream[:, None, :] + lifted[:, :, None] * right_rows[None, :, :]
    differ = gain_part * hidden * inverse[:, :, None] - target_rows[:, None, :]
    return jnp.sum(differ * differ, axis=(0, 2))


def utility(member_ranks, count_all):
    levels = jnp.arange(count_all).astype(jnp.float32)
    ceiling = math.log(count_all / 2 + 1)
    baseline = jnp.maximum(0.0, ceiling - jnp.log(levels + 1.0))
    shaped = jnp.maximum(0.0, ceiling - jnp.log(member_ranks.astype(jnp.float32) + 1.0))
    return shaped / jnp.sum(baseline) - 1.0 / count_all


def shards(
    context, out_weight, residual, target, norm_gain, left_factors, right_factors, member_ranks
):
    tok_count = context.shape[0]
    shard_width = context.shape[1]
    full_width = out_weight.shape[1]
    factor = SIGMA / math.sqrt(full_width)
    offset = lax.axis_index("mp") * shard_width
    left_cols = lax.dynamic_slice_in_dim(left_factors, offset, shard_width, 1)
    right_cols = lax.dynamic_slice_in_dim(right_factors, offset, shard_width, 1)
    partial_value = jnp.dot(context, out_weight, preferred_element_type=jnp.float32)
    projected = lax.dot_general(
        context, left_cols, (((1,), (1,)), ((), ())), preferred_element_type=jnp.float32
    )
    summed = lax.psum_scatter(
        partial_value.astype(jnp.bfloat16), "mp", scatter_dimension=1, tiled=True
    ).astype(jnp.float32)
    stream = residual.astype(jnp.float32) + summed
    gain_part = lax.dynamic_slice_in_dim(norm_gain, offset, shard_width, 0)
    factor_f = right_cols.astype(jnp.float32)
    crossed = jnp.dot(stream, factor_f.T, precision=lax.Precision.HIGHEST)
    per_token = jnp.sum(stream * stream, axis=1)
    per_member = jnp.sum(factor_f * factor_f, axis=1)
    projected, crossed, per_token, per_member = lax.psum(
        (projected, crossed, per_token, per_member), "mp"
    )
    lifted = factor * projected
    meansq = (
        per_token[:, None] + 2.0 * lifted * crossed + lifted * lifted * per_member[None, :]
    ) / full_width
    inverse = lax.rsqrt(meansq + EPSILON)
    local_error = error_sums(
        stream, lifted, factor_f, gain_part, target.astype(jnp.float32), inverse
    )
    member_total = lax.psum(local_error, "mp")
    fitness = -member_total / (tok_count * full_width)
    everyone = lax.all_gather(fitness, "pop", axis=0, tiled=True)
    count_all = everyone.shape[0]
    average = jnp.mean(everyone)
    centre = everyone - average
    spread = jnp.sqrt(jnp.mean(centre * centre) + 1e-05)
    weight = utility(member_ranks, count_all) + (fitness - average) / spread / count_all
    weighted = (weight[:, None] * left_factors.astype(jnp.float32)).astype(jnp.bfloat16)
    weighted_rows = lax.all_to_all(weighted, "pop", split_axis=1, concat_axis=0, tiled=True)
    right_all = lax.all_gather(right_cols, "pop", axis=0, tiled=True)
    update = lax.dot_general(
        weighted_rows, right_all, (((0,), (0,)), ((), ())), preferred_element_type=jnp.float32
    ) * (math.sqrt(count_all) / SIGMA)
    return (update, fitness, stream)


BLK = 256
LANES = 128
F32 = jnp.float32
BF = jnp.bfloat16


def nt_dot(a, b):
    return lax.dot_general(a, b, (((1,), (1,)), ((), ())), preferred_element_type=F32)


def split_two(x):
    hi = x.astype(BF)
    return hi, (x - hi.astype(F32)).astype(BF)


def halves(parts):
    return jnp.concatenate([piece for part in parts for piece in split_two(part)], axis=1)


def row_picker(count):
    shape = (8, count * 2 * LANES)
    owner = lax.broadcasted_iota(jnp.int32, shape, 1) // (2 * LANES)
    return jnp.where(owner == lax.broadcasted_iota(jnp.int32, shape, 0), 1.0, 0.0).astype(BF)


def flip(index, bits):
    for bit in (1, 2, 4):
        if bits & bit:
            index = index + bit - 2 * bit * ((index // bit) % 2)
    return index


def kernel(
    n_pop, n_mp, ctx_h, w_h, res_h, tgt_h, gain_h, left_h, right_h, ranks_h,
    base, left_t, right_all, fits,
    w_v, ctx, res, tgt, lcols, gain, right, ranks, send, recv, first_v, direct, lall, rall,
    sq_s, sq_a, sq_e, sq_t, lin, lin_in, lin_out, lin_far, post, post_in, swap, swap_in, marks, left_v, ranked,
    w_sem, top_sem, near_sem, loc_sem, sent, r_a, r_y, r_b, r_top, r_lin, r_far, r_post, r_swap, r_l, r_r, r_u, r_f, rounds,
):
    tok, width = ctx.shape
    mem = right.shape[0]
    full = right.shape[1]
    rows = full // n_pop
    chunks = width // BLK
    units = width // LANES
    last = units - 1
    pieces = tok // LANES
    upper = 96
    low = (tok - upper) // 2
    cuts = [(0, upper), (upper, upper + low), (upper + low, tok)]
    members = mem * n_pop
    p = lax.axis_index("pop")
    q = lax.axis_index("mp")
    y = q // 2
    c = q % 2
    mate = flip(q, 1)
    across = flip(q, 2)
    diagonal = flip(q, 3)
    blocks = (diagonal, across, mate, q)
    other = 2 - 2 * y

    def remote(src, dst, ss, rs, pop, mp):
        return pltpu.make_async_remote_copy(
            src_ref=src, dst_ref=dst, send_sem=ss, recv_sem=rs,
            device_id=(pop, mp), device_id_type=pl.DeviceIdType.MESH,
        )

    def signal(sem, pop, mp):
        pl.semaphore_signal(sem, inc=1, device_id=(pop, mp), device_id_type=pl.DeviceIdType.MESH)

    def wait_for(ref, sem):
        pltpu.make_async_copy(ref, ref, sem).wait()

    def w_copy(s, k, sem):
        start = pl.multiple_of(blocks[s] * width + k * BLK, BLK)
        return pltpu.make_async_copy(w_h.at[:, pl.ds(start, BLK)], w_v.at[s, k], sem)

    def w_first(n):
        start = pl.multiple_of((other + n) * width, BLK)
        slot = 1 - c if n == 0 else c
        return pltpu.make_async_copy(w_h.at[:, pl.ds(start, BLK)], w_v.at[slot, 0], top_sem.at[n])

    def near_copy(k):
        return w_copy(3, k, near_sem)

    def w_step(k, more):
        steps = [(1, k), (2, k)] if isinstance(k, jax.Array) or k > 0 else [(2, k)]
        if more:
            steps.append((0, k + 1))
        return [w_copy(s, i, w_sem.at[k % 2]) for s, i in steps]

    my_cols = pl.ds(pl.multiple_of(q * width, BLK), width)
    my_rows = pl.ds(pl.multiple_of(p * rows, LANES), rows)
    locals_ = [
        pltpu.make_async_copy(ctx_h.at[0:upper], ctx.at[0:upper], loc_sem.at[0]),
        pltpu.make_async_copy(ctx_h.at[upper:tok], ctx.at[upper:tok], loc_sem.at[1]),
        pltpu.make_async_copy(res_h, res, loc_sem.at[2]),
        pltpu.make_async_copy(tgt_h, tgt, loc_sem.at[2]),
        pltpu.make_async_copy(left_h.at[:, my_cols], lcols, loc_sem.at[2]),
        pltpu.make_async_copy(left_h.at[:, my_rows], lall.at[0], loc_sem.at[2]),
        pltpu.make_async_copy(right_h.at[:, my_cols], rall.at[0], loc_sem.at[2]),
        pltpu.make_async_copy(gain_h, gain, loc_sem.at[2]),
        pltpu.make_async_copy(right_h, right, loc_sem.at[2]),
        pltpu.make_async_copy(ranks_h, ranks, loc_sem.at[2]),
    ]
    locals_[0].start()
    w_first(0).start()

    barrier = pltpu.get_barrier_semaphore()
    for peer in (mate, across, diagonal):
        signal(barrier, p, peer)
    locals_[1].start()
    for bit in (1, 2, 4):
        signal(barrier, flip(p, bit), q)

    copy_top = remote(first_v, direct.at[c], sent, r_top, p, other)

    def copy_a(k):
        cols = pl.ds(2 * k, 2)
        return remote(send.at[0, cols], recv.at[0, cols], sent, r_a.at[pieces + k - 1], p, mate)

    tail = slice(0, LANES)

    def strip(i):
        return slice(*cuts[i])

    def copy_a0(i):
        return remote(send.at[0, 0:2, strip(i)], recv.at[0, 0:2, strip(i)], sent, r_a.at[i], p, mate)

    def copy_y0(i):
        return remote(send.at[1, 0:2, strip(i)], recv.at[1, 0:2, strip(i)], sent, r_y.at[i], p, across)

    def copy_y(k, count=2):
        cols = pl.ds(2 * k, count)
        return remote(send.at[1, cols], recv.at[1, cols], sent, r_y.at[pieces + k - 1], p, across)

    def copy_end(i):
        part = slice(i * LANES, (i + 1) * LANES)
        return remote(send.at[1, last, part], recv.at[1, last, part], sent, r_y.at[pieces + chunks - 1 + i], p, across)

    copy_swap = remote(send.at[1, last, tail], swap_in, sent, r_swap, p, mate)
    copy_swapped = remote(swap, recv.at[1, last, tail], sent, r_y.at[pieces + chunks - 1], p, diagonal)

    def copy_b(k):
        cols = pl.ds(2 * k, 2)
        return remote(send.at[2, cols], recv.at[2, cols], sent, r_b, p, mate)

    def copy_l(d):
        peer = flip(p, d)
        cols = pl.ds(pl.multiple_of(peer * rows, LANES), rows)
        return remote(left_h.at[:, cols], lall.at[d], sent, r_l, peer, q)

    def copy_r(d):
        return remote(right_h.at[:, my_cols], rall.at[d], sent, r_r, flip(p, d), q)

    def copy_u(d):
        return remote(ranked.at[0], ranked.at[d], sent, r_u, flip(p, d), q)

    def copy_f(d, core):
        return remote(marks.at[0], marks.at[d], sent, r_f, flip(p, d), 2 * y + core)

    copy_lin = remote(lin, lin_in, sent, r_lin, p, mate)
    copy_far = remote(lin_out, lin_far, sent, r_far, p, across)

    def copy_post(i, d):
        return remote(post.at[i], post_in.at[d - 1, i], sent, r_post, p, flip(q, d))

    def split_store(which, k, value):
        send[which, 2 * k] = value[:, :LANES]
        send[which, 2 * k + 1] = value[:, LANES:]

    def product(s, k):
        return jnp.dot(ctx[...], w_v[s, k], preferred_element_type=F32)

    everything = slice(0, tok)
    order = [*range(1, pieces), 0]
    with jax.named_scope("load0"):
        locals_[0].wait()
        w_first(0).wait()
    w_first(1).start()
    top = jnp.dot(ctx[0:upper, :], w_v[1 - c, 0], preferred_element_type=F32).astype(BF)
    first_v[0] = top[:, :LANES]
    first_v[1] = top[:, LANES:]
    def strip_product(s, i):
        return jnp.dot(ctx[strip(i), :], w_v[s, 0], preferred_element_type=F32)

    def prepare(i):
        value = strip_product(0, i).astype(BF)
        send[0, 0, strip(i)] = value[:, :LANES]
        send[0, 1, strip(i)] = value[:, LANES:]

    def give(i):
        prepare(i)
        copy_a0(i).start()

    @pl.when((c == 1) & (y == 0))
    def _():
        locals_[1].wait()
        prepare(1)

    with jax.named_scope("barrier"):
        pl.semaphore_wait(barrier, 6)
    copy_top.start()
    signal(rounds.at[0], flip(p, 1), q)
    for item in w_step(0, True):
        item.start()

    @pl.when((c == 0) | (y == 1))
    def _():
        locals_[1].wait()

    def pass_on(i, value):
        send[1, 0, strip(i)] = (value[:, :LANES] + recv[0, 0, strip(i)].astype(F32)).astype(BF)
        send[1, 1, strip(i)] = (value[:, LANES:] + recv[0, 1, strip(i)].astype(F32)).astype(BF)
        copy_y0(i).start()

    @pl.when(c == 0)
    def _():
        mine = [strip_product(1, i) for i in (1, 2)]
        copy_a0(1).wait_recv()
        pass_on(1, mine[0])
        w_first(1).wait()
        give(1)
        copy_a0(2).wait_recv()
        pass_on(2, mine[1])
        give(2)
        give(0)
        send[1, 0, strip(0)] = first_v[0]
        send[1, 1, strip(0)] = first_v[1]

    @pl.when((c == 1) & (y == 1))
    def _():
        prepare(1)

    @pl.when(c == 1)
    def _():
        copy_a0(1).start()
        give(2)
        send[0, 0, strip(0)] = first_v[0]
        send[0, 1, strip(0)] = first_v[1]
        w_first(1).wait()

    for item in w_step(1, True):
        item.start()
    near_copy(0).start()
    for item in w_step(0, True):
        item.wait()
    split_store(0, 1, product(0, 1).astype(BF))
    copy_a(1).start()
    for item in w_step(2, True):
        item.start()

    @pl.when(c == 1)
    def _():
        mine = [strip_product(1, i) for i in (1, 2, 0)]
        with jax.named_scope("wait_a0"):
            for i in (1, 2, 0):
                copy_a0(i).wait_recv()
                pass_on(i, mine[i - 1])


    def far(k, carry):
        for item in w_step(k, False):
            item.wait()

        @pl.when(k + 1 < chunks)
        def _():
            w_copy(0, k + 1, w_sem.at[k % 2]).wait()

        mine = product(1, k)
        with jax.named_scope("wait_a"):
            copy_a(k).wait_recv()
        send[1, 2 * k] = (mine[:, :LANES] + recv[0, 2 * k].astype(F32)).astype(BF)
        send[1, 2 * k + 1] = (mine[:, LANES:] + recv[0, 2 * k + 1].astype(F32)).astype(BF)

        @pl.when(k + 1 < chunks)
        def _():
            copy_y(k).start()

        @pl.when((k + 1 == chunks) & (c == 0))
        def _():
            send[1, last, tail] = mine[0:LANES, LANES:].astype(BF)
            copy_swap.start()

        @pl.when(k + 2 < chunks)
        def _():
            for item in w_step(k + 2, False):
                item.start()

        @pl.when(k + 3 < chunks)
        def _():
            w_copy(0, k + 3, w_sem.at[k % 2]).start()

        near_copy(k).start()

        @pl.when(k == 1)
        def _():
            for item in locals_[2:]:
                item.start()
            pl.semaphore_wait(rounds.at[0], 1)
            signal(rounds.at[1], flip(p, 2), q)

        @pl.when(k == 2)
        def _():
            pl.semaphore_wait(rounds.at[1], 1)
            signal(rounds.at[2], flip(p, 4), q)

        @pl.when(k == 3)
        def _():
            pl.semaphore_wait(rounds.at[2], 1)
            for d in range(1, n_pop):
                copy_r(n_pop - d).start()
                copy_l(n_pop - d).start()

        @pl.when(k + 1 < chunks)
        def _():
            split_store(0, k + 1, product(0, k + 1).astype(BF))
            copy_a(k + 1).start()

        @pl.when(k == 1)
        def _():
            split_store(2, 0, product(2, 0).astype(BF))
            copy_b(0).start()

        split_store(2, k, product(2, k).astype(BF))
        copy_b(k).start()
        return carry

    with jax.named_scope("far"):
        lax.fori_loop(1, chunks, far, 0)

    for item in locals_[2:]:
        item.wait()
    wait_for(w_v.at[3], near_sem)

    lane = lax.broadcasted_iota(jnp.int32, (1, LANES), 1)
    ceiling = math.log(members / 2 + 1)
    whole = sum(max(0.0, ceiling - math.log(i + 1.0)) for i in range(members))
    shaped = jnp.maximum(0.0, ceiling - jnp.log(ranks[...].astype(F32) + 1.0)) / whole - 1.0 / members
    ranked[0] = jnp.where(lane // mem == p, jnp.concatenate([shaped] * n_pop, axis=1), 0.0)
    for d in range(1, n_pop):
        copy_u(d).start()

    def near(k, carry):
        cols = pl.ds(pl.multiple_of(k * BLK, BLK), BLK)
        base[:, cols] = product(3, k) + res[:, cols].astype(F32)
        return carry

    with jax.named_scope("near"):
        lax.fori_loop(0, chunks, near, 0)

    @pl.when(c == 1)
    def _():
        copy_swap.wait_recv()
        swap[...] = (send[0, last, tail].astype(F32) + swap_in[...].astype(F32)).astype(BF)
        copy_swapped.start()

    copy_y(chunks - 1, 1).start()

    def spread(slot, value):
        lin[slot * mem:(slot + 1) * mem, :] = value

    with jax.named_scope("early"):
        r_mine = rall[0].astype(F32)
        gr_hi, gr_lo = split_two(r_mine * gain[:, my_cols])
        spread(0, nt_dot(lcols[...], ctx[...]))
        spread(1, nt_dot(gr_hi, tgt[...]) + nt_dot(gr_lo, tgt[...]))
        r_full = right[...].astype(F32)
        gr_full = r_full * gain[...]
        norm_r = jnp.sum(r_full * r_full, axis=1, keepdims=True)
        norm_gr = jnp.sum(gr_full * gr_full, axis=1, keepdims=True)
        for acc in (sq_s, sq_a, sq_e, sq_t):
            acc[...] = jnp.zeros_like(acc)

    def mixed(block, start, size):
        cols = pl.ds(pl.multiple_of(block * width + start, LANES), size)
        r = right[:, cols]
        g = gain[:, cols]
        hi, low = split_two(r.astype(F32) * (g * g))
        return jnp.concatenate([r, hi, low], axis=0)

    def linear(k, carry):
        crossed, crossed_g = carry
        near_rows = mixed(q, k * BLK, BLK)
        far_rows = mixed(across, k * BLK, BLK)
        for h in range(2):
            cols = pl.ds(pl.multiple_of(k * BLK + h * LANES, LANES), LANES)
            part = slice(h * LANES, (h + 1) * LANES)
            u = 2 * k + h
            s = base[:, cols] + recv[2, u].astype(F32)
            base[:, cols] = s
            hi, low = split_two(s)
            both = nt_dot(near_rows[:, part], hi) + nt_dot(near_rows[:, part], low) + nt_dot(far_rows[:, part], send[1, u])
            crossed = crossed + both[0:mem]
            crossed_g = crossed_g + both[mem:2 * mem] + both[2 * mem:3 * mem]
            wide = tgt[:, cols].astype(F32)
            sq_t[...] += wide * wide
        return crossed, crossed_g

    with jax.named_scope("wait_b"):
        wait_for(recv.at[2], r_b)
    with jax.named_scope("linear"):
        top_rows = mixed(other, 0, BLK)
        top = nt_dot(top_rows[:, :LANES], first_v[0]) + nt_dot(top_rows[:, LANES:], first_v[1])
        late = nt_dot(mixed(other, last * LANES, LANES), send[0, last, tail])
        top = sum(jnp.concatenate([v, jnp.zeros((3 * mem, tok - v.shape[1]), F32)], axis=1) for v in (top, late))
        top = top * jnp.where(c == 1, 1.0, 0.0)
        carry = (top[0:mem], top[mem:2 * mem] + top[2 * mem:3 * mem])
        crossed, crossed_g = lax.fori_loop(0, chunks, linear, carry)
        spread(2, crossed)
        spread(3, crossed_g)

    @pl.when(c == 0)
    def _():
        copy_lin.start()
        for i in order[:-1]:
            copy_end(i).start()

    def arrived(u, part):
        cols = pl.ds(pl.multiple_of(u * LANES, LANES), LANES)
        gain_u = gain[:, pl.ds(pl.multiple_of(q * width + u * LANES, LANES), LANES)]
        s = base[part, cols] + recv[1, u, part].astype(F32)
        base[part, cols] = s
        gs = s * gain_u
        return s * s, gs * gs, gs * tgt[part, cols].astype(F32)

    def settle(u, carry):
        for acc, item in zip((sq_s, sq_a, sq_e), arrived(u, everything)):
            acc[...] += item
        return carry

    with jax.named_scope("wait_y0"):
        for i in range(1, pieces):
            copy_y0(i).wait_recv()

        @pl.when(c == 0)
        def _():
            wait_for(direct, r_top)
            for u in range(2):
                recv[1, u, strip(0)] = jnp.zeros((upper, LANES), BF)
                base[0:upper, u * LANES:(u + 1) * LANES] += direct[0, u].astype(F32) + direct[1, u].astype(F32)

        @pl.when(c == 1)
        def _():
            copy_y0(0).wait_recv()

    lax.fori_loop(0, 2, settle, 0)

    @pl.when(c == 1)
    def _():
        for i in order:
            copy_end(i).start()
        with jax.named_scope("wait_lin"):
            copy_lin.wait_recv()
        lin_out[...] = lin[...] + lin_in[...]
        copy_far.start()

    def settle_chunk(k, carry):
        with jax.named_scope("wait_y"):
            copy_y(k).wait_recv()
        settle(2 * k, 0)
        settle(2 * k + 1, 0)
        return carry

    with jax.named_scope("settle"):
        lax.fori_loop(1, chunks - 1, settle_chunk, 0)
    half_of = slice(1, n_pop)
    with jax.named_scope("wait_lr"):
        wait_for(lall.at[half_of], r_l)
        wait_for(rall.at[half_of], r_r)
        wait_for(ranked.at[half_of], r_u)
    with jax.named_scope("turn"):
        for d in range(n_pop):
            place = pl.ds(pl.multiple_of(flip(p, d) * mem, mem), mem)
            right_all[place, :] = rall[d]
            left_v[place, :] = lall[d].astype(F32)
        left_t[...] = left_v[...].T
    with jax.named_scope("wait_y8"):
        copy_y(chunks - 1, 1).wait_recv()
    settle(last - 1, 0)
    before = nt_dot(row_picker(4), halves((sq_s[...], sq_a[...], sq_e[...], sq_t[...])))
    picker = row_picker(3)
    for i in order:
        part = slice(i * LANES, (i + 1) * LANES)
        with jax.named_scope("wait_end"):
            copy_end(i).wait_recv()
        with jax.named_scope("end"):
            post[i] = (before[:, part] + nt_dot(picker, halves(arrived(last, part))))[0:4]

            @pl.when(c == 0)
            def _():
                copy_post(i, 3).start()
                copy_post(i, 1).start()

            @pl.when(c == 1)
            def _():
                copy_post(i, 2).start()

    others = marks.at[half_of]

    @pl.when(c == 1)
    def _():
        with jax.named_scope("wait_far"):
            copy_far.wait_recv()
        own = lin_out[...] + lin_far[...]
        lifted = own[0:mem] * (SIGMA / math.sqrt(full))
        lifted2 = lifted * lifted
        extra_s = 2.0 * lifted * own[2 * mem:3 * mem] + lifted2 * norm_r
        extra_a = 2.0 * lifted * own[3 * mem:4 * mem] + lifted2 * norm_gr
        extra_e = lifted * own[mem:2 * mem]
        with jax.named_scope("wait_post"):
            wait_for(post_in, r_post)
        with jax.named_scope("errors"):
            late = jnp.concatenate([post[i] + post_in[0, i] + post_in[1, i] + post_in[2, i] for i in range(pieces)], axis=1)
            meansq = (late[0:1] + extra_s) / full
            inverse = lax.rsqrt(meansq + EPSILON)
            errors = inverse * inverse * (late[1:2] + extra_a) - 2.0 * inverse * (late[2:3] + extra_e) + late[3:4]
            summed = jnp.sum(errors, axis=1, keepdims=True)
            spot = lax.broadcasted_iota(jnp.int32, (mem, LANES), 0) + p * mem
            here = lax.broadcasted_iota(jnp.int32, (mem, LANES), 1) == spot
            marks[0] = jnp.sum(jnp.where(here, summed, 0.0), axis=0, keepdims=True)
            for d in range(n_pop - 1, -1, -1):
                copy_f(d, 0).start()
                if d > 0:
                    copy_f(d, 1).start()

    @pl.when(c == 0)
    def _():
        with jax.named_scope("wait_f"):
            wait_for(marks, r_f)

    @pl.when(c == 1)
    def _():
        with jax.named_scope("wait_f"):
            wait_for(others, r_f)

    fits[0:1] = sum((marks[d] for d in range(1, n_pop)), marks[0])
    fits[1:2] = sum((ranked[d] for d in range(1, n_pop)), ranked[0])
    for which in range(2):
        wait_for(send.at[which, 2:units], sent)
    wait_for(send.at[2], sent)
    wait_for(first_v, sent)
    wait_for(lall.at[half_of], sent)
    wait_for(rall.at[half_of], sent)
    wait_for(ranked.at[half_of], sent)
    for core in range(2):
        @pl.when(c == core)
        def _(core=core):
            for i in range(core, pieces):
                copy_a0(i).wait_send()
            for i in range(1 - core, pieces):
                copy_y0(i).wait_send()
            if core == 1:
                copy_swapped.wait_send()
            if core == 0:
                copy_lin.wait_send()
                wait_for(post_in.at[0:2], sent)
            else:
                copy_far.wait_send()
                wait_for(post_in.at[0], sent)
                wait_for(marks, sent)
                wait_for(others, sent)


def in_hbm(x):
    return pltpu.with_memory_space_constraint(x, pltpu.HBM)


def fused_shards(
    n_pop, n_mp, context, out_weight, residual, target, norm_gain, left_factors, right_factors, member_ranks
):
    tok, width = context.shape
    full = out_weight.shape[1]
    mem = left_factors.shape[0]
    rows = full // n_pop
    chunks = width // BLK
    units = width // LANES
    pieces = tok // LANES
    ranks = member_ranks.reshape(1, mem)
    anywhere = pl.BlockSpec(memory_space=pltpu.HBM)
    vmem = pl.BlockSpec(memory_space=pltpu.VMEM)
    dma = pltpu.SemaphoreType.DMA
    acc = pltpu.VMEM((tok, LANES), F32)
    group = pltpu.VMEM((4 * mem, tok), F32)
    base, left_t, right_all, fits = pl.pallas_call(
        functools.partial(kernel, n_pop, n_mp),
        name="es_step",
        out_shape=(
            jax.ShapeDtypeStruct((tok, width), F32),
            jax.ShapeDtypeStruct((rows, n_pop * mem), F32),
            jax.ShapeDtypeStruct((n_pop * mem, width), BF),
            jax.ShapeDtypeStruct((2, n_pop * mem), F32),
        ),
        in_specs=[anywhere] * 8,
        out_specs=[vmem] * 4,
        scratch_shapes=[
            pltpu.VMEM((4, chunks, width, BLK), BF),
            pltpu.VMEM((tok, width), BF),
            pltpu.VMEM((tok, width), BF),
            pltpu.VMEM((tok, width), BF),
            pltpu.VMEM((mem, width), BF),
            pltpu.VMEM((1, full), F32),
            pltpu.VMEM((mem, full), BF),
            pltpu.VMEM((1, mem), jnp.int32),
            pltpu.VMEM((3, units, tok, LANES), BF),
            pltpu.VMEM((3, units, tok, LANES), BF),
            pltpu.VMEM((2, 96, LANES), BF),
            pltpu.VMEM((2, 2, 96, LANES), BF),
            pltpu.VMEM((n_pop, mem, rows), BF),
            pltpu.VMEM((n_pop, mem, width), BF),
            acc, acc, acc, acc,
            group, group, group, group,
            pltpu.VMEM((pieces, 4, LANES), F32),
            pltpu.VMEM((n_mp - 1, pieces, 4, LANES), F32),
            pltpu.VMEM((LANES, LANES), BF),
            pltpu.VMEM((LANES, LANES), BF),
            pltpu.VMEM((n_pop, 1, LANES), F32),
            pltpu.VMEM((n_pop * mem, rows), F32),
            pltpu.VMEM((n_pop, 1, LANES), F32),
            dma((2,)),
            dma((2,)),
            dma,
            dma((3,)),
            dma,
            dma((chunks - 1 + pieces,)),
            dma((chunks - 1 + 2 * pieces,)),
        ]
        + [dma] * 10
        + [pltpu.SemaphoreType.REGULAR((3,))],
        compiler_params=pltpu.CompilerParams(
            collective_id=0, has_side_effects=True, vmem_limit_bytes=48 * 1024 * 1024
        ),
    )(
        *map(in_hbm, (
            context, out_weight, residual, target, norm_gain.reshape(1, full), left_factors,
            right_factors, ranks,
        ))
    )
    count_all = n_pop * mem
    update, base, fitness = pl.pallas_call(
        functools.partial(finish, n_pop, math.sqrt(count_all) / SIGMA, tok * full),
        name="es_update",
        out_shape=(
            jax.ShapeDtypeStruct((rows, width), F32),
            jax.ShapeDtypeStruct((tok, width), F32),
            jax.ShapeDtypeStruct((1, mem), F32),
        ),
        in_specs=[vmem] * 4,
        out_specs=[anywhere] * 3,
        scratch_shapes=[
            pltpu.VMEM((rows, width), F32),
            pltpu.VMEM((1, mem), F32),
            dma((rows // 128 + 2,)),
        ],
        compiler_params=pltpu.CompilerParams(vmem_limit_bytes=16 * 1024 * 1024),
    )(left_t, right_all, base, fits)
    return (update, fitness.reshape(mem), base)


def finish(n_pop, scale, count, left_t, right_all, base_in, fits, update, base, fit, held, fit_v, sems):
    steps = held.shape[0] // 128
    mem = fit_v.shape[1]
    members = n_pop * mem
    copies = [
        pltpu.make_async_copy(base_in, base, sems.at[steps]),
        pltpu.make_async_copy(fit_v, fit, sems.at[steps + 1]),
    ]
    copies[0].start()
    all_fit = fits[0:1] * (-1.0 / count)
    centre = all_fit - jnp.sum(all_fit, axis=1, keepdims=True) / members
    deviation = jnp.sqrt(jnp.sum(centre * centre, axis=1, keepdims=True) / members + 1e-05)
    weight = fits[1:2] + centre / deviation / members
    for i in range(steps):
        part = slice(i * 128, (i + 1) * 128)
        weighted = (left_t[part, :] * weight).astype(BF)
        held[part, :] = jnp.dot(weighted, right_all[...], preferred_element_type=F32) * scale
        copies.append(pltpu.make_async_copy(held.at[part], update.at[part], sems.at[i]))
        copies[-1].start()
    p = lax.axis_index("pop")
    mine = jnp.zeros((1, mem), F32)
    for d in range(n_pop):
        mine = mine + jnp.where(p == d, 1.0, 0.0) * all_fit[:, d * mem:(d + 1) * mem]
    fit_v[...] = mine
    copies[1].start()
    for item in copies:
        item.wait()


def chosen(n_pop, n_mp, context, out_weight, *rest):
    tok, width = context.shape
    mem = rest[3].shape[0]
    full = out_weight.shape[1]
    chunks = width // BLK
    if n_mp == 4 and n_pop == 8 and width % BLK == 0 and chunks > 3 and (full // n_pop) % 128 == 0 and tok % 128 == 0 and mem == 16:
        return fused_shards(n_pop, n_mp, context, out_weight, *rest)
    return shards(context, out_weight, *rest)


def solution(mesh):
    in_specs = (
        P("pop", "mp"),
        P("mp", None),
        P("pop", "mp"),
        P("pop", "mp"),
        P(),
        P("pop", None),
        P("pop", None),
        P("pop"),
    )
    out_specs = (P("pop", "mp"), P("pop"), P("pop", "mp"))
    return jax.shard_map(
        functools.partial(chosen, mesh.shape["pop"], mesh.shape["mp"]), mesh=mesh, in_specs=in_specs, out_specs=out_specs, check_vma=False)
```

```python
import functools
import math

import jax
import jax.numpy as jnp
from jax import lax
from jax.experimental import pallas as pl
from jax.experimental.pallas import tpu as pltpu
from jax.sharding import PartitionSpec as P

SIGMA = 1.0
EPSILON = 1e-06


def error_sums(stream, lifted, right_rows, gain_part, target_rows, inverse):
    hidden = stream[:, None, :] + lifted[:, :, None] * right_rows[None, :, :]
    differ = gain_part * hidden * inverse[:, :, None] - target_rows[:, None, :]
    return jnp.sum(differ * differ, axis=(0, 2))


def utility(member_ranks, count_all):
    levels = jnp.arange(count_all).astype(jnp.float32)
    ceiling = math.log(count_all / 2 + 1)
    baseline = jnp.maximum(0.0, ceiling - jnp.log(levels + 1.0))
    shaped = jnp.maximum(0.0, ceiling - jnp.log(member_ranks.astype(jnp.float32) + 1.0))
    return shaped / jnp.sum(baseline) - 1.0 / count_all


def shards(
    context, out_weight, residual, target, norm_gain, left_factors, right_factors, member_ranks
):
    tok_count = context.shape[0]
    shard_width = context.shape[1]
    full_width = out_weight.shape[1]
    factor = SIGMA / math.sqrt(full_width)
    offset = lax.axis_index("mp") * shard_width
    left_cols = lax.dynamic_slice_in_dim(left_factors, offset, shard_width, 1)
    right_cols = lax.dynamic_slice_in_dim(right_factors, offset, shard_width, 1)
    partial_value = jnp.dot(context, out_weight, preferred_element_type=jnp.float32)
    projected = lax.dot_general(
        context, left_cols, (((1,), (1,)), ((), ())), preferred_element_type=jnp.float32
    )
    summed = lax.psum_scatter(
        partial_value.astype(jnp.bfloat16), "mp", scatter_dimension=1, tiled=True
    ).astype(jnp.float32)
    stream = residual.astype(jnp.float32) + summed
    gain_part = lax.dynamic_slice_in_dim(norm_gain, offset, shard_width, 0)
    factor_f = right_cols.astype(jnp.float32)
    crossed = jnp.dot(stream, factor_f.T, precision=lax.Precision.HIGHEST)
    per_token = jnp.sum(stream * stream, axis=1)
    per_member = jnp.sum(factor_f * factor_f, axis=1)
    projected, crossed, per_token, per_member = lax.psum(
        (projected, crossed, per_token, per_member), "mp"
    )
    lifted = factor * projected
    meansq = (
        per_token[:, None] + 2.0 * lifted * crossed + lifted * lifted * per_member[None, :]
    ) / full_width
    inverse = lax.rsqrt(meansq + EPSILON)
    local_error = error_sums(
        stream, lifted, factor_f, gain_part, target.astype(jnp.float32), inverse
    )
    member_total = lax.psum(local_error, "mp")
    fitness = -member_total / (tok_count * full_width)
    everyone = lax.all_gather(fitness, "pop", axis=0, tiled=True)
    count_all = everyone.shape[0]
    average = jnp.mean(everyone)
    centre = everyone - average
    spread = jnp.sqrt(jnp.mean(centre * centre) + 1e-05)
    weight = utility(member_ranks, count_all) + (fitness - average) / spread / count_all
    weighted = (weight[:, None] * left_factors.astype(jnp.float32)).astype(jnp.bfloat16)
    weighted_rows = lax.all_to_all(weighted, "pop", split_axis=1, concat_axis=0, tiled=True)
    right_all = lax.all_gather(right_cols, "pop", axis=0, tiled=True)
    update = lax.dot_general(
        weighted_rows, right_all, (((0,), (0,)), ((), ())), preferred_element_type=jnp.float32
    ) * (math.sqrt(count_all) / SIGMA)
    return (update, fitness, stream)


BLK = 256
LANES = 128
F32 = jnp.float32
BF = jnp.bfloat16


def nt_dot(a, b):
    return lax.dot_general(a, b, (((1,), (1,)), ((), ())), preferred_element_type=F32)


def split_two(x):
    hi = x.astype(BF)
    return hi, (x - hi.astype(F32)).astype(BF)


def halves(parts):
    return jnp.concatenate([piece for part in parts for piece in split_two(part)], axis=1)


def row_picker(count):
    shape = (8, count * 2 * LANES)
    owner = lax.broadcasted_iota(jnp.int32, shape, 1) // (2 * LANES)
    return jnp.where(owner == lax.broadcasted_iota(jnp.int32, shape, 0), 1.0, 0.0).astype(BF)


def flip(index, bits):
    for bit in (1, 2, 4):
        if bits & bit:
            index = index + bit - 2 * bit * ((index // bit) % 2)
    return index


def kernel(
    n_pop, n_mp, ctx_h, w_h, res_h, tgt_h, gain_h, left_h, right_h, ranks_h,
    base, left_t, right_all, fits,
    w_v, ctx, res, tgt, lcols, gain, right, ranks, send, recv, first_v, direct, lall, rall,
    sq_s, sq_a, sq_e, sq_t, lin, lin_in, lin_out, lin_far, post, post_in, swap, swap_in, marks, left_v, ranked,
    w_sem, top_sem, loc_sem, sent, r_a, r_y, r_b, r_top, r_lin, r_far, r_post, r_swap, r_l, r_r, r_u, r_f, rounds,
):
    tok, width = ctx.shape
    mem = right.shape[0]
    full = right.shape[1]
    rows = full // n_pop
    chunks = width // BLK
    units = width // LANES
    last = units - 1
    pieces = tok // LANES
    upper = 96
    low = (tok - upper) // 2
    cuts = [(0, upper), (upper, upper + low), (upper + low, tok)]
    members = mem * n_pop
    p = lax.axis_index("pop")
    q = lax.axis_index("mp")
    y = q // 2
    c = q % 2
    mate = flip(q, 1)
    across = flip(q, 2)
    diagonal = flip(q, 3)
    blocks = (diagonal, across, mate, q)
    other = 2 - 2 * y

    def remote(src, dst, ss, rs, pop, mp):
        return pltpu.make_async_remote_copy(
            src_ref=src, dst_ref=dst, send_sem=ss, recv_sem=rs,
            device_id=(pop, mp), device_id_type=pl.DeviceIdType.MESH,
        )

    def signal(sem, pop, mp):
        pl.semaphore_signal(sem, inc=1, device_id=(pop, mp), device_id_type=pl.DeviceIdType.MESH)

    def wait_for(ref, sem):
        pltpu.make_async_copy(ref, ref, sem).wait()

    def w_copy(s, k, sem):
        start = pl.multiple_of(blocks[s] * width + k * BLK, BLK)
        return pltpu.make_async_copy(w_h.at[:, pl.ds(start, BLK)], w_v.at[s, k], sem)

    def w_first(n):
        start = pl.multiple_of((other + n) * width, BLK)
        slot = 1 - c if n == 0 else c
        return pltpu.make_async_copy(w_h.at[:, pl.ds(start, BLK)], w_v.at[slot, 0], top_sem.at[n])

    def near_copy(k):
        return w_copy(3, k, loc_sem.at[2])

    def w_step(k, more):
        steps = [(1, k), (2, k)] if isinstance(k, jax.Array) or k > 0 else [(2, k)]
        if more:
            steps.append((0, k + 1))
        return [w_copy(s, i, w_sem.at[k % 2]) for s, i in steps]

    my_cols = pl.ds(pl.multiple_of(q * width, BLK), width)
    my_rows = pl.ds(pl.multiple_of(p * rows, LANES), rows)
    locals_ = [
        pltpu.make_async_copy(ctx_h.at[0:upper], ctx.at[0:upper], loc_sem.at[0]),
        pltpu.make_async_copy(ctx_h.at[upper:tok], ctx.at[upper:tok], loc_sem.at[1]),
        pltpu.make_async_copy(res_h, res, loc_sem.at[2]),
        pltpu.make_async_copy(tgt_h, tgt, loc_sem.at[2]),
        pltpu.make_async_copy(left_h.at[:, my_cols], lcols, loc_sem.at[2]),
        pltpu.make_async_copy(left_h.at[:, my_rows], lall.at[0], loc_sem.at[2]),
        pltpu.make_async_copy(right_h.at[:, my_cols], rall.at[0], loc_sem.at[2]),
        pltpu.make_async_copy(gain_h, gain, loc_sem.at[2]),
        pltpu.make_async_copy(right_h, right, loc_sem.at[2]),
        pltpu.make_async_copy(ranks_h, ranks, loc_sem.at[2]),
    ]
    locals_[0].start()
    w_first(0).start()

    barrier = pltpu.get_barrier_semaphore()
    for peer in (mate, across, diagonal):
        signal(barrier, p, peer)
    locals_[1].start()
    for bit in (1, 2, 4):
        signal(barrier, flip(p, bit), q)

    copy_top = remote(first_v, direct.at[c], sent, r_top, p, other)

    def copy_a(k):
        cols = pl.ds(2 * k, 2)
        return remote(send.at[0, cols], recv.at[0, cols], sent, r_a.at[pieces + k - 1], p, mate)

    tail = slice(0, LANES)

    def strip(i):
        return slice(*cuts[i])

    def copy_a0(i):
        return remote(send.at[0, 0:2, strip(i)], recv.at[0, 0:2, strip(i)], sent, r_a.at[i], p, mate)

    def copy_y0(i):
        return remote(send.at[1, 0:2, strip(i)], recv.at[1, 0:2, strip(i)], sent, r_y.at[i], p, across)

    def copy_y(k, count=2):
        cols = pl.ds(2 * k, count)
        return remote(send.at[1, cols], recv.at[1, cols], sent, r_y.at[pieces + k - 1], p, across)

    def copy_end(i):
        part = slice(i * LANES, (i + 1) * LANES)
        return remote(send.at[1, last, part], recv.at[1, last, part], sent, r_y.at[pieces + chunks - 1 + i], p, across)

    copy_swap = remote(send.at[1, last, tail], swap_in, sent, r_swap, p, mate)
    copy_swapped = remote(swap, recv.at[1, last, tail], sent, r_y.at[pieces + chunks - 1], p, diagonal)

    def copy_b(k):
        cols = pl.ds(2 * k, 2)
        return remote(send.at[2, cols], recv.at[2, cols], sent, r_b, p, mate)

    def copy_l(d):
        peer = flip(p, d)
        cols = pl.ds(pl.multiple_of(peer * rows, LANES), rows)
        return remote(left_h.at[:, cols], lall.at[d], sent, r_l, peer, q)

    def copy_r(d):
        return remote(right_h.at[:, my_cols], rall.at[d], sent, r_r, flip(p, d), q)

    def copy_u(d):
        return remote(ranked.at[0], ranked.at[d], sent, r_u, flip(p, d), q)

    def copy_f(d, core):
        return remote(marks.at[0], marks.at[d], sent, r_f, flip(p, d), 2 * y + core)

    copy_lin = remote(lin, lin_in, sent, r_lin, p, mate)
    copy_far = remote(lin_out, lin_far, sent, r_far, p, across)

    def copy_post(i, d):
        return remote(post.at[i], post_in.at[d - 1, i], sent, r_post, p, flip(q, d))

    def split_store(which, k, value):
        send[which, 2 * k] = value[:, :LANES]
        send[which, 2 * k + 1] = value[:, LANES:]

    def product(s, k):
        return jnp.dot(ctx[...], w_v[s, k], preferred_element_type=F32)

    everything = slice(0, tok)
    order = [*range(1, pieces), 0]
    with jax.named_scope("load0"):
        locals_[0].wait()
        w_first(0).wait()
    w_first(1).start()
    top = jnp.dot(ctx[0:upper, :], w_v[1 - c, 0], preferred_element_type=F32).astype(BF)
    first_v[0] = top[:, :LANES]
    first_v[1] = top[:, LANES:]
    def strip_product(s, i):
        return jnp.dot(ctx[strip(i), :], w_v[s, 0], preferred_element_type=F32)

    def prepare(i):
        value = strip_product(0, i).astype(BF)
        send[0, 0, strip(i)] = value[:, :LANES]
        send[0, 1, strip(i)] = value[:, LANES:]

    def give(i):
        prepare(i)
        copy_a0(i).start()

    @pl.when((c == 1) & (y == 0))
    def _():
        locals_[1].wait()
        prepare(1)

    with jax.named_scope("barrier"):
        pl.semaphore_wait(barrier, 6)
    copy_top.start()
    signal(rounds.at[0], flip(p, 1), q)
    for item in w_step(0, True):
        item.start()

    @pl.when((c == 0) | (y == 1))
    def _():
        locals_[1].wait()

    def pass_on(i, value):
        send[1, 0, strip(i)] = (value[:, :LANES] + recv[0, 0, strip(i)].astype(F32)).astype(BF)
        send[1, 1, strip(i)] = (value[:, LANES:] + recv[0, 1, strip(i)].astype(F32)).astype(BF)
        copy_y0(i).start()

    @pl.when(c == 0)
    def _():
        mine = [strip_product(1, i) for i in (1, 2)]
        copy_a0(1).wait_recv()
        pass_on(1, mine[0])
        w_first(1).wait()
        give(1)
        copy_a0(2).wait_recv()
        pass_on(2, mine[1])
        give(2)
        give(0)
        send[1, 0, strip(0)] = first_v[0]
        send[1, 1, strip(0)] = first_v[1]

    @pl.when((c == 1) & (y == 1))
    def _():
        prepare(1)

    @pl.when(c == 1)
    def _():
        copy_a0(1).start()
        give(2)
        send[0, 0, strip(0)] = first_v[0]
        send[0, 1, strip(0)] = first_v[1]
        w_first(1).wait()

    for item in w_step(1, True):
        item.start()
    near_copy(0).start()
    for item in w_step(0, True):
        item.wait()
    split_store(0, 1, product(0, 1).astype(BF))
    copy_a(1).start()
    for item in w_step(2, True):
        item.start()

    @pl.when(c == 1)
    def _():
        mine = [strip_product(1, i) for i in (1, 2, 0)]
        with jax.named_scope("wait_a0"):
            for i in (1, 2, 0):
                copy_a0(i).wait_recv()
                pass_on(i, mine[i - 1])


    def far(k, carry):
        for item in w_step(k, False):
            item.wait()

        @pl.when(k + 1 < chunks)
        def _():
            w_copy(0, k + 1, w_sem.at[k % 2]).wait()

        mine = product(1, k)
        with jax.named_scope("wait_a"):
            copy_a(k).wait_recv()
        send[1, 2 * k] = (mine[:, :LANES] + recv[0, 2 * k].astype(F32)).astype(BF)
        send[1, 2 * k + 1] = (mine[:, LANES:] + recv[0, 2 * k + 1].astype(F32)).astype(BF)

        @pl.when(k + 1 < chunks)
        def _():
            copy_y(k).start()

        @pl.when((k + 1 == chunks) & (c == 0))
        def _():
            send[1, last, tail] = mine[0:LANES, LANES:].astype(BF)
            copy_swap.start()

        @pl.when(k + 2 < chunks)
        def _():
            for item in w_step(k + 2, False):
                item.start()

        @pl.when(k + 3 < chunks)
        def _():
            w_copy(0, k + 3, w_sem.at[k % 2]).start()

        near_copy(k).start()

        @pl.when(k == 1)
        def _():
            for item in locals_[2:]:
                item.start()
            pl.semaphore_wait(rounds.at[0], 1)
            signal(rounds.at[1], flip(p, 2), q)

        @pl.when(k == 2)
        def _():
            pl.semaphore_wait(rounds.at[1], 1)
            signal(rounds.at[2], flip(p, 4), q)

        @pl.when(k == 3)
        def _():
            pl.semaphore_wait(rounds.at[2], 1)
            for d in range(1, n_pop):
                copy_r(n_pop - d).start()
                copy_l(n_pop - d).start()

        @pl.when(k + 1 < chunks)
        def _():
            split_store(0, k + 1, product(0, k + 1).astype(BF))
            copy_a(k + 1).start()

        @pl.when(k == 1)
        def _():
            split_store(2, 0, product(2, 0).astype(BF))
            copy_b(0).start()

        split_store(2, k, product(2, k).astype(BF))
        copy_b(k).start()
        return carry

    with jax.named_scope("far"):
        lax.fori_loop(1, chunks, far, 0)

    for item in locals_[2:]:
        item.wait()
    wait_for(w_v.at[3], loc_sem.at[2])

    lane = lax.broadcasted_iota(jnp.int32, (1, LANES), 1)
    ceiling = math.log(members / 2 + 1)
    whole = sum(max(0.0, ceiling - math.log(i + 1.0)) for i in range(members))
    shaped = jnp.maximum(0.0, ceiling - jnp.log(ranks[...].astype(F32) + 1.0)) / whole - 1.0 / members
    ranked[0] = jnp.where(lane // mem == p, jnp.concatenate([shaped] * n_pop, axis=1), 0.0)
    for d in range(1, n_pop):
        copy_u(d).start()

    def near(k, carry):
        cols = pl.ds(pl.multiple_of(k * BLK, BLK), BLK)
        base[:, cols] = product(3, k) + res[:, cols].astype(F32)
        return carry

    with jax.named_scope("near"):
        lax.fori_loop(0, chunks, near, 0)

    @pl.when(c == 1)
    def _():
        copy_swap.wait_recv()
        swap[...] = (send[0, last, tail].astype(F32) + swap_in[...].astype(F32)).astype(BF)
        copy_swapped.start()

    copy_y(chunks - 1, 1).start()

    def spread(slot, value):
        lin[slot * mem:(slot + 1) * mem, :] = value

    with jax.named_scope("early"):
        r_mine = rall[0].astype(F32)
        gr_hi, gr_lo = split_two(r_mine * gain[:, my_cols])
        spread(0, nt_dot(lcols[...], ctx[...]))
        spread(1, nt_dot(gr_hi, tgt[...]) + nt_dot(gr_lo, tgt[...]))
        r_full = right[...].astype(F32)
        gr_full = r_full * gain[...]
        norm_r = jnp.sum(r_full * r_full, axis=1, keepdims=True)
        norm_gr = jnp.sum(gr_full * gr_full, axis=1, keepdims=True)
        for acc in (sq_s, sq_a, sq_e, sq_t):
            acc[...] = jnp.zeros_like(acc)

    def mixed(block, start, size):
        cols = pl.ds(pl.multiple_of(block * width + start, LANES), size)
        r = right[:, cols]
        g = gain[:, cols]
        hi, low = split_two(r.astype(F32) * (g * g))
        return jnp.concatenate([r, hi, low], axis=0)

    def linear(k, carry):
        crossed, crossed_g = carry
        near_rows = mixed(q, k * BLK, BLK)
        far_rows = mixed(across, k * BLK, BLK)
        for h in range(2):
            cols = pl.ds(pl.multiple_of(k * BLK + h * LANES, LANES), LANES)
            part = slice(h * LANES, (h + 1) * LANES)
            u = 2 * k + h
            s = base[:, cols] + recv[2, u].astype(F32)
            base[:, cols] = s
            hi, low = split_two(s)
            both = nt_dot(near_rows[:, part], hi) + nt_dot(near_rows[:, part], low) + nt_dot(far_rows[:, part], send[1, u])
            crossed = crossed + both[0:mem]
            crossed_g = crossed_g + both[mem:2 * mem] + both[2 * mem:3 * mem]
            wide = tgt[:, cols].astype(F32)
            sq_t[...] += wide * wide
        return crossed, crossed_g

    with jax.named_scope("wait_b"):
        wait_for(recv.at[2], r_b)
    with jax.named_scope("linear"):
        top_rows = mixed(other, 0, BLK)
        top = nt_dot(top_rows[:, :LANES], first_v[0]) + nt_dot(top_rows[:, LANES:], first_v[1])
        late = nt_dot(mixed(other, last * LANES, LANES), send[0, last, tail])
        top = sum(jnp.concatenate([v, jnp.zeros((3 * mem, tok - v.shape[1]), F32)], axis=1) for v in (top, late))
        top = top * jnp.where(c == 1, 1.0, 0.0)
        carry = (top[0:mem], top[mem:2 * mem] + top[2 * mem:3 * mem])
        crossed, crossed_g = lax.fori_loop(0, chunks, linear, carry)
        spread(2, crossed)
        spread(3, crossed_g)

    @pl.when(c == 0)
    def _():
        copy_lin.start()
        for i in order[:-1]:
            copy_end(i).start()

    def arrived(u, part):
        cols = pl.ds(pl.multiple_of(u * LANES, LANES), LANES)
        gain_u = gain[:, pl.ds(pl.multiple_of(q * width + u * LANES, LANES), LANES)]
        s = base[part, cols] + recv[1, u, part].astype(F32)
        base[part, cols] = s
        gs = s * gain_u
        return s * s, gs * gs, gs * tgt[part, cols].astype(F32)

    def settle(u, carry):
        for acc, item in zip((sq_s, sq_a, sq_e), arrived(u, everything)):
            acc[...] += item
        return carry

    with jax.named_scope("wait_y0"):
        for i in range(1, pieces):
            copy_y0(i).wait_recv()

        @pl.when(c == 0)
        def _():
            wait_for(direct, r_top)
            for u in range(2):
                recv[1, u, strip(0)] = jnp.zeros((upper, LANES), BF)
                base[0:upper, u * LANES:(u + 1) * LANES] += direct[0, u].astype(F32) + direct[1, u].astype(F32)

        @pl.when(c == 1)
        def _():
            copy_y0(0).wait_recv()

    lax.fori_loop(0, 2, settle, 0)

    @pl.when(c == 1)
    def _():
        for i in order:
            copy_end(i).start()
        with jax.named_scope("wait_lin"):
            copy_lin.wait_recv()
        lin_out[...] = lin[...] + lin_in[...]
        copy_far.start()

    def settle_chunk(k, carry):
        with jax.named_scope("wait_y"):
            copy_y(k).wait_recv()
        settle(2 * k, 0)
        settle(2 * k + 1, 0)
        return carry

    with jax.named_scope("settle"):
        lax.fori_loop(1, chunks - 1, settle_chunk, 0)
    half_of = slice(1, n_pop)
    with jax.named_scope("wait_lr"):
        wait_for(lall.at[half_of], r_l)
        wait_for(rall.at[half_of], r_r)
        wait_for(ranked.at[half_of], r_u)
    with jax.named_scope("turn"):
        for d in range(n_pop):
            place = pl.ds(pl.multiple_of(flip(p, d) * mem, mem), mem)
            right_all[place, :] = rall[d]
            left_v[place, :] = lall[d].astype(F32)
        left_t[...] = left_v[...].T
    with jax.named_scope("wait_y8"):
        copy_y(chunks - 1, 1).wait_recv()
    settle(last - 1, 0)
    before = nt_dot(row_picker(4), halves((sq_s[...], sq_a[...], sq_e[...], sq_t[...])))
    picker = row_picker(3)
    for i in order:
        part = slice(i * LANES, (i + 1) * LANES)
        with jax.named_scope("wait_end"):
            copy_end(i).wait_recv()
        with jax.named_scope("end"):
            post[i] = (before[:, part] + nt_dot(picker, halves(arrived(last, part))))[0:4]

            @pl.when(c == 0)
            def _():
                copy_post(i, 3).start()
                copy_post(i, 1).start()

            @pl.when(c == 1)
            def _():
                copy_post(i, 2).start()

    others = marks.at[half_of]

    @pl.when(c == 1)
    def _():
        with jax.named_scope("wait_far"):
            copy_far.wait_recv()
        own = lin_out[...] + lin_far[...]
        lifted = own[0:mem] * (SIGMA / math.sqrt(full))
        lifted2 = lifted * lifted
        extra_s = 2.0 * lifted * own[2 * mem:3 * mem] + lifted2 * norm_r
        extra_a = 2.0 * lifted * own[3 * mem:4 * mem] + lifted2 * norm_gr
        extra_e = lifted * own[mem:2 * mem]
        with jax.named_scope("wait_post"):
            wait_for(post_in, r_post)
        with jax.named_scope("errors"):
            late = jnp.concatenate([post[i] + post_in[0, i] + post_in[1, i] + post_in[2, i] for i in range(pieces)], axis=1)
            meansq = (late[0:1] + extra_s) / full
            inverse = lax.rsqrt(meansq + EPSILON)
            errors = inverse * inverse * (late[1:2] + extra_a) - 2.0 * inverse * (late[2:3] + extra_e) + late[3:4]
            summed = jnp.sum(errors, axis=1, keepdims=True)
            spot = lax.broadcasted_iota(jnp.int32, (mem, LANES), 0) + p * mem
            here = lax.broadcasted_iota(jnp.int32, (mem, LANES), 1) == spot
            marks[0] = jnp.sum(jnp.where(here, summed, 0.0), axis=0, keepdims=True)
            for d in range(n_pop - 1, -1, -1):
                copy_f(d, 0).start()
                if d > 0:
                    copy_f(d, 1).start()

    @pl.when(c == 0)
    def _():
        with jax.named_scope("wait_f"):
            wait_for(marks, r_f)

    @pl.when(c == 1)
    def _():
        with jax.named_scope("wait_f"):
            wait_for(others, r_f)

    fits[0:1] = sum((marks[d] for d in range(1, n_pop)), marks[0])
    fits[1:2] = sum((ranked[d] for d in range(1, n_pop)), ranked[0])
    for which in range(2):
        wait_for(send.at[which, 2:units], sent)
    wait_for(send.at[2], sent)
    wait_for(first_v, sent)
    wait_for(lall.at[half_of], sent)
    wait_for(rall.at[half_of], sent)
    wait_for(ranked.at[half_of], sent)
    for core in range(2):
        @pl.when(c == core)
        def _(core=core):
            for i in range(core, pieces):
                copy_a0(i).wait_send()
            for i in range(1 - core, pieces):
                copy_y0(i).wait_send()
            if core == 1:
                copy_swapped.wait_send()
            if core == 0:
                copy_lin.wait_send()
                wait_for(post_in.at[0:2], sent)
            else:
                copy_far.wait_send()
                wait_for(post_in.at[0], sent)
                wait_for(marks, sent)
                wait_for(others, sent)


def in_hbm(x):
    return pltpu.with_memory_space_constraint(x, pltpu.HBM)


def fused_shards(
    n_pop, n_mp, context, out_weight, residual, target, norm_gain, left_factors, right_factors, member_ranks
):
    tok, width = context.shape
    full = out_weight.shape[1]
    mem = left_factors.shape[0]
    rows = full // n_pop
    chunks = width // BLK
    units = width // LANES
    pieces = tok // LANES
    ranks = member_ranks.reshape(1, mem)
    anywhere = pl.BlockSpec(memory_space=pltpu.HBM)
    vmem = pl.BlockSpec(memory_space=pltpu.VMEM)
    dma = pltpu.SemaphoreType.DMA
    acc = pltpu.VMEM((tok, LANES), F32)
    group = pltpu.VMEM((4 * mem, tok), F32)
    base, left_t, right_all, fits = pl.pallas_call(
        functools.partial(kernel, n_pop, n_mp),
        name="es_step",
        out_shape=(
            jax.ShapeDtypeStruct((tok, width), F32),
            jax.ShapeDtypeStruct((rows, n_pop * mem), F32),
            jax.ShapeDtypeStruct((n_pop * mem, width), BF),
            jax.ShapeDtypeStruct((2, n_pop * mem), F32),
        ),
        in_specs=[anywhere] * 8,
        out_specs=[vmem] * 4,
        scratch_shapes=[
            pltpu.VMEM((4, chunks, width, BLK), BF),
            pltpu.VMEM((tok, width), BF),
            pltpu.VMEM((tok, width), BF),
            pltpu.VMEM((tok, width), BF),
            pltpu.VMEM((mem, width), BF),
            pltpu.VMEM((1, full), F32),
            pltpu.VMEM((mem, full), BF),
            pltpu.VMEM((1, mem), jnp.int32),
            pltpu.VMEM((3, units, tok, LANES), BF),
            pltpu.VMEM((3, units, tok, LANES), BF),
            pltpu.VMEM((2, 96, LANES), BF),
            pltpu.VMEM((2, 2, 96, LANES), BF),
            pltpu.VMEM((n_pop, mem, rows), BF),
            pltpu.VMEM((n_pop, mem, width), BF),
            acc, acc, acc, acc,
            group, group, group, group,
            pltpu.VMEM((pieces, 4, LANES), F32),
            pltpu.VMEM((n_mp - 1, pieces, 4, LANES), F32),
            pltpu.VMEM((LANES, LANES), BF),
            pltpu.VMEM((LANES, LANES), BF),
            pltpu.VMEM((n_pop, 1, LANES), F32),
            pltpu.VMEM((n_pop * mem, rows), F32),
            pltpu.VMEM((n_pop, 1, LANES), F32),
            dma((2,)),
            dma((2,)),
            dma((3,)),
            dma,
            dma((chunks - 1 + pieces,)),
            dma((chunks - 1 + 2 * pieces,)),
        ]
        + [dma] * 10
        + [pltpu.SemaphoreType.REGULAR((3,))],
        compiler_params=pltpu.CompilerParams(
            collective_id=0,
            has_side_effects=True,
            vmem_limit_bytes=48 * 1024 * 1024,
        ),
    )(
        *map(in_hbm, (
            context, out_weight, residual, target, norm_gain.reshape(1, full), left_factors,
            right_factors, ranks,
        ))
    )
    count_all = n_pop * mem
    update, base, fitness = pl.pallas_call(
        functools.partial(finish, n_pop, math.sqrt(count_all) / SIGMA, tok * full),
        name="es_update",
        out_shape=(
            jax.ShapeDtypeStruct((rows, width), F32),
            jax.ShapeDtypeStruct((tok, width), F32),
            jax.ShapeDtypeStruct((1, mem), F32),
        ),
        in_specs=[vmem] * 4,
        out_specs=[anywhere] * 3,
        scratch_shapes=[
            pltpu.VMEM((rows, width), F32),
            pltpu.VMEM((1, mem), F32),
            dma,
        ],
        compiler_params=pltpu.CompilerParams(vmem_limit_bytes=16 * 1024 * 1024),
    )(left_t, right_all, base, fits)
    return (update, fitness.reshape(mem), base)


def finish(n_pop, scale, count, left_t, right_all, base_in, fits, update, base, fit, held, fit_v, sem):
    steps = held.shape[0] // 128
    mem = fit_v.shape[1]
    members = n_pop * mem
    copies = [
        pltpu.make_async_copy(base_in, base, sem),
        pltpu.make_async_copy(fit_v, fit, sem),
    ]
    copies[0].start()
    all_fit = fits[0:1] * (-1.0 / count)
    centre = all_fit - jnp.sum(all_fit, axis=1, keepdims=True) / members
    deviation = jnp.sqrt(jnp.sum(centre * centre, axis=1, keepdims=True) / members + 1e-05)
    weight = fits[1:2] + centre / deviation / members
    for i in range(steps):
        part = slice(i * 128, (i + 1) * 128)
        weighted = (left_t[part, :] * weight).astype(BF)
        held[part, :] = jnp.dot(weighted, right_all[...], preferred_element_type=F32) * scale
        copies.append(pltpu.make_async_copy(held.at[part], update.at[part], sem))
        copies[-1].start()
    p = lax.axis_index("pop")
    mine = jnp.zeros((1, mem), F32)
    for d in range(n_pop):
        mine = mine + jnp.where(p == d, 1.0, 0.0) * all_fit[:, d * mem:(d + 1) * mem]
    fit_v[...] = mine
    copies[1].start()
    for item in copies:
        item.wait()


def chosen(n_pop, n_mp, context, out_weight, *rest):
    tok, width = context.shape
    mem = rest[3].shape[0]
    full = out_weight.shape[1]
    chunks = width // BLK
    if n_mp == 4 and n_pop == 8 and width % BLK == 0 and chunks > 3 and (full // n_pop) % 128 == 0 and tok % 128 == 0 and mem == 16:
        return fused_shards(n_pop, n_mp, context, out_weight, *rest)
    return shards(context, out_weight, *rest)


def solution(mesh):
    in_specs = (
        P("pop", "mp"),
        P("mp", None),
        P("pop", "mp"),
        P("pop", "mp"),
        P(),
        P("pop", None),
        P("pop", None),
        P("pop"),
    )
    out_specs = (P("pop", "mp"), P("pop"), P("pop", "mp"))
    return jax.shard_map(
        functools.partial(chosen, mesh.shape["pop"], mesh.shape["mp"]), mesh=mesh, in_specs=in_specs, out_specs=out_specs, check_vma=False)
```

```python
import functools
import math

import jax
import jax.numpy as jnp
from jax import lax
from jax.experimental import pallas as pl
from jax.experimental.pallas import tpu as pltpu
from jax.sharding import PartitionSpec as P

SIGMA = 1.0
EPSILON = 1e-06


def error_sums(stream, lifted, right_rows, gain_part, target_rows, inverse):
    hidden = stream[:, None, :] + lifted[:, :, None] * right_rows[None, :, :]
    differ = gain_part * hidden * inverse[:, :, None] - target_rows[:, None, :]
    return jnp.sum(differ * differ, axis=(0, 2))


def utility(member_ranks, count_all):
    levels = jnp.arange(count_all).astype(jnp.float32)
    ceiling = math.log(count_all / 2 + 1)
    baseline = jnp.maximum(0.0, ceiling - jnp.log(levels + 1.0))
    shaped = jnp.maximum(0.0, ceiling - jnp.log(member_ranks.astype(jnp.float32) + 1.0))
    return shaped / jnp.sum(baseline) - 1.0 / count_all


def shards(
    context, out_weight, residual, target, norm_gain, left_factors, right_factors, member_ranks
):
    tok_count = context.shape[0]
    shard_width = context.shape[1]
    full_width = out_weight.shape[1]
    factor = SIGMA / math.sqrt(full_width)
    offset = lax.axis_index("mp") * shard_width
    left_cols = lax.dynamic_slice_in_dim(left_factors, offset, shard_width, 1)
    right_cols = lax.dynamic_slice_in_dim(right_factors, offset, shard_width, 1)
    partial_value = jnp.dot(context, out_weight, preferred_element_type=jnp.float32)
    projected = lax.dot_general(
        context, left_cols, (((1,), (1,)), ((), ())), preferred_element_type=jnp.float32
    )
    summed = lax.psum_scatter(
        partial_value.astype(jnp.bfloat16), "mp", scatter_dimension=1, tiled=True
    ).astype(jnp.float32)
    stream = residual.astype(jnp.float32) + summed
    gain_part = lax.dynamic_slice_in_dim(norm_gain, offset, shard_width, 0)
    factor_f = right_cols.astype(jnp.float32)
    crossed = jnp.dot(stream, factor_f.T, precision=lax.Precision.HIGHEST)
    per_token = jnp.sum(stream * stream, axis=1)
    per_member = jnp.sum(factor_f * factor_f, axis=1)
    projected, crossed, per_token, per_member = lax.psum(
        (projected, crossed, per_token, per_member), "mp"
    )
    lifted = factor * projected
    meansq = (
        per_token[:, None] + 2.0 * lifted * crossed + lifted * lifted * per_member[None, :]
    ) / full_width
    inverse = lax.rsqrt(meansq + EPSILON)
    local_error = error_sums(
        stream, lifted, factor_f, gain_part, target.astype(jnp.float32), inverse
    )
    member_total = lax.psum(local_error, "mp")
    fitness = -member_total / (tok_count * full_width)
    everyone = lax.all_gather(fitness, "pop", axis=0, tiled=True)
    count_all = everyone.shape[0]
    average = jnp.mean(everyone)
    centre = everyone - average
    spread = jnp.sqrt(jnp.mean(centre * centre) + 1e-05)
    weight = utility(member_ranks, count_all) + (fitness - average) / spread / count_all
    weighted = (weight[:, None] * left_factors.astype(jnp.float32)).astype(jnp.bfloat16)
    weighted_rows = lax.all_to_all(weighted, "pop", split_axis=1, concat_axis=0, tiled=True)
    right_all = lax.all_gather(right_cols, "pop", axis=0, tiled=True)
    update = lax.dot_general(
        weighted_rows, right_all, (((0,), (0,)), ((), ())), preferred_element_type=jnp.float32
    ) * (math.sqrt(count_all) / SIGMA)
    return (update, fitness, stream)


BLK = 256
LANES = 128
F32 = jnp.float32
BF = jnp.bfloat16


def nt_dot(a, b):
    return lax.dot_general(a, b, (((1,), (1,)), ((), ())), preferred_element_type=F32)


def split_two(x):
    hi = x.astype(BF)
    return hi, (x - hi.astype(F32)).astype(BF)


def halves(parts):
    return jnp.concatenate([piece for part in parts for piece in split_two(part)], axis=1)


def row_picker(count):
    shape = (8, count * 2 * LANES)
    owner = lax.broadcasted_iota(jnp.int32, shape, 1) // (2 * LANES)
    return jnp.where(owner == lax.broadcasted_iota(jnp.int32, shape, 0), 1.0, 0.0).astype(BF)


def flip(index, bits):
    for bit in (1, 2, 4):
        if bits & bit:
            index = index + bit - 2 * bit * ((index // bit) % 2)
    return index


def kernel(
    n_pop, n_mp, ctx_h, w_h, res_h, tgt_h, gain_h, left_h, right_h, ranks_h,
    base, left_t, right_all, fits,
    w_v, ctx, res, tgt, lcols, gain, right, ranks, send, recv, first_v, direct, lall, rall,
    sq_s, sq_a, sq_e, sq_t, lin, lin_in, lin_out, lin_far, post, post_in, swap, swap_in, detour_a, detour_b, marks, left_v, ranked,
    w_sem, top_sem, loc_sem, sent, r_a, r_y, r_b, r_top, r_lin, r_far, r_post, r_swap, r_d, r_l, r_r, r_u, r_f, rounds,
):
    tok, width = ctx.shape
    mem = right.shape[0]
    full = right.shape[1]
    rows = full // n_pop
    chunks = width // BLK
    units = width // LANES
    last = units - 1
    pieces = tok // LANES
    upper = 96
    low = (tok - upper) // 2
    cuts = [(0, upper), (upper, upper + low), (upper + low, tok)]
    members = mem * n_pop
    p = lax.axis_index("pop")
    q = lax.axis_index("mp")
    y = q // 2
    c = q % 2
    outer = (c == 1) & (p % 2 == 1)
    inner = (c == 1) & (p % 2 == 0)
    mate = flip(q, 1)
    across = flip(q, 2)
    diagonal = flip(q, 3)
    blocks = (diagonal, across, mate, q)
    other = 2 - 2 * y

    def remote(src, dst, ss, rs, pop, mp):
        return pltpu.make_async_remote_copy(
            src_ref=src, dst_ref=dst, send_sem=ss, recv_sem=rs,
            device_id=(pop, mp), device_id_type=pl.DeviceIdType.MESH,
        )

    def signal(sem, pop, mp):
        pl.semaphore_signal(sem, inc=1, device_id=(pop, mp), device_id_type=pl.DeviceIdType.MESH)

    def wait_for(ref, sem):
        pltpu.make_async_copy(ref, ref, sem).wait()

    def w_copy(s, k, sem):
        start = pl.multiple_of(blocks[s] * width + k * BLK, BLK)
        return pltpu.make_async_copy(w_h.at[:, pl.ds(start, BLK)], w_v.at[s, k], sem)

    def w_first(n):
        start = pl.multiple_of((other + n) * width, BLK)
        slot = 1 - c if n == 0 else c
        return pltpu.make_async_copy(w_h.at[:, pl.ds(start, BLK)], w_v.at[slot, 0], top_sem.at[n])

    def near_copy(k):
        return w_copy(3, k, loc_sem.at[2])

    def w_step(k, more):
        steps = [(1, k), (2, k)] if isinstance(k, jax.Array) or k > 0 else [(2, k)]
        if more:
            steps.append((0, k + 1))
        return [w_copy(s, i, w_sem.at[k % 2]) for s, i in steps]

    my_cols = pl.ds(pl.multiple_of(q * width, BLK), width)
    my_rows = pl.ds(pl.multiple_of(p * rows, LANES), rows)
    locals_ = [
        pltpu.make_async_copy(ctx_h.at[0:upper], ctx.at[0:upper], loc_sem.at[0]),
        pltpu.make_async_copy(ctx_h.at[upper:tok], ctx.at[upper:tok], loc_sem.at[1]),
        pltpu.make_async_copy(res_h, res, loc_sem.at[2]),
        pltpu.make_async_copy(tgt_h, tgt, loc_sem.at[2]),
        pltpu.make_async_copy(left_h.at[:, my_cols], lcols, loc_sem.at[2]),
        pltpu.make_async_copy(left_h.at[:, my_rows], lall.at[0], loc_sem.at[2]),
        pltpu.make_async_copy(right_h.at[:, my_cols], rall.at[0], loc_sem.at[2]),
        pltpu.make_async_copy(gain_h, gain, loc_sem.at[2]),
        pltpu.make_async_copy(right_h, right, loc_sem.at[2]),
        pltpu.make_async_copy(ranks_h, ranks, loc_sem.at[2]),
    ]
    locals_[0].start()
    w_first(0).start()

    barrier = pltpu.get_barrier_semaphore()
    for peer in (mate, across, diagonal):
        signal(barrier, p, peer)
    locals_[1].start()
    for bit in (1, 2, 4):
        signal(barrier, flip(p, bit), q)

    copy_top = remote(first_v, direct.at[c], sent, r_top, p, other)

    def copy_a(k):
        cols = pl.ds(2 * k, 2)
        return remote(send.at[0, cols], recv.at[0, cols], sent, r_a.at[pieces + k - 1], p, mate)

    tail = slice(0, LANES)

    def strip(i):
        return slice(*cuts[i])

    def copy_a0(i):
        return remote(send.at[0, 0:2, strip(i)], recv.at[0, 0:2, strip(i)], sent, r_a.at[i], p, mate)

    def copy_y0(i):
        return remote(send.at[1, 0:2, strip(i)], recv.at[1, 0:2, strip(i)], sent, r_y.at[i], p, across)

    def copy_y(k, count=2):
        cols = pl.ds(2 * k, count)
        return remote(send.at[1, cols], recv.at[1, cols], sent, r_y.at[pieces + k - 1], p, across)

    def copy_end(i):
        part = slice(i * LANES, (i + 1) * LANES)
        return remote(send.at[1, last, part], recv.at[1, last, part], sent, r_y.at[pieces + chunks - 1 + i], p, across)

    detour = detour_a.shape[0]
    turn_unit = 5
    away = slice(0, detour)
    rest = slice(detour, tok)
    copy_d1 = remote(send.at[1, turn_unit, away], detour_a, sent, r_d.at[0], flip(p, 1), q)
    copy_d2 = remote(detour_a, detour_b, sent, r_d.at[1], p, across)
    copy_d3 = remote(detour_b, recv.at[1, turn_unit, away], sent, r_d.at[0], flip(p, 1), q)
    copy_first = remote(send.at[1, turn_unit - 1], recv.at[1, turn_unit - 1], sent, r_y.at[pieces + 1], p, across)
    copy_rest = remote(send.at[1, turn_unit, rest], recv.at[1, turn_unit, rest], sent, r_d.at[1], p, across)

    copy_swap = remote(send.at[1, last, tail], swap_in, sent, r_swap, p, mate)
    copy_swapped = remote(swap, recv.at[1, last, tail], sent, r_y.at[pieces + chunks - 1], p, diagonal)

    def copy_b(k):
        cols = pl.ds(2 * k, 2)
        return remote(send.at[2, cols], recv.at[2, cols], sent, r_b, p, mate)

    def copy_l(d):
        peer = flip(p, d)
        cols = pl.ds(pl.multiple_of(peer * rows, LANES), rows)
        return remote(left_h.at[:, cols], lall.at[d], sent, r_l, peer, q)

    def copy_r(d):
        return remote(right_h.at[:, my_cols], rall.at[d], sent, r_r, flip(p, d), q)

    def copy_u(d):
        return remote(ranked.at[0], ranked.at[d], sent, r_u, flip(p, d), q)

    def copy_f(d, core):
        return remote(marks.at[0], marks.at[d], sent, r_f, flip(p, d), 2 * y + core)

    copy_lin = remote(lin, lin_in, sent, r_lin, p, mate)
    copy_far = remote(lin_out, lin_far, sent, r_far, p, across)

    def copy_post(i, d):
        return remote(post.at[i], post_in.at[d - 1, i], sent, r_post, p, flip(q, d))

    def split_store(which, k, value):
        send[which, 2 * k] = value[:, :LANES]
        send[which, 2 * k + 1] = value[:, LANES:]

    def product(s, k):
        return jnp.dot(ctx[...], w_v[s, k], preferred_element_type=F32)

    everything = slice(0, tok)
    order = [*range(1, pieces), 0]
    with jax.named_scope("load0"):
        locals_[0].wait()
        w_first(0).wait()
    w_first(1).start()
    top = jnp.dot(ctx[0:upper, :], w_v[1 - c, 0], preferred_element_type=F32).astype(BF)
    first_v[0] = top[:, :LANES]
    first_v[1] = top[:, LANES:]
    def strip_product(s, i):
        return jnp.dot(ctx[strip(i), :], w_v[s, 0], preferred_element_type=F32)

    def prepare(i):
        value = strip_product(0, i).astype(BF)
        send[0, 0, strip(i)] = value[:, :LANES]
        send[0, 1, strip(i)] = value[:, LANES:]

    def give(i):
        prepare(i)
        copy_a0(i).start()

    @pl.when((c == 1) & (y == 0))
    def _():
        locals_[1].wait()
        prepare(1)

    with jax.named_scope("barrier"):
        pl.semaphore_wait(barrier, 6)
    copy_top.start()
    signal(rounds.at[0], flip(p, 1), q)
    for item in w_step(0, True):
        item.start()

    @pl.when((c == 0) | (y == 1))
    def _():
        locals_[1].wait()

    def pass_on(i, value):
        send[1, 0, strip(i)] = (value[:, :LANES] + recv[0, 0, strip(i)].astype(F32)).astype(BF)
        send[1, 1, strip(i)] = (value[:, LANES:] + recv[0, 1, strip(i)].astype(F32)).astype(BF)
        copy_y0(i).start()

    @pl.when(c == 0)
    def _():
        mine = [strip_product(1, i) for i in (1, 2)]
        copy_a0(1).wait_recv()
        pass_on(1, mine[0])
        w_first(1).wait()
        give(1)
        copy_a0(2).wait_recv()
        pass_on(2, mine[1])
        give(2)
        give(0)
        send[1, 0, strip(0)] = first_v[0]
        send[1, 1, strip(0)] = first_v[1]

    @pl.when((c == 1) & (y == 1))
    def _():
        prepare(1)

    @pl.when(c == 1)
    def _():
        copy_a0(1).start()
        give(2)
        send[0, 0, strip(0)] = first_v[0]
        send[0, 1, strip(0)] = first_v[1]
        w_first(1).wait()

    for item in w_step(1, True):
        item.start()
    near_copy(0).start()
    for item in w_step(0, True):
        item.wait()
    split_store(0, 1, product(0, 1).astype(BF))
    copy_a(1).start()
    for item in w_step(2, True):
        item.start()

    @pl.when(c == 1)
    def _():
        mine = [strip_product(1, i) for i in (1, 2, 0)]
        with jax.named_scope("wait_a0"):
            for i in (1, 2, 0):
                copy_a0(i).wait_recv()
                pass_on(i, mine[i - 1])


    def far(k, carry):
        for item in w_step(k, False):
            item.wait()

        @pl.when(k + 1 < chunks)
        def _():
            w_copy(0, k + 1, w_sem.at[k % 2]).wait()

        mine = product(1, k)
        @pl.when((k == 3) & inner)
        def _():
            with jax.named_scope("wait_d1"):
                copy_d1.wait_recv()
            copy_d2.start()

        with jax.named_scope("wait_a"):
            copy_a(k).wait_recv()
        send[1, 2 * k] = (mine[:, :LANES] + recv[0, 2 * k].astype(F32)).astype(BF)
        send[1, 2 * k + 1] = (mine[:, LANES:] + recv[0, 2 * k + 1].astype(F32)).astype(BF)

        @pl.when((k + 1 < chunks) & ((k != 2) | jnp.logical_not(outer)))
        def _():
            copy_y(k).start()

        @pl.when((k == 2) & outer)
        def _():
            copy_d1.start()
            copy_first.start()
            copy_rest.start()

        @pl.when((k + 1 == chunks) & (c == 0))
        def _():
            send[1, last, tail] = mine[0:LANES, LANES:].astype(BF)
            copy_swap.start()

        @pl.when(k + 2 < chunks)
        def _():
            for item in w_step(k + 2, False):
                item.start()

        @pl.when(k + 3 < chunks)
        def _():
            w_copy(0, k + 3, w_sem.at[k % 2]).start()

        near_copy(k).start()

        @pl.when(k == 1)
        def _():
            for item in locals_[2:]:
                item.start()
            pl.semaphore_wait(rounds.at[0], 1)
            signal(rounds.at[1], flip(p, 2), q)

        @pl.when(k == 2)
        def _():
            pl.semaphore_wait(rounds.at[1], 1)
            signal(rounds.at[2], flip(p, 4), q)

        @pl.when(k == 3)
        def _():
            pl.semaphore_wait(rounds.at[2], 1)
            for d in range(1, n_pop):
                copy_r(n_pop - d).start()
                copy_l(n_pop - d).start()

        @pl.when(k + 1 < chunks)
        def _():
            split_store(0, k + 1, product(0, k + 1).astype(BF))
            copy_a(k + 1).start()

        @pl.when(k == 1)
        def _():
            split_store(2, 0, product(2, 0).astype(BF))
            copy_b(0).start()

        split_store(2, k, product(2, k).astype(BF))
        copy_b(k).start()
        return carry

    with jax.named_scope("far"):
        lax.fori_loop(1, chunks, far, 0)

    for item in locals_[2:]:
        item.wait()
    wait_for(w_v.at[3], loc_sem.at[2])

    lane = lax.broadcasted_iota(jnp.int32, (1, LANES), 1)
    ceiling = math.log(members / 2 + 1)
    whole = sum(max(0.0, ceiling - math.log(i + 1.0)) for i in range(members))
    shaped = jnp.maximum(0.0, ceiling - jnp.log(ranks[...].astype(F32) + 1.0)) / whole - 1.0 / members
    ranked[0] = jnp.where(lane // mem == p, jnp.concatenate([shaped] * n_pop, axis=1), 0.0)
    for d in range(1, n_pop):
        copy_u(d).start()

    def near(k, carry):
        cols = pl.ds(pl.multiple_of(k * BLK, BLK), BLK)
        base[:, cols] = product(3, k) + res[:, cols].astype(F32)
        return carry

    with jax.named_scope("near"):
        lax.fori_loop(0, chunks, near, 0)

    @pl.when(c == 1)
    def _():
        copy_swap.wait_recv()
        swap[...] = (send[0, last, tail].astype(F32) + swap_in[...].astype(F32)).astype(BF)
        copy_swapped.start()

    copy_y(chunks - 1, 1).start()

    def spread(slot, value):
        lin[slot * mem:(slot + 1) * mem, :] = value

    with jax.named_scope("early"):
        r_mine = rall[0].astype(F32)
        gr_hi, gr_lo = split_two(r_mine * gain[:, my_cols])
        spread(0, nt_dot(lcols[...], ctx[...]))
        spread(1, nt_dot(gr_hi, tgt[...]) + nt_dot(gr_lo, tgt[...]))
        r_full = right[...].astype(F32)
        gr_full = r_full * gain[...]
        norm_r = jnp.sum(r_full * r_full, axis=1, keepdims=True)
        norm_gr = jnp.sum(gr_full * gr_full, axis=1, keepdims=True)
        for acc in (sq_s, sq_a, sq_e, sq_t):
            acc[...] = jnp.zeros_like(acc)

    def mixed(block, start, size):
        cols = pl.ds(pl.multiple_of(block * width + start, LANES), size)
        r = right[:, cols]
        g = gain[:, cols]
        hi, low = split_two(r.astype(F32) * (g * g))
        return jnp.concatenate([r, hi, low], axis=0)

    def linear(k, carry):
        crossed, crossed_g = carry
        near_rows = mixed(q, k * BLK, BLK)
        far_rows = mixed(across, k * BLK, BLK)
        for h in range(2):
            cols = pl.ds(pl.multiple_of(k * BLK + h * LANES, LANES), LANES)
            part = slice(h * LANES, (h + 1) * LANES)
            u = 2 * k + h
            s = base[:, cols] + recv[2, u].astype(F32)
            base[:, cols] = s
            hi, low = split_two(s)
            both = nt_dot(near_rows[:, part], hi) + nt_dot(near_rows[:, part], low) + nt_dot(far_rows[:, part], send[1, u])
            crossed = crossed + both[0:mem]
            crossed_g = crossed_g + both[mem:2 * mem] + both[2 * mem:3 * mem]
            wide = tgt[:, cols].astype(F32)
            sq_t[...] += wide * wide
        return crossed, crossed_g

    with jax.named_scope("wait_b"):
        wait_for(recv.at[2], r_b)
    with jax.named_scope("linear"):
        top_rows = mixed(other, 0, BLK)
        top = nt_dot(top_rows[:, :LANES], first_v[0]) + nt_dot(top_rows[:, LANES:], first_v[1])
        late = nt_dot(mixed(other, last * LANES, LANES), send[0, last, tail])
        top = sum(jnp.concatenate([v, jnp.zeros((3 * mem, tok - v.shape[1]), F32)], axis=1) for v in (top, late))
        top = top * jnp.where(c == 1, 1.0, 0.0)
        carry = (top[0:mem], top[mem:2 * mem] + top[2 * mem:3 * mem])
        crossed, crossed_g = lax.fori_loop(0, chunks, linear, carry)
        spread(2, crossed)
        spread(3, crossed_g)

    @pl.when(c == 0)
    def _():
        copy_lin.start()
        for i in order[:-1]:
            copy_end(i).start()

    def arrived(u, part):
        cols = pl.ds(pl.multiple_of(u * LANES, LANES), LANES)
        gain_u = gain[:, pl.ds(pl.multiple_of(q * width + u * LANES, LANES), LANES)]
        s = base[part, cols] + recv[1, u, part].astype(F32)
        base[part, cols] = s
        gs = s * gain_u
        return s * s, gs * gs, gs * tgt[part, cols].astype(F32)

    def settle(u, carry):
        for acc, item in zip((sq_s, sq_a, sq_e), arrived(u, everything)):
            acc[...] += item
        return carry

    with jax.named_scope("wait_y0"):
        for i in range(1, pieces):
            copy_y0(i).wait_recv()

        @pl.when(c == 0)
        def _():
            wait_for(direct, r_top)
            for u in range(2):
                recv[1, u, strip(0)] = jnp.zeros((upper, LANES), BF)
                base[0:upper, u * LANES:(u + 1) * LANES] += direct[0, u].astype(F32) + direct[1, u].astype(F32)

        @pl.when(c == 1)
        def _():
            copy_y0(0).wait_recv()

    lax.fori_loop(0, 2, settle, 0)

    @pl.when(c == 1)
    def _():
        for i in order:
            copy_end(i).start()
        with jax.named_scope("wait_lin"):
            copy_lin.wait_recv()
        lin_out[...] = lin[...] + lin_in[...]
        copy_far.start()

    @pl.when(inner)
    def _():
        with jax.named_scope("wait_d2"):
            copy_d2.wait_recv()
        copy_d3.start()

    def settle_chunk(k, carry):
        with jax.named_scope("wait_y"):
            @pl.when((k != 2) | jnp.logical_not(outer))
            def _():
                copy_y(k).wait_recv()

            @pl.when((k == 2) & outer)
            def _():
                copy_first.wait_recv()
                copy_rest.wait_recv()
                with jax.named_scope("wait_d3"):
                    copy_d3.wait_recv()

        settle(2 * k, 0)
        settle(2 * k + 1, 0)
        return carry

    with jax.named_scope("settle"):
        lax.fori_loop(1, chunks - 1, settle_chunk, 0)
    half_of = slice(1, n_pop)
    with jax.named_scope("wait_lr"):
        wait_for(lall.at[half_of], r_l)
        wait_for(rall.at[half_of], r_r)
        wait_for(ranked.at[half_of], r_u)
    with jax.named_scope("turn"):
        for d in range(n_pop):
            place = pl.ds(pl.multiple_of(flip(p, d) * mem, mem), mem)
            right_all[place, :] = rall[d]
            left_v[place, :] = lall[d].astype(F32)
        left_t[...] = left_v[...].T
    with jax.named_scope("wait_y8"):
        copy_y(chunks - 1, 1).wait_recv()
    settle(last - 1, 0)
    before = nt_dot(row_picker(4), halves((sq_s[...], sq_a[...], sq_e[...], sq_t[...])))
    picker = row_picker(3)
    for i in order:
        part = slice(i * LANES, (i + 1) * LANES)
        with jax.named_scope("wait_end"):
            copy_end(i).wait_recv()
        with jax.named_scope("end"):
            post[i] = (before[:, part] + nt_dot(picker, halves(arrived(last, part))))[0:4]

            @pl.when(c == 0)
            def _():
                copy_post(i, 3).start()
                copy_post(i, 1).start()

            @pl.when(c == 1)
            def _():
                copy_post(i, 2).start()

    others = marks.at[half_of]

    @pl.when(c == 1)
    def _():
        with jax.named_scope("wait_far"):
            copy_far.wait_recv()
        own = lin_out[...] + lin_far[...]
        lifted = own[0:mem] * (SIGMA / math.sqrt(full))
        lifted2 = lifted * lifted
        extra_s = 2.0 * lifted * own[2 * mem:3 * mem] + lifted2 * norm_r
        extra_a = 2.0 * lifted * own[3 * mem:4 * mem] + lifted2 * norm_gr
        extra_e = lifted * own[mem:2 * mem]
        with jax.named_scope("wait_post"):
            wait_for(post_in, r_post)
        with jax.named_scope("errors"):
            late = jnp.concatenate([post[i] + post_in[0, i] + post_in[1, i] + post_in[2, i] for i in range(pieces)], axis=1)
            meansq = (late[0:1] + extra_s) / full
            inverse = lax.rsqrt(meansq + EPSILON)
            errors = inverse * inverse * (late[1:2] + extra_a) - 2.0 * inverse * (late[2:3] + extra_e) + late[3:4]
            summed = jnp.sum(errors, axis=1, keepdims=True)
            spot = lax.broadcasted_iota(jnp.int32, (mem, LANES), 0) + p * mem
            here = lax.broadcasted_iota(jnp.int32, (mem, LANES), 1) == spot
            marks[0] = jnp.sum(jnp.where(here, summed, 0.0), axis=0, keepdims=True)
            for d in range(n_pop - 1, -1, -1):
                copy_f(d, 0).start()
                if d > 0:
                    copy_f(d, 1).start()

    @pl.when(c == 0)
    def _():
        with jax.named_scope("wait_f"):
            wait_for(marks, r_f)

    @pl.when(c == 1)
    def _():
        with jax.named_scope("wait_f"):
            wait_for(others, r_f)

    fits[0:1] = sum((marks[d] for d in range(1, n_pop)), marks[0])
    fits[1:2] = sum((ranked[d] for d in range(1, n_pop)), ranked[0])
    for which in range(2):
        wait_for(send.at[which, 2:units], sent)
    wait_for(send.at[2], sent)
    wait_for(first_v, sent)
    wait_for(lall.at[half_of], sent)
    wait_for(rall.at[half_of], sent)
    wait_for(ranked.at[half_of], sent)
    for core in range(2):
        @pl.when(c == core)
        def _(core=core):
            for i in range(core, pieces):
                copy_a0(i).wait_send()
            for i in range(1 - core, pieces):
                copy_y0(i).wait_send()
            if core == 1:
                copy_swapped.wait_send()
            if core == 1:
                @pl.when(inner)
                def _():
                    copy_d2.wait_send()
                    copy_d3.wait_send()

            if core == 0:
                copy_lin.wait_send()
                wait_for(post_in.at[0:2], sent)
            else:
                copy_far.wait_send()
                wait_for(post_in.at[0], sent)
                wait_for(marks, sent)
                wait_for(others, sent)


def in_hbm(x):
    return pltpu.with_memory_space_constraint(x, pltpu.HBM)


def fused_shards(
    n_pop, n_mp, context, out_weight, residual, target, norm_gain, left_factors, right_factors, member_ranks
):
    tok, width = context.shape
    full = out_weight.shape[1]
    mem = left_factors.shape[0]
    rows = full // n_pop
    chunks = width // BLK
    units = width // LANES
    pieces = tok // LANES
    ranks = member_ranks.reshape(1, mem)
    anywhere = pl.BlockSpec(memory_space=pltpu.HBM)
    vmem = pl.BlockSpec(memory_space=pltpu.VMEM)
    dma = pltpu.SemaphoreType.DMA
    acc = pltpu.VMEM((tok, LANES), F32)
    group = pltpu.VMEM((4 * mem, tok), F32)
    base, left_t, right_all, fits = pl.pallas_call(
        functools.partial(kernel, n_pop, n_mp),
        name="es_step",
        out_shape=(
            jax.ShapeDtypeStruct((tok, width), F32),
            jax.ShapeDtypeStruct((rows, n_pop * mem), F32),
            jax.ShapeDtypeStruct((n_pop * mem, width), BF),
            jax.ShapeDtypeStruct((2, n_pop * mem), F32),
        ),
        in_specs=[anywhere] * 8,
        out_specs=[vmem] * 4,
        scratch_shapes=[
            pltpu.VMEM((4, chunks, width, BLK), BF),
            pltpu.VMEM((tok, width), BF),
            pltpu.VMEM((tok, width), BF),
            pltpu.VMEM((tok, width), BF),
            pltpu.VMEM((mem, width), BF),
            pltpu.VMEM((1, full), F32),
            pltpu.VMEM((mem, full), BF),
            pltpu.VMEM((1, mem), jnp.int32),
            pltpu.VMEM((3, units, tok, LANES), BF),
            pltpu.VMEM((3, units, tok, LANES), BF),
            pltpu.VMEM((2, 96, LANES), BF),
            pltpu.VMEM((2, 2, 96, LANES), BF),
            pltpu.VMEM((n_pop, mem, rows), BF),
            pltpu.VMEM((n_pop, mem, width), BF),
            acc, acc, acc, acc,
            group, group, group, group,
            pltpu.VMEM((pieces, 4, LANES), F32),
            pltpu.VMEM((n_mp - 1, pieces, 4, LANES), F32),
            pltpu.VMEM((LANES, LANES), BF),
            pltpu.VMEM((LANES, LANES), BF),
            pltpu.VMEM((160, LANES), BF),
            pltpu.VMEM((160, LANES), BF),
            pltpu.VMEM((n_pop, 1, LANES), F32),
            pltpu.VMEM((n_pop * mem, rows), F32),
            pltpu.VMEM((n_pop, 1, LANES), F32),
            dma((2,)),
            dma((2,)),
            dma((3,)),
            dma,
            dma((chunks - 1 + pieces,)),
            dma((chunks - 1 + 2 * pieces,)),
        ]
        + [dma] * 6
        + [dma((2,))]
        + [dma] * 4
        + [pltpu.SemaphoreType.REGULAR((3,))],
        compiler_params=pltpu.CompilerParams(
            collective_id=0,
            has_side_effects=True,
            vmem_limit_bytes=48 * 1024 * 1024,
        ),
    )(
        *map(in_hbm, (
            context, out_weight, residual, target, norm_gain.reshape(1, full), left_factors,
            right_factors, ranks,
        ))
    )
    count_all = n_pop * mem
    update, base, fitness = pl.pallas_call(
        functools.partial(finish, n_pop, math.sqrt(count_all) / SIGMA, tok * full),
        name="es_update",
        out_shape=(
            jax.ShapeDtypeStruct((rows, width), F32),
            jax.ShapeDtypeStruct((tok, width), F32),
            jax.ShapeDtypeStruct((1, mem), F32),
        ),
        in_specs=[vmem] * 4,
        out_specs=[anywhere] * 3,
        scratch_shapes=[
            pltpu.VMEM((rows, width), F32),
            pltpu.VMEM((1, mem), F32),
            dma,
        ],
        compiler_params=pltpu.CompilerParams(vmem_limit_bytes=16 * 1024 * 1024),
    )(left_t, right_all, base, fits)
    return (update, fitness.reshape(mem), base)


def finish(n_pop, scale, count, left_t, right_all, base_in, fits, update, base, fit, held, fit_v, sem):
    steps = held.shape[0] // 128
    mem = fit_v.shape[1]
    members = n_pop * mem
    copies = [
        pltpu.make_async_copy(base_in, base, sem),
        pltpu.make_async_copy(fit_v, fit, sem),
    ]
    copies[0].start()
    all_fit = fits[0:1] * (-1.0 / count)
    centre = all_fit - jnp.sum(all_fit, axis=1, keepdims=True) / members
    deviation = jnp.sqrt(jnp.sum(centre * centre, axis=1, keepdims=True) / members + 1e-05)
    weight = fits[1:2] + centre / deviation / members
    for i in range(steps):
        part = slice(i * 128, (i + 1) * 128)
        weighted = (left_t[part, :] * weight).astype(BF)
        held[part, :] = jnp.dot(weighted, right_all[...], preferred_element_type=F32) * scale
        copies.append(pltpu.make_async_copy(held.at[part], update.at[part], sem))
        copies[-1].start()
    p = lax.axis_index("pop")
    mine = jnp.zeros((1, mem), F32)
    for d in range(n_pop):
        mine = mine + jnp.where(p == d, 1.0, 0.0) * all_fit[:, d * mem:(d + 1) * mem]
    fit_v[...] = mine
    copies[1].start()
    for item in copies:
        item.wait()


def chosen(n_pop, n_mp, context, out_weight, *rest):
    tok, width = context.shape
    mem = rest[3].shape[0]
    full = out_weight.shape[1]
    chunks = width // BLK
    if n_mp == 4 and n_pop == 8 and width % BLK == 0 and chunks > 3 and (full // n_pop) % 128 == 0 and tok % 128 == 0 and mem == 16:
        return fused_shards(n_pop, n_mp, context, out_weight, *rest)
    return shards(context, out_weight, *rest)


def solution(mesh):
    in_specs = (
        P("pop", "mp"),
        P("mp", None),
        P("pop", "mp"),
        P("pop", "mp"),
        P(),
        P("pop", None),
        P("pop", None),
        P("pop"),
    )
    out_specs = (P("pop", "mp"), P("pop"), P("pop", "mp"))
    return jax.shard_map(
        functools.partial(chosen, mesh.shape["pop"], mesh.shape["mp"]), mesh=mesh, in_specs=in_specs, out_specs=out_specs, check_vma=False)
```

```python
import functools
import math

import jax
import jax.numpy as jnp
from jax import lax
from jax.experimental import pallas as pl
from jax.experimental.pallas import tpu as pltpu
from jax.sharding import PartitionSpec as P

SIGMA = 1.0
EPSILON = 1e-06


def error_sums(stream, lifted, right_rows, gain_part, target_rows, inverse):
    hidden = stream[:, None, :] + lifted[:, :, None] * right_rows[None, :, :]
    differ = gain_part * hidden * inverse[:, :, None] - target_rows[:, None, :]
    return jnp.sum(differ * differ, axis=(0, 2))


def utility(member_ranks, count_all):
    levels = jnp.arange(count_all).astype(jnp.float32)
    ceiling = math.log(count_all / 2 + 1)
    baseline = jnp.maximum(0.0, ceiling - jnp.log(levels + 1.0))
    shaped = jnp.maximum(0.0, ceiling - jnp.log(member_ranks.astype(jnp.float32) + 1.0))
    return shaped / jnp.sum(baseline) - 1.0 / count_all


def shards(
    context, out_weight, residual, target, norm_gain, left_factors, right_factors, member_ranks
):
    tok_count = context.shape[0]
    shard_width = context.shape[1]
    full_width = out_weight.shape[1]
    factor = SIGMA / math.sqrt(full_width)
    offset = lax.axis_index("mp") * shard_width
    left_cols = lax.dynamic_slice_in_dim(left_factors, offset, shard_width, 1)
    right_cols = lax.dynamic_slice_in_dim(right_factors, offset, shard_width, 1)
    partial_value = jnp.dot(context, out_weight, preferred_element_type=jnp.float32)
    projected = lax.dot_general(
        context, left_cols, (((1,), (1,)), ((), ())), preferred_element_type=jnp.float32
    )
    summed = lax.psum_scatter(
        partial_value.astype(jnp.bfloat16), "mp", scatter_dimension=1, tiled=True
    ).astype(jnp.float32)
    stream = residual.astype(jnp.float32) + summed
    gain_part = lax.dynamic_slice_in_dim(norm_gain, offset, shard_width, 0)
    factor_f = right_cols.astype(jnp.float32)
    crossed = jnp.dot(stream, factor_f.T, precision=lax.Precision.HIGHEST)
    per_token = jnp.sum(stream * stream, axis=1)
    per_member = jnp.sum(factor_f * factor_f, axis=1)
    projected, crossed, per_token, per_member = lax.psum(
        (projected, crossed, per_token, per_member), "mp"
    )
    lifted = factor * projected
    meansq = (
        per_token[:, None] + 2.0 * lifted * crossed + lifted * lifted * per_member[None, :]
    ) / full_width
    inverse = lax.rsqrt(meansq + EPSILON)
    local_error = error_sums(
        stream, lifted, factor_f, gain_part, target.astype(jnp.float32), inverse
    )
    member_total = lax.psum(local_error, "mp")
    fitness = -member_total / (tok_count * full_width)
    everyone = lax.all_gather(fitness, "pop", axis=0, tiled=True)
    count_all = everyone.shape[0]
    average = jnp.mean(everyone)
    centre = everyone - average
    spread = jnp.sqrt(jnp.mean(centre * centre) + 1e-05)
    weight = utility(member_ranks, count_all) + (fitness - average) / spread / count_all
    weighted = (weight[:, None] * left_factors.astype(jnp.float32)).astype(jnp.bfloat16)
    weighted_rows = lax.all_to_all(weighted, "pop", split_axis=1, concat_axis=0, tiled=True)
    right_all = lax.all_gather(right_cols, "pop", axis=0, tiled=True)
    update = lax.dot_general(
        weighted_rows, right_all, (((0,), (0,)), ((), ())), preferred_element_type=jnp.float32
    ) * (math.sqrt(count_all) / SIGMA)
    return (update, fitness, stream)


BLK = 256
LANES = 128
F32 = jnp.float32
BF = jnp.bfloat16


def nt_dot(a, b):
    return lax.dot_general(a, b, (((1,), (1,)), ((), ())), preferred_element_type=F32)


def split_two(x):
    hi = x.astype(BF)
    return hi, (x - hi.astype(F32)).astype(BF)


def halves(parts):
    return jnp.concatenate([piece for part in parts for piece in split_two(part)], axis=1)


def row_picker(count):
    shape = (8, count * 2 * LANES)
    owner = lax.broadcasted_iota(jnp.int32, shape, 1) // (2 * LANES)
    return jnp.where(owner == lax.broadcasted_iota(jnp.int32, shape, 0), 1.0, 0.0).astype(BF)


def flip(index, bits):
    for bit in (1, 2, 4):
        if bits & bit:
            index = index + bit - 2 * bit * ((index // bit) % 2)
    return index


def kernel(
    n_pop, n_mp, ctx_h, w_h, res_h, tgt_h, gain_h, left_h, right_h, ranks_h,
    base, left_t, right_all, fits,
    w_v, ctx, res, tgt, lcols, gain, right, ranks, send, recv, first_v, direct, lall, rall,
    sq_s, sq_a, sq_e, sq_t, lin, lin_in, lin_out, lin_far, post, post_in, swap, swap_in, detour_a, detour_b, detour_c, detour_e, marks, left_v, ranked,
    w_sem, top_sem, loc_sem, sent, r_a, r_y, r_b, r_top, r_lin, r_far, r_post, r_swap, r_d, r_z, r_l, r_r, r_u, r_f, rounds,
):
    tok, width = ctx.shape
    mem = right.shape[0]
    full = right.shape[1]
    rows = full // n_pop
    chunks = width // BLK
    units = width // LANES
    last = units - 1
    pieces = tok // LANES
    upper = 96
    low = (tok - upper) // 2
    cuts = [(0, upper), (upper, upper + low), (upper + low, tok)]
    members = mem * n_pop
    p = lax.axis_index("pop")
    q = lax.axis_index("mp")
    y = q // 2
    c = q % 2
    outer = (c == 1) & (p % 2 == 1)
    inner = (c == 1) & (p % 2 == 0)
    upper_z = (c == 1) & ((p // 2) % 2 == 1)
    lower_z = (c == 1) & ((p // 2) % 2 == 0)
    mate = flip(q, 1)
    across = flip(q, 2)
    diagonal = flip(q, 3)
    blocks = (diagonal, across, mate, q)
    other = 2 - 2 * y

    def remote(src, dst, ss, rs, pop, mp):
        return pltpu.make_async_remote_copy(
            src_ref=src, dst_ref=dst, send_sem=ss, recv_sem=rs,
            device_id=(pop, mp), device_id_type=pl.DeviceIdType.MESH,
        )

    def signal(sem, pop, mp):
        pl.semaphore_signal(sem, inc=1, device_id=(pop, mp), device_id_type=pl.DeviceIdType.MESH)

    def wait_for(ref, sem):
        pltpu.make_async_copy(ref, ref, sem).wait()

    def w_copy(s, k, sem):
        start = pl.multiple_of(blocks[s] * width + k * BLK, BLK)
        return pltpu.make_async_copy(w_h.at[:, pl.ds(start, BLK)], w_v.at[s, k], sem)

    def w_first(n):
        start = pl.multiple_of((other + n) * width, BLK)
        slot = 1 - c if n == 0 else c
        return pltpu.make_async_copy(w_h.at[:, pl.ds(start, BLK)], w_v.at[slot, 0], top_sem.at[n])

    def near_copy(k):
        return w_copy(3, k, loc_sem.at[2])

    def w_step(k, more):
        steps = [(1, k), (2, k)] if isinstance(k, jax.Array) or k > 0 else [(2, k)]
        if more:
            steps.append((0, k + 1))
        return [w_copy(s, i, w_sem.at[k % 2]) for s, i in steps]

    my_cols = pl.ds(pl.multiple_of(q * width, BLK), width)
    my_rows = pl.ds(pl.multiple_of(p * rows, LANES), rows)
    locals_ = [
        pltpu.make_async_copy(ctx_h.at[0:upper], ctx.at[0:upper], loc_sem.at[0]),
        pltpu.make_async_copy(ctx_h.at[upper:tok], ctx.at[upper:tok], loc_sem.at[1]),
        pltpu.make_async_copy(res_h, res, loc_sem.at[2]),
        pltpu.make_async_copy(tgt_h, tgt, loc_sem.at[2]),
        pltpu.make_async_copy(left_h.at[:, my_cols], lcols, loc_sem.at[2]),
        pltpu.make_async_copy(left_h.at[:, my_rows], lall.at[0], loc_sem.at[2]),
        pltpu.make_async_copy(right_h.at[:, my_cols], rall.at[0], loc_sem.at[2]),
        pltpu.make_async_copy(gain_h, gain, loc_sem.at[2]),
        pltpu.make_async_copy(right_h, right, loc_sem.at[2]),
        pltpu.make_async_copy(ranks_h, ranks, loc_sem.at[2]),
    ]
    locals_[0].start()
    w_first(0).start()

    barrier = pltpu.get_barrier_semaphore()
    for peer in (mate, across, diagonal):
        signal(barrier, p, peer)
    locals_[1].start()
    for bit in (1, 2, 4):
        signal(barrier, flip(p, bit), q)

    copy_top = remote(first_v, direct.at[c], sent, r_top, p, other)

    def copy_a(k):
        cols = pl.ds(2 * k, 2)
        return remote(send.at[0, cols], recv.at[0, cols], sent, r_a.at[pieces + k - 1], p, mate)

    tail = slice(0, 2 * LANES)
    everything = slice(0, tok)
    extra = chunks - 1 + 2 * pieces

    def strip(i):
        return slice(*cuts[i])

    def copy_a0(i):
        return remote(send.at[0, 0:2, strip(i)], recv.at[0, 0:2, strip(i)], sent, r_a.at[i], p, mate)

    def copy_y0(i):
        return remote(send.at[1, 0:2, strip(i)], recv.at[1, 0:2, strip(i)], sent, r_y.at[i], p, across)

    def copy_y(k, count=2):
        cols = pl.ds(2 * k, count)
        return remote(send.at[1, cols], recv.at[1, cols], sent, r_y.at[pieces + k - 1], p, across)

    def copy_end(i):
        part = slice(i * LANES, (i + 1) * LANES)
        return remote(send.at[1, last, part], recv.at[1, last, part], sent, r_y.at[pieces + chunks - 1 + i], p, across)

    detour = detour_a.shape[0]
    turn_unit = 5
    away = slice(0, detour)
    rest = slice(detour, tok)
    copy_d1 = remote(send.at[1, turn_unit, away], detour_a, sent, r_d.at[0], flip(p, 1), q)
    copy_d2 = remote(detour_a, detour_b, sent, r_d.at[1], p, across)
    copy_d3 = remote(detour_b, recv.at[1, turn_unit, away], sent, r_d.at[0], flip(p, 1), q)
    copy_z1 = remote(send.at[1, turn_unit - 1, away], detour_c, sent, r_z.at[0], flip(p, 2), q)
    copy_z2 = remote(detour_c, detour_e, sent, r_z.at[1], p, across)
    copy_z3 = remote(detour_e, recv.at[1, turn_unit - 1, away], sent, r_z.at[0], flip(p, 2), q)

    def copy_part(u, part, n):
        return remote(send.at[1, u, part], recv.at[1, u, part], sent, r_y.at[n], p, across)

    whole_4 = copy_part(turn_unit - 1, everything, pieces + 1)
    rest_4 = copy_part(turn_unit - 1, rest, pieces + 1)
    whole_5 = copy_part(turn_unit, everything, extra)
    rest_5 = copy_part(turn_unit, rest, extra)

    copy_swap = remote(send.at[1, last, tail], swap_in, sent, r_swap, p, mate)
    swapped = []
    for i in range(2):
        part = slice(i * LANES, (i + 1) * LANES)
        swapped.append(
            remote(swap.at[part], recv.at[1, last, part], sent, r_y.at[pieces + chunks - 1 + i], p, diagonal)
        )

    def copy_b(k):
        cols = pl.ds(2 * k, 2)
        return remote(send.at[2, cols], recv.at[2, cols], sent, r_b, p, mate)

    def copy_l(d):
        peer = flip(p, d)
        cols = pl.ds(pl.multiple_of(peer * rows, LANES), rows)
        return remote(left_h.at[:, cols], lall.at[d], sent, r_l, peer, q)

    def copy_r(d):
        return remote(right_h.at[:, my_cols], rall.at[d], sent, r_r, flip(p, d), q)

    def copy_u(d):
        return remote(ranked.at[0], ranked.at[d], sent, r_u, flip(p, d), q)

    def copy_f(d, core):
        return remote(marks.at[0], marks.at[d], sent, r_f, flip(p, d), 2 * y + core)

    copy_lin = remote(lin, lin_in, sent, r_lin, p, mate)
    copy_far = remote(lin_out, lin_far, sent, r_far, p, across)

    def copy_post(i, d):
        return remote(post.at[i], post_in.at[d - 1, i], sent, r_post, p, flip(q, d))

    def split_store(which, k, value):
        send[which, 2 * k] = value[:, :LANES]
        send[which, 2 * k + 1] = value[:, LANES:]

    def product(s, k):
        return jnp.dot(ctx[...], w_v[s, k], preferred_element_type=F32)

    order = [*range(2, pieces), 1, 0]
    with jax.named_scope("load0"):
        locals_[0].wait()
        w_first(0).wait()
    w_first(1).start()
    top = jnp.dot(ctx[0:upper, :], w_v[1 - c, 0], preferred_element_type=F32).astype(BF)
    first_v[0] = top[:, :LANES]
    first_v[1] = top[:, LANES:]
    def strip_product(s, i):
        return jnp.dot(ctx[strip(i), :], w_v[s, 0], preferred_element_type=F32)

    def prepare(i):
        value = strip_product(0, i).astype(BF)
        send[0, 0, strip(i)] = value[:, :LANES]
        send[0, 1, strip(i)] = value[:, LANES:]

    def give(i):
        prepare(i)
        copy_a0(i).start()

    @pl.when((c == 1) & (y == 0))
    def _():
        locals_[1].wait()
        prepare(1)

    with jax.named_scope("barrier"):
        pl.semaphore_wait(barrier, 6)
    copy_top.start()
    signal(rounds.at[0], flip(p, 1), q)
    for item in w_step(0, True):
        item.start()

    @pl.when((c == 0) | (y == 1))
    def _():
        locals_[1].wait()

    def pass_on(i, value):
        send[1, 0, strip(i)] = (value[:, :LANES] + recv[0, 0, strip(i)].astype(F32)).astype(BF)
        send[1, 1, strip(i)] = (value[:, LANES:] + recv[0, 1, strip(i)].astype(F32)).astype(BF)
        copy_y0(i).start()

    @pl.when(c == 0)
    def _():
        mine = [strip_product(1, i) for i in (1, 2)]
        copy_a0(1).wait_recv()
        pass_on(1, mine[0])
        w_first(1).wait()
        give(1)
        copy_a0(2).wait_recv()
        pass_on(2, mine[1])
        give(2)
        give(0)
        send[1, 0, strip(0)] = first_v[0]
        send[1, 1, strip(0)] = first_v[1]

    @pl.when((c == 1) & (y == 1))
    def _():
        prepare(1)

    @pl.when(c == 1)
    def _():
        copy_a0(1).start()
        give(2)
        send[0, 0, strip(0)] = first_v[0]
        send[0, 1, strip(0)] = first_v[1]
        w_first(1).wait()

    for item in w_step(1, True):
        item.start()
    near_copy(0).start()
    for item in w_step(0, True):
        item.wait()
    split_store(0, 1, product(0, 1).astype(BF))
    copy_a(1).start()
    for item in w_step(2, True):
        item.start()

    @pl.when(c == 1)
    def _():
        mine = [strip_product(1, i) for i in (1, 2, 0)]
        with jax.named_scope("wait_a0"):
            for i in (1, 2, 0):
                copy_a0(i).wait_recv()
                pass_on(i, mine[i - 1])


    def far(k, carry):
        for item in w_step(k, False):
            item.wait()

        @pl.when(k + 1 < chunks)
        def _():
            w_copy(0, k + 1, w_sem.at[k % 2]).wait()

        mine = product(1, k)
        @pl.when((k == 3) & inner)
        def _():
            with jax.named_scope("wait_d1"):
                copy_d1.wait_recv()
            copy_d2.start()

        @pl.when((k == 3) & lower_z)
        def _():
            with jax.named_scope("wait_z1"):
                copy_z1.wait_recv()
            copy_z2.start()

        with jax.named_scope("wait_a"):
            copy_a(k).wait_recv()
        send[1, 2 * k] = (mine[:, :LANES] + recv[0, 2 * k].astype(F32)).astype(BF)
        send[1, 2 * k + 1] = (mine[:, LANES:] + recv[0, 2 * k + 1].astype(F32)).astype(BF)

        @pl.when((k + 1 < chunks) & (k != 2))
        def _():
            copy_y(k).start()

        @pl.when((k == 2) & outer)
        def _():
            copy_d1.start()

        @pl.when((k == 2) & upper_z)
        def _():
            copy_z1.start()
            rest_4.start()

        @pl.when((k == 2) & jnp.logical_not(upper_z))
        def _():
            whole_4.start()

        @pl.when((k == 2) & outer)
        def _():
            rest_5.start()

        @pl.when((k == 2) & jnp.logical_not(outer))
        def _():
            whole_5.start()

        @pl.when((k + 1 == chunks) & (c == 0))
        def _():
            send[1, last, tail] = mine[tail, LANES:].astype(BF)
            copy_swap.start()

        @pl.when(k + 2 < chunks)
        def _():
            for item in w_step(k + 2, False):
                item.start()

        @pl.when(k + 3 < chunks)
        def _():
            w_copy(0, k + 3, w_sem.at[k % 2]).start()

        near_copy(k).start()

        @pl.when(k == 1)
        def _():
            for item in locals_[2:]:
                item.start()
            pl.semaphore_wait(rounds.at[0], 1)
            signal(rounds.at[1], flip(p, 2), q)

        @pl.when(k == 2)
        def _():
            pl.semaphore_wait(rounds.at[1], 1)
            signal(rounds.at[2], flip(p, 4), q)

        @pl.when(k == 3)
        def _():
            pl.semaphore_wait(rounds.at[2], 1)
            for d in range(1, n_pop):
                copy_r(n_pop - d).start()
                copy_l(n_pop - d).start()

        @pl.when(k + 1 < chunks)
        def _():
            split_store(0, k + 1, product(0, k + 1).astype(BF))
            copy_a(k + 1).start()

        @pl.when(k == 1)
        def _():
            split_store(2, 0, product(2, 0).astype(BF))
            copy_b(0).start()

        split_store(2, k, product(2, k).astype(BF))
        copy_b(k).start()
        return carry

    with jax.named_scope("far"):
        lax.fori_loop(1, chunks, far, 0)

    for item in locals_[2:]:
        item.wait()
    wait_for(w_v.at[3], loc_sem.at[2])

    lane = lax.broadcasted_iota(jnp.int32, (1, LANES), 1)
    ceiling = math.log(members / 2 + 1)
    whole = sum(max(0.0, ceiling - math.log(i + 1.0)) for i in range(members))
    shaped = jnp.maximum(0.0, ceiling - jnp.log(ranks[...].astype(F32) + 1.0)) / whole - 1.0 / members
    ranked[0] = jnp.where(lane // mem == p, jnp.concatenate([shaped] * n_pop, axis=1), 0.0)
    for d in range(1, n_pop):
        copy_u(d).start()

    def near(k, carry):
        cols = pl.ds(pl.multiple_of(k * BLK, BLK), BLK)
        base[:, cols] = product(3, k) + res[:, cols].astype(F32)
        return carry

    with jax.named_scope("near"):
        lax.fori_loop(0, chunks, near, 0)

    @pl.when(c == 1)
    def _():
        copy_swap.wait_recv()
        swap[...] = (send[0, last, tail].astype(F32) + swap_in[...].astype(F32)).astype(BF)
        for item in reversed(swapped):
            item.start()

    copy_y(chunks - 1, 1).start()

    def spread(slot, value):
        lin[slot * mem:(slot + 1) * mem, :] = value

    with jax.named_scope("early"):
        r_mine = rall[0].astype(F32)
        gr_hi, gr_lo = split_two(r_mine * gain[:, my_cols])
        spread(0, nt_dot(lcols[...], ctx[...]))
        spread(1, nt_dot(gr_hi, tgt[...]) + nt_dot(gr_lo, tgt[...]))
        r_full = right[...].astype(F32)
        gr_full = r_full * gain[...]
        norm_r = jnp.sum(r_full * r_full, axis=1, keepdims=True)
        norm_gr = jnp.sum(gr_full * gr_full, axis=1, keepdims=True)
        for acc in (sq_s, sq_a, sq_e, sq_t):
            acc[...] = jnp.zeros_like(acc)

    def mixed(block, start, size):
        cols = pl.ds(pl.multiple_of(block * width + start, LANES), size)
        r = right[:, cols]
        g = gain[:, cols]
        hi, low = split_two(r.astype(F32) * (g * g))
        return jnp.concatenate([r, hi, low], axis=0)

    def linear(k, carry):
        crossed, crossed_g = carry
        near_rows = mixed(q, k * BLK, BLK)
        far_rows = mixed(across, k * BLK, BLK)
        for h in range(2):
            cols = pl.ds(pl.multiple_of(k * BLK + h * LANES, LANES), LANES)
            part = slice(h * LANES, (h + 1) * LANES)
            u = 2 * k + h
            s = base[:, cols] + recv[2, u].astype(F32)
            base[:, cols] = s
            hi, low = split_two(s)
            both = nt_dot(near_rows[:, part], hi) + nt_dot(near_rows[:, part], low) + nt_dot(far_rows[:, part], send[1, u])
            crossed = crossed + both[0:mem]
            crossed_g = crossed_g + both[mem:2 * mem] + both[2 * mem:3 * mem]
            wide = tgt[:, cols].astype(F32)
            sq_t[...] += wide * wide
        return crossed, crossed_g

    with jax.named_scope("wait_b"):
        wait_for(recv.at[2], r_b)
    with jax.named_scope("linear"):
        top_rows = mixed(other, 0, BLK)
        top = nt_dot(top_rows[:, :LANES], first_v[0]) + nt_dot(top_rows[:, LANES:], first_v[1])
        late = nt_dot(mixed(other, last * LANES, LANES), send[0, last, tail])
        top = sum(jnp.concatenate([v, jnp.zeros((3 * mem, tok - v.shape[1]), F32)], axis=1) for v in (top, late))
        top = top * jnp.where(c == 1, 1.0, 0.0)
        carry = (top[0:mem], top[mem:2 * mem] + top[2 * mem:3 * mem])
        crossed, crossed_g = lax.fori_loop(0, chunks, linear, carry)
        spread(2, crossed)
        spread(3, crossed_g)

    @pl.when(c == 0)
    def _():
        copy_lin.start()
        for i in order[:-2]:
            copy_end(i).start()

    def arrived(u, part):
        cols = pl.ds(pl.multiple_of(u * LANES, LANES), LANES)
        gain_u = gain[:, pl.ds(pl.multiple_of(q * width + u * LANES, LANES), LANES)]
        s = base[part, cols] + recv[1, u, part].astype(F32)
        base[part, cols] = s
        gs = s * gain_u
        return s * s, gs * gs, gs * tgt[part, cols].astype(F32)

    def settle(u, carry):
        for acc, item in zip((sq_s, sq_a, sq_e), arrived(u, everything)):
            acc[...] += item
        return carry

    with jax.named_scope("wait_y0"):
        for i in range(1, pieces):
            copy_y0(i).wait_recv()

        @pl.when(c == 0)
        def _():
            wait_for(direct, r_top)
            for u in range(2):
                recv[1, u, strip(0)] = jnp.zeros((upper, LANES), BF)
                base[0:upper, u * LANES:(u + 1) * LANES] += direct[0, u].astype(F32) + direct[1, u].astype(F32)

        @pl.when(c == 1)
        def _():
            copy_y0(0).wait_recv()

    lax.fori_loop(0, 2, settle, 0)

    @pl.when(c == 1)
    def _():
        for i in order:
            copy_end(i).start()
        with jax.named_scope("wait_lin"):
            copy_lin.wait_recv()
        lin_out[...] = lin[...] + lin_in[...]
        copy_far.start()

    @pl.when(inner)
    def _():
        with jax.named_scope("wait_d2"):
            copy_d2.wait_recv()
        copy_d3.start()

    @pl.when(lower_z)
    def _():
        with jax.named_scope("wait_z2"):
            copy_z2.wait_recv()
        copy_z3.start()

    def settle_chunk(k, carry):
        with jax.named_scope("wait_y"):
            @pl.when(k != 2)
            def _():
                copy_y(k).wait_recv()

            @pl.when((k == 2) & upper_z)
            def _():
                rest_4.wait_recv()
                with jax.named_scope("wait_z3"):
                    copy_z3.wait_recv()

            @pl.when((k == 2) & jnp.logical_not(upper_z))
            def _():
                whole_4.wait_recv()

            @pl.when((k == 2) & outer)
            def _():
                rest_5.wait_recv()
                with jax.named_scope("wait_d3"):
                    copy_d3.wait_recv()

            @pl.when((k == 2) & jnp.logical_not(outer))
            def _():
                whole_5.wait_recv()

        settle(2 * k, 0)
        settle(2 * k + 1, 0)
        return carry

    with jax.named_scope("settle"):
        lax.fori_loop(1, 2, settle_chunk, 0)
        lax.fori_loop(3, chunks - 1, settle_chunk, 0)
    half_of = slice(1, n_pop)
    with jax.named_scope("wait_lr"):
        wait_for(lall.at[half_of], r_l)
        wait_for(rall.at[half_of], r_r)
        wait_for(ranked.at[half_of], r_u)
    with jax.named_scope("turn"):
        for d in range(n_pop):
            place = pl.ds(pl.multiple_of(flip(p, d) * mem, mem), mem)
            right_all[place, :] = rall[d]
            left_v[place, :] = lall[d].astype(F32)
        left_t[...] = left_v[...].T
    with jax.named_scope("wait_y8"):
        copy_y(chunks - 1, 1).wait_recv()
    settle(last - 1, 0)
    lax.fori_loop(2, 3, settle_chunk, 0)
    before = nt_dot(row_picker(4), halves((sq_s[...], sq_a[...], sq_e[...], sq_t[...])))
    picker = row_picker(3)
    for i in order:
        part = slice(i * LANES, (i + 1) * LANES)
        with jax.named_scope("wait_end"):
            copy_end(i).wait_recv()
        with jax.named_scope("end"):
            post[i] = (before[:, part] + nt_dot(picker, halves(arrived(last, part))))[0:4]

            @pl.when(c == 0)
            def _():
                copy_post(i, 3).start()
                copy_post(i, 1).start()

            @pl.when(c == 1)
            def _():
                copy_post(i, 2).start()

    others = marks.at[half_of]

    @pl.when(c == 1)
    def _():
        with jax.named_scope("wait_far"):
            copy_far.wait_recv()
        own = lin_out[...] + lin_far[...]
        lifted = own[0:mem] * (SIGMA / math.sqrt(full))
        lifted2 = lifted * lifted
        extra_s = 2.0 * lifted * own[2 * mem:3 * mem] + lifted2 * norm_r
        extra_a = 2.0 * lifted * own[3 * mem:4 * mem] + lifted2 * norm_gr
        extra_e = lifted * own[mem:2 * mem]
        with jax.named_scope("wait_post"):
            wait_for(post_in, r_post)
        with jax.named_scope("errors"):
            late = jnp.concatenate([post[i] + post_in[0, i] + post_in[1, i] + post_in[2, i] for i in range(pieces)], axis=1)
            meansq = (late[0:1] + extra_s) / full
            inverse = lax.rsqrt(meansq + EPSILON)
            errors = inverse * inverse * (late[1:2] + extra_a) - 2.0 * inverse * (late[2:3] + extra_e) + late[3:4]
            summed = jnp.sum(errors, axis=1, keepdims=True)
            spot = lax.broadcasted_iota(jnp.int32, (mem, LANES), 0) + p * mem
            here = lax.broadcasted_iota(jnp.int32, (mem, LANES), 1) == spot
            marks[0] = jnp.sum(jnp.where(here, summed, 0.0), axis=0, keepdims=True)
            for d in range(n_pop - 1, -1, -1):
                copy_f(d, 0).start()
                if d > 0:
                    copy_f(d, 1).start()

    @pl.when(c == 0)
    def _():
        with jax.named_scope("wait_f"):
            wait_for(marks, r_f)

    @pl.when(c == 1)
    def _():
        with jax.named_scope("wait_f"):
            wait_for(others, r_f)

    fits[0:1] = sum((marks[d] for d in range(1, n_pop)), marks[0])
    fits[1:2] = sum((ranked[d] for d in range(1, n_pop)), ranked[0])
    for which in range(2):
        wait_for(send.at[which, 2:units], sent)
    wait_for(send.at[2], sent)
    wait_for(first_v, sent)
    wait_for(lall.at[half_of], sent)
    wait_for(rall.at[half_of], sent)
    wait_for(ranked.at[half_of], sent)
    for core in range(2):
        @pl.when(c == core)
        def _(core=core):
            for i in range(core, pieces):
                copy_a0(i).wait_send()
            for i in range(1 - core, pieces):
                copy_y0(i).wait_send()
            if core == 1:
                for item in swapped:
                    item.wait_send()
            if core == 1:
                @pl.when(inner)
                def _():
                    copy_d2.wait_send()
                    copy_d3.wait_send()

                @pl.when(lower_z)
                def _():
                    copy_z2.wait_send()
                    copy_z3.wait_send()

            if core == 0:
                copy_lin.wait_send()
                wait_for(post_in.at[0:2], sent)
            else:
                copy_far.wait_send()
                wait_for(post_in.at[0], sent)
                wait_for(marks, sent)
                wait_for(others, sent)


def in_hbm(x):
    return pltpu.with_memory_space_constraint(x, pltpu.HBM)


def fused_shards(
    n_pop, n_mp, context, out_weight, residual, target, norm_gain, left_factors, right_factors, member_ranks
):
    tok, width = context.shape
    full = out_weight.shape[1]
    mem = left_factors.shape[0]
    rows = full // n_pop
    chunks = width // BLK
    units = width // LANES
    pieces = tok // LANES
    ranks = member_ranks.reshape(1, mem)
    anywhere = pl.BlockSpec(memory_space=pltpu.HBM)
    vmem = pl.BlockSpec(memory_space=pltpu.VMEM)
    dma = pltpu.SemaphoreType.DMA
    acc = pltpu.VMEM((tok, LANES), F32)
    group = pltpu.VMEM((4 * mem, tok), F32)
    base, left_t, right_all, fits = pl.pallas_call(
        functools.partial(kernel, n_pop, n_mp),
        name="es_step",
        out_shape=(
            jax.ShapeDtypeStruct((tok, width), F32),
            jax.ShapeDtypeStruct((rows, n_pop * mem), F32),
            jax.ShapeDtypeStruct((n_pop * mem, width), BF),
            jax.ShapeDtypeStruct((2, n_pop * mem), F32),
        ),
        in_specs=[anywhere] * 8,
        out_specs=[vmem] * 4,
        scratch_shapes=[
            pltpu.VMEM((4, chunks, width, BLK), BF),
            pltpu.VMEM((tok, width), BF),
            pltpu.VMEM((tok, width), BF),
            pltpu.VMEM((tok, width), BF),
            pltpu.VMEM((mem, width), BF),
            pltpu.VMEM((1, full), F32),
            pltpu.VMEM((mem, full), BF),
            pltpu.VMEM((1, mem), jnp.int32),
            pltpu.VMEM((3, units, tok, LANES), BF),
            pltpu.VMEM((3, units, tok, LANES), BF),
            pltpu.VMEM((2, 96, LANES), BF),
            pltpu.VMEM((2, 2, 96, LANES), BF),
            pltpu.VMEM((n_pop, mem, rows), BF),
            pltpu.VMEM((n_pop, mem, width), BF),
            acc, acc, acc, acc,
            group, group, group, group,
            pltpu.VMEM((pieces, 4, LANES), F32),
            pltpu.VMEM((n_mp - 1, pieces, 4, LANES), F32),
            pltpu.VMEM((2 * LANES, LANES), BF),
            pltpu.VMEM((2 * LANES, LANES), BF),
            pltpu.VMEM((160, LANES), BF),
            pltpu.VMEM((160, LANES), BF),
            pltpu.VMEM((160, LANES), BF),
            pltpu.VMEM((160, LANES), BF),
            pltpu.VMEM((n_pop, 1, LANES), F32),
            pltpu.VMEM((n_pop * mem, rows), F32),
            pltpu.VMEM((n_pop, 1, LANES), F32),
            dma((2,)),
            dma((2,)),
            dma((3,)),
            dma,
            dma((chunks - 1 + pieces,)),
            dma((chunks + 2 * pieces,)),
        ]
        + [dma] * 6
        + [dma((2,))] * 2
        + [dma] * 4
        + [pltpu.SemaphoreType.REGULAR((3,))],
        compiler_params=pltpu.CompilerParams(
            collective_id=0,
            has_side_effects=True,
            vmem_limit_bytes=48 * 1024 * 1024,
        ),
    )(
        *map(in_hbm, (
            context, out_weight, residual, target, norm_gain.reshape(1, full), left_factors,
            right_factors, ranks,
        ))
    )
    count_all = n_pop * mem
    update, base, fitness = pl.pallas_call(
        functools.partial(finish, n_pop, math.sqrt(count_all) / SIGMA, tok * full),
        name="es_update",
        out_shape=(
            jax.ShapeDtypeStruct((rows, width), F32),
            jax.ShapeDtypeStruct((tok, width), F32),
            jax.ShapeDtypeStruct((1, mem), F32),
        ),
        in_specs=[vmem] * 4,
        out_specs=[anywhere] * 3,
        scratch_shapes=[
            pltpu.VMEM((rows, width), F32),
            pltpu.VMEM((1, mem), F32),
            dma,
        ],
        compiler_params=pltpu.CompilerParams(vmem_limit_bytes=16 * 1024 * 1024),
    )(left_t, right_all, base, fits)
    return (update, fitness.reshape(mem), base)


def finish(n_pop, scale, count, left_t, right_all, base_in, fits, update, base, fit, held, fit_v, sem):
    steps = held.shape[0] // 128
    mem = fit_v.shape[1]
    members = n_pop * mem
    copies = [
        pltpu.make_async_copy(base_in, base, sem),
        pltpu.make_async_copy(fit_v, fit, sem),
    ]
    copies[0].start()
    all_fit = fits[0:1] * (-1.0 / count)
    centre = all_fit - jnp.sum(all_fit, axis=1, keepdims=True) / members
    deviation = jnp.sqrt(jnp.sum(centre * centre, axis=1, keepdims=True) / members + 1e-05)
    weight = fits[1:2] + centre / deviation / members
    for i in range(steps):
        part = slice(i * 128, (i + 1) * 128)
        weighted = (left_t[part, :] * weight).astype(BF)
        held[part, :] = jnp.dot(weighted, right_all[...], preferred_element_type=F32) * scale
        copies.append(pltpu.make_async_copy(held.at[part], update.at[part], sem))
        copies[-1].start()
    p = lax.axis_index("pop")
    mine = jnp.zeros((1, mem), F32)
    for d in range(n_pop):
        mine = mine + jnp.where(p == d, 1.0, 0.0) * all_fit[:, d * mem:(d + 1) * mem]
    fit_v[...] = mine
    copies[1].start()
    for item in copies:
        item.wait()


def chosen(n_pop, n_mp, context, out_weight, *rest):
    tok, width = context.shape
    mem = rest[3].shape[0]
    full = out_weight.shape[1]
    chunks = width // BLK
    if n_mp == 4 and n_pop == 8 and width % BLK == 0 and chunks > 3 and (full // n_pop) % 128 == 0 and tok == 3 * LANES and mem == 16:
        return fused_shards(n_pop, n_mp, context, out_weight, *rest)
    return shards(context, out_weight, *rest)


def solution(mesh):
    in_specs = (
        P("pop", "mp"),
        P("mp", None),
        P("pop", "mp"),
        P("pop", "mp"),
        P(),
        P("pop", None),
        P("pop", None),
        P("pop"),
    )
    out_specs = (P("pop", "mp"), P("pop"), P("pop", "mp"))
    return jax.shard_map(
        functools.partial(chosen, mesh.shape["pop"], mesh.shape["mp"]), mesh=mesh, in_specs=in_specs, out_specs=out_specs, check_vma=False)
```

```python
import functools
import math

import jax
import jax.numpy as jnp
from jax import lax
from jax.experimental import pallas as pl
from jax.experimental.pallas import tpu as pltpu
from jax.sharding import PartitionSpec as P

SIGMA = 1.0
EPSILON = 1e-06


def error_sums(stream, lifted, right_rows, gain_part, target_rows, inverse):
    hidden = stream[:, None, :] + lifted[:, :, None] * right_rows[None, :, :]
    differ = gain_part * hidden * inverse[:, :, None] - target_rows[:, None, :]
    return jnp.sum(differ * differ, axis=(0, 2))


def utility(member_ranks, count_all):
    levels = jnp.arange(count_all).astype(jnp.float32)
    ceiling = math.log(count_all / 2 + 1)
    baseline = jnp.maximum(0.0, ceiling - jnp.log(levels + 1.0))
    shaped = jnp.maximum(0.0, ceiling - jnp.log(member_ranks.astype(jnp.float32) + 1.0))
    return shaped / jnp.sum(baseline) - 1.0 / count_all


def shards(
    context, out_weight, residual, target, norm_gain, left_factors, right_factors, member_ranks
):
    tok_count = context.shape[0]
    shard_width = context.shape[1]
    full_width = out_weight.shape[1]
    factor = SIGMA / math.sqrt(full_width)
    offset = lax.axis_index("mp") * shard_width
    left_cols = lax.dynamic_slice_in_dim(left_factors, offset, shard_width, 1)
    right_cols = lax.dynamic_slice_in_dim(right_factors, offset, shard_width, 1)
    partial_value = jnp.dot(context, out_weight, preferred_element_type=jnp.float32)
    projected = lax.dot_general(
        context, left_cols, (((1,), (1,)), ((), ())), preferred_element_type=jnp.float32
    )
    summed = lax.psum_scatter(
        partial_value.astype(jnp.bfloat16), "mp", scatter_dimension=1, tiled=True
    ).astype(jnp.float32)
    stream = residual.astype(jnp.float32) + summed
    gain_part = lax.dynamic_slice_in_dim(norm_gain, offset, shard_width, 0)
    factor_f = right_cols.astype(jnp.float32)
    crossed = jnp.dot(stream, factor_f.T, precision=lax.Precision.HIGHEST)
    per_token = jnp.sum(stream * stream, axis=1)
    per_member = jnp.sum(factor_f * factor_f, axis=1)
    projected, crossed, per_token, per_member = lax.psum(
        (projected, crossed, per_token, per_member), "mp"
    )
    lifted = factor * projected
    meansq = (
        per_token[:, None] + 2.0 * lifted * crossed + lifted * lifted * per_member[None, :]
    ) / full_width
    inverse = lax.rsqrt(meansq + EPSILON)
    local_error = error_sums(
        stream, lifted, factor_f, gain_part, target.astype(jnp.float32), inverse
    )
    member_total = lax.psum(local_error, "mp")
    fitness = -member_total / (tok_count * full_width)
    everyone = lax.all_gather(fitness, "pop", axis=0, tiled=True)
    count_all = everyone.shape[0]
    average = jnp.mean(everyone)
    centre = everyone - average
    spread = jnp.sqrt(jnp.mean(centre * centre) + 1e-05)
    weight = utility(member_ranks, count_all) + (fitness - average) / spread / count_all
    weighted = (weight[:, None] * left_factors.astype(jnp.float32)).astype(jnp.bfloat16)
    weighted_rows = lax.all_to_all(weighted, "pop", split_axis=1, concat_axis=0, tiled=True)
    right_all = lax.all_gather(right_cols, "pop", axis=0, tiled=True)
    update = lax.dot_general(
        weighted_rows, right_all, (((0,), (0,)), ((), ())), preferred_element_type=jnp.float32
    ) * (math.sqrt(count_all) / SIGMA)
    return (update, fitness, stream)


BLK = 256
LANES = 128
F32 = jnp.float32
BF = jnp.bfloat16


def nt_dot(a, b):
    return lax.dot_general(a, b, (((1,), (1,)), ((), ())), preferred_element_type=F32)


def split_two(x):
    hi = x.astype(BF)
    return hi, (x - hi.astype(F32)).astype(BF)


def halves(parts):
    return jnp.concatenate([piece for part in parts for piece in split_two(part)], axis=1)


def row_picker(count):
    shape = (8, count * 2 * LANES)
    owner = lax.broadcasted_iota(jnp.int32, shape, 1) // (2 * LANES)
    return jnp.where(owner == lax.broadcasted_iota(jnp.int32, shape, 0), 1.0, 0.0).astype(BF)


def flip(index, bits):
    for bit in (1, 2, 4):
        if bits & bit:
            index = index + bit - 2 * bit * ((index // bit) % 2)
    return index


def kernel(
    n_pop, n_mp, ctx_h, w_h, res_h, tgt_h, gain_h, left_h, right_h, ranks_h,
    base, left_t, right_all, fits,
    w_v, ctx, res, tgt, lcols, gain, right, ranks, send, recv, first_v, direct, lall, rall,
    sq_s, sq_a, sq_e, sq_t, lin, lin_in, lin_out, lin_far, post, post_in, swap, swap_in, detour_a, detour_b, detour_c, detour_e, marks, left_v, ranked,
    w_sem, top_sem, loc_sem, sent, r_a, r_y, r_b, r_top, r_lin, r_far, r_post, r_swap, r_d, r_z, r_l, r_r, r_u, r_f, rounds,
):
    tok, width = ctx.shape
    mem = right.shape[0]
    full = right.shape[1]
    rows = full // n_pop
    chunks = width // BLK
    units = width // LANES
    last = units - 1
    pieces = tok // LANES
    upper = 96
    low = (tok - upper) // 2
    cuts = [(0, upper), (upper, upper + low), (upper + low, tok)]
    members = mem * n_pop
    p = lax.axis_index("pop")
    q = lax.axis_index("mp")
    y = q // 2
    c = q % 2
    outer = (c == 1) & (p % 2 == 1)
    inner = (c == 1) & (p % 2 == 0)
    upper_z = (c == 1) & ((p // 2) % 2 == 1)
    lower_z = (c == 1) & ((p // 2) % 2 == 0)
    mate = flip(q, 1)
    across = flip(q, 2)
    diagonal = flip(q, 3)
    blocks = (diagonal, across, mate, q)
    other = 2 - 2 * y

    def remote(src, dst, ss, rs, pop, mp):
        return pltpu.make_async_remote_copy(
            src_ref=src, dst_ref=dst, send_sem=ss, recv_sem=rs,
            device_id=(pop, mp), device_id_type=pl.DeviceIdType.MESH,
        )

    def signal(sem, pop, mp):
        pl.semaphore_signal(sem, inc=1, device_id=(pop, mp), device_id_type=pl.DeviceIdType.MESH)

    def wait_for(ref, sem):
        pltpu.make_async_copy(ref, ref, sem).wait()

    def w_copy(s, k, sem):
        start = pl.multiple_of(blocks[s] * width + k * BLK, BLK)
        return pltpu.make_async_copy(w_h.at[:, pl.ds(start, BLK)], w_v.at[s, k], sem)

    def w_first(n):
        start = pl.multiple_of((other + n) * width, BLK)
        slot = 1 - c if n == 0 else c
        return pltpu.make_async_copy(w_h.at[:, pl.ds(start, BLK)], w_v.at[slot, 0], top_sem.at[n])

    def near_copy(k):
        return w_copy(3, k, loc_sem.at[2])

    def w_step(k, more):
        steps = [(1, k), (2, k)] if isinstance(k, jax.Array) or k > 0 else [(2, k)]
        if more:
            steps.append((0, k + 1))
        return [w_copy(s, i, w_sem.at[k % 2]) for s, i in steps]

    my_cols = pl.ds(pl.multiple_of(q * width, BLK), width)
    my_rows = pl.ds(pl.multiple_of(p * rows, LANES), rows)
    locals_ = [
        pltpu.make_async_copy(ctx_h.at[0:upper], ctx.at[0:upper], loc_sem.at[0]),
        pltpu.make_async_copy(ctx_h.at[upper:tok], ctx.at[upper:tok], loc_sem.at[1]),
        pltpu.make_async_copy(res_h, res, loc_sem.at[2]),
        pltpu.make_async_copy(tgt_h, tgt, loc_sem.at[2]),
        pltpu.make_async_copy(left_h.at[:, my_cols], lcols, loc_sem.at[2]),
        pltpu.make_async_copy(left_h.at[:, my_rows], lall.at[0], loc_sem.at[2]),
        pltpu.make_async_copy(right_h.at[:, my_cols], rall.at[0], loc_sem.at[2]),
        pltpu.make_async_copy(gain_h, gain, loc_sem.at[2]),
        pltpu.make_async_copy(right_h, right, loc_sem.at[2]),
        pltpu.make_async_copy(ranks_h, ranks, loc_sem.at[2]),
    ]
    locals_[0].start()
    w_first(0).start()

    barrier = pltpu.get_barrier_semaphore()
    for peer in (mate, across, diagonal):
        signal(barrier, p, peer)
    locals_[1].start()
    for bit in (1, 2, 4):
        signal(barrier, flip(p, bit), q)

    copy_top = remote(first_v, direct.at[c], sent, r_top, p, other)

    def copy_a(k):
        cols = pl.ds(2 * k, 2)
        return remote(send.at[0, cols], recv.at[0, cols], sent, r_a.at[pieces + k - 1], p, mate)

    tail = slice(0, 2 * LANES)
    everything = slice(0, tok)
    extra = chunks - 1 + 2 * pieces

    def strip(i):
        return slice(*cuts[i])

    def copy_a0(i):
        return remote(send.at[0, 0:2, strip(i)], recv.at[0, 0:2, strip(i)], sent, r_a.at[i], p, mate)

    def copy_y0(i):
        return remote(send.at[1, 0:2, strip(i)], recv.at[1, 0:2, strip(i)], sent, r_y.at[i], p, across)

    def copy_y(k, count=2):
        cols = pl.ds(2 * k, count)
        return remote(send.at[1, cols], recv.at[1, cols], sent, r_y.at[pieces + k - 1], p, across)

    def copy_end(i):
        part = slice(i * LANES, (i + 1) * LANES)
        return remote(send.at[1, last, part], recv.at[1, last, part], sent, r_y.at[pieces + chunks - 1 + i], p, across)

    detour = detour_a.shape[0]
    turn_unit = 5
    away = slice(0, detour)
    rest = slice(detour, tok)
    copy_d1 = remote(send.at[1, turn_unit, away], detour_a, sent, r_d.at[0], flip(p, 1), q)
    copy_d2 = remote(detour_a, detour_b, sent, r_d.at[1], p, across)
    copy_d3 = remote(detour_b, recv.at[1, turn_unit, away], sent, r_d.at[0], flip(p, 1), q)
    copy_z1 = remote(send.at[1, turn_unit - 1, away], detour_c, sent, r_z.at[0], flip(p, 2), q)
    copy_z2 = remote(detour_c, detour_e, sent, r_z.at[1], p, across)
    copy_z3 = remote(detour_e, recv.at[1, turn_unit - 1, away], sent, r_z.at[0], flip(p, 2), q)

    def copy_part(u, part, n):
        return remote(send.at[1, u, part], recv.at[1, u, part], sent, r_y.at[n], p, across)

    whole_4 = copy_part(turn_unit - 1, everything, pieces + 1)
    rest_4 = copy_part(turn_unit - 1, rest, pieces + 1)
    whole_5 = copy_part(turn_unit, everything, extra)
    rest_5 = copy_part(turn_unit, rest, extra)

    copy_swap = remote(send.at[1, last, tail], swap_in, sent, r_swap, p, mate)
    swapped = []
    for i in range(2):
        part = slice(i * LANES, (i + 1) * LANES)
        swapped.append(
            remote(swap.at[part], recv.at[1, last, part], sent, r_y.at[pieces + chunks - 1 + i], p, diagonal)
        )

    def copy_b(k):
        cols = pl.ds(2 * k, 2)
        return remote(send.at[2, cols], recv.at[2, cols], sent, r_b, p, mate)

    def copy_l(d):
        peer = flip(p, d)
        cols = pl.ds(pl.multiple_of(peer * rows, LANES), rows)
        return remote(left_h.at[:, cols], lall.at[d], sent, r_l, peer, q)

    def copy_r(d):
        return remote(right_h.at[:, my_cols], rall.at[d], sent, r_r, flip(p, d), q)

    def copy_u(d):
        return remote(ranked.at[0], ranked.at[d], sent, r_u, flip(p, d), q)

    def copy_f(d, core):
        return remote(marks.at[0], marks.at[d], sent, r_f, flip(p, d), 2 * y + core)

    copy_lin = remote(lin, lin_in, sent, r_lin, p, mate)
    copy_far = remote(lin_out, lin_far, sent, r_far, p, across)

    def copy_post(i, d):
        return remote(post.at[i], post_in.at[d - 1, i], sent, r_post, p, flip(q, d))

    def split_store(which, k, value):
        send[which, 2 * k] = value[:, :LANES]
        send[which, 2 * k + 1] = value[:, LANES:]

    def product(s, k):
        return jnp.dot(ctx[...], w_v[s, k], preferred_element_type=F32)

    order = [*range(2, pieces), 1, 0]
    with jax.named_scope("load0"):
        locals_[0].wait()
        w_first(0).wait()
    w_first(1).start()
    top = jnp.dot(ctx[0:upper, :], w_v[1 - c, 0], preferred_element_type=F32).astype(BF)
    first_v[0] = top[:, :LANES]
    first_v[1] = top[:, LANES:]
    def strip_product(s, i):
        return jnp.dot(ctx[strip(i), :], w_v[s, 0], preferred_element_type=F32)

    def prepare(i):
        value = strip_product(0, i).astype(BF)
        send[0, 0, strip(i)] = value[:, :LANES]
        send[0, 1, strip(i)] = value[:, LANES:]

    def give(i):
        prepare(i)
        copy_a0(i).start()

    @pl.when((c == 1) & (y == 0))
    def _():
        locals_[1].wait()
        prepare(1)

    with jax.named_scope("barrier"):
        pl.semaphore_wait(barrier, 6)
    copy_top.start()
    signal(rounds.at[0], flip(p, 1), q)
    for item in w_step(0, True):
        item.start()

    @pl.when((c == 0) | (y == 1))
    def _():
        locals_[1].wait()

    def pass_on(i, value):
        send[1, 0, strip(i)] = (value[:, :LANES] + recv[0, 0, strip(i)].astype(F32)).astype(BF)
        send[1, 1, strip(i)] = (value[:, LANES:] + recv[0, 1, strip(i)].astype(F32)).astype(BF)
        copy_y0(i).start()

    @pl.when(c == 0)
    def _():
        mine = [strip_product(1, i) for i in (1, 2)]
        copy_a0(1).wait_recv()
        pass_on(1, mine[0])
        w_first(1).wait()
        give(1)
        copy_a0(2).wait_recv()
        pass_on(2, mine[1])
        give(2)
        give(0)
        send[1, 0, strip(0)] = first_v[0]
        send[1, 1, strip(0)] = first_v[1]

    @pl.when((c == 1) & (y == 1))
    def _():
        prepare(1)

    @pl.when(c == 1)
    def _():
        copy_a0(1).start()
        give(2)
        send[0, 0, strip(0)] = first_v[0]
        send[0, 1, strip(0)] = first_v[1]
        w_first(1).wait()

    for item in w_step(1, True):
        item.start()
    near_copy(0).start()
    for item in w_step(0, True):
        item.wait()
    split_store(0, 1, product(0, 1).astype(BF))
    copy_a(1).start()
    for item in w_step(2, True):
        item.start()

    @pl.when(c == 1)
    def _():
        mine = [strip_product(1, i) for i in (1, 2, 0)]
        with jax.named_scope("wait_a0"):
            for i in (1, 2, 0):
                copy_a0(i).wait_recv()
                pass_on(i, mine[i - 1])


    def far(k, carry):
        for item in w_step(k, False):
            item.wait()

        @pl.when(k + 1 < chunks)
        def _():
            w_copy(0, k + 1, w_sem.at[k % 2]).wait()

        mine = product(1, k)
        @pl.when((k == 3) & inner)
        def _():
            with jax.named_scope("wait_d1"):
                copy_d1.wait_recv()
            copy_d2.start()

        @pl.when((k == 3) & lower_z)
        def _():
            with jax.named_scope("wait_z1"):
                copy_z1.wait_recv()
            copy_z2.start()

        with jax.named_scope("wait_a"):
            copy_a(k).wait_recv()
        send[1, 2 * k] = (mine[:, :LANES] + recv[0, 2 * k].astype(F32)).astype(BF)
        send[1, 2 * k + 1] = (mine[:, LANES:] + recv[0, 2 * k + 1].astype(F32)).astype(BF)

        @pl.when((k + 1 < chunks) & (k != 2))
        def _():
            copy_y(k).start()

        @pl.when((k == 2) & outer)
        def _():
            copy_d1.start()

        @pl.when((k == 2) & upper_z)
        def _():
            copy_z1.start()
            rest_4.start()

        @pl.when((k == 2) & jnp.logical_not(upper_z))
        def _():
            whole_4.start()

        @pl.when((k == 2) & outer)
        def _():
            rest_5.start()

        @pl.when((k == 2) & jnp.logical_not(outer))
        def _():
            whole_5.start()

        @pl.when((k + 1 == chunks) & (c == 0))
        def _():
            send[1, last, tail] = mine[tail, LANES:].astype(BF)
            copy_swap.start()

        @pl.when(k + 2 < chunks)
        def _():
            for item in w_step(k + 2, False):
                item.start()

        @pl.when(k + 3 < chunks)
        def _():
            w_copy(0, k + 3, w_sem.at[k % 2]).start()

        near_copy(k).start()

        @pl.when(k == 1)
        def _():
            for item in locals_[2:]:
                item.start()
            pl.semaphore_wait(rounds.at[0], 1)
            signal(rounds.at[1], flip(p, 2), q)

        @pl.when(k == 2)
        def _():
            pl.semaphore_wait(rounds.at[1], 1)
            signal(rounds.at[2], flip(p, 4), q)

        @pl.when(k == 3)
        def _():
            pl.semaphore_wait(rounds.at[2], 1)
            for d in range(1, n_pop):
                copy_r(n_pop - d).start()
                copy_l(n_pop - d).start()

        @pl.when(k + 1 < chunks)
        def _():
            split_store(0, k + 1, product(0, k + 1).astype(BF))
            copy_a(k + 1).start()

        @pl.when(k == 1)
        def _():
            split_store(2, 0, product(2, 0).astype(BF))
            copy_b(0).start()

        split_store(2, k, product(2, k).astype(BF))
        copy_b(k).start()
        return carry

    with jax.named_scope("far"):
        lax.fori_loop(1, chunks, far, 0)

    for item in locals_[2:]:
        item.wait()
    wait_for(w_v.at[3], loc_sem.at[2])

    lane = lax.broadcasted_iota(jnp.int32, (1, LANES), 1)
    ceiling = math.log(members / 2 + 1)
    whole = sum(max(0.0, ceiling - math.log(i + 1.0)) for i in range(members))
    shaped = jnp.maximum(0.0, ceiling - jnp.log(ranks[...].astype(F32) + 1.0)) / whole - 1.0 / members
    ranked[0] = jnp.where(lane // mem == p, jnp.concatenate([shaped] * n_pop, axis=1), 0.0)
    for d in range(1, n_pop):
        copy_u(d).start()

    def near(k, carry):
        cols = pl.ds(pl.multiple_of(k * BLK, BLK), BLK)
        base[:, cols] = product(3, k) + res[:, cols].astype(F32)
        return carry

    with jax.named_scope("near"):
        lax.fori_loop(0, chunks, near, 0)

    @pl.when(c == 1)
    def _():
        copy_swap.wait_recv()
        swap[...] = (send[0, last, tail].astype(F32) + swap_in[...].astype(F32)).astype(BF)
        for item in reversed(swapped):
            item.start()

    copy_y(chunks - 1, 1).start()

    def spread(slot, value):
        lin[slot * mem:(slot + 1) * mem, :] = value

    with jax.named_scope("early"):
        r_mine = rall[0].astype(F32)
        gr_hi, gr_lo = split_two(r_mine * gain[:, my_cols])
        spread(0, nt_dot(lcols[...], ctx[...]))
        spread(1, nt_dot(gr_hi, tgt[...]) + nt_dot(gr_lo, tgt[...]))
        r_full = right[...].astype(F32)
        gr_full = r_full * gain[...]
        norm_r = jnp.sum(r_full * r_full, axis=1, keepdims=True)
        norm_gr = jnp.sum(gr_full * gr_full, axis=1, keepdims=True)
        for acc in (sq_s, sq_a, sq_e, sq_t):
            acc[...] = jnp.zeros_like(acc)

    def mixed(block, start, size):
        cols = pl.ds(pl.multiple_of(block * width + start, LANES), size)
        r = right[:, cols]
        g = gain[:, cols]
        hi, low = split_two(r.astype(F32) * (g * g))
        return jnp.concatenate([r, hi, low], axis=0)

    def linear(k, carry):
        crossed, crossed_g = carry
        near_rows = mixed(q, k * BLK, BLK)
        far_rows = mixed(across, k * BLK, BLK)
        for h in range(2):
            cols = pl.ds(pl.multiple_of(k * BLK + h * LANES, LANES), LANES)
            part = slice(h * LANES, (h + 1) * LANES)
            u = 2 * k + h
            s = base[:, cols] + recv[2, u].astype(F32)
            base[:, cols] = s
            hi, low = split_two(s)
            both = nt_dot(near_rows[:, part], hi) + nt_dot(near_rows[:, part], low) + nt_dot(far_rows[:, part], send[1, u])
            crossed = crossed + both[0:mem]
            crossed_g = crossed_g + both[mem:2 * mem] + both[2 * mem:3 * mem]
            wide = tgt[:, cols].astype(F32)
            sq_t[...] += wide * wide
        return crossed, crossed_g

    with jax.named_scope("wait_b"):
        wait_for(recv.at[2], r_b)
    with jax.named_scope("linear"):
        top_rows = mixed(other, 0, BLK)
        top = nt_dot(top_rows[:, :LANES], first_v[0]) + nt_dot(top_rows[:, LANES:], first_v[1])
        late = nt_dot(mixed(other, last * LANES, LANES), send[0, last, tail])
        top = sum(jnp.concatenate([v, jnp.zeros((3 * mem, tok - v.shape[1]), F32)], axis=1) for v in (top, late))
        top = top * jnp.where(c == 1, 1.0, 0.0)
        carry = (top[0:mem], top[mem:2 * mem] + top[2 * mem:3 * mem])
        crossed, crossed_g = lax.fori_loop(0, chunks, linear, carry)
        spread(2, crossed)
        spread(3, crossed_g)

    @pl.when(c == 0)
    def _():
        copy_lin.start()
        for i in order[:-2]:
            copy_end(i).start()

    def arrived(u, part):
        cols = pl.ds(pl.multiple_of(u * LANES, LANES), LANES)
        gain_u = gain[:, pl.ds(pl.multiple_of(q * width + u * LANES, LANES), LANES)]
        s = base[part, cols] + recv[1, u, part].astype(F32)
        base[part, cols] = s
        gs = s * gain_u
        return s * s, gs * gs, gs * tgt[part, cols].astype(F32)

    def settle(u, carry):
        for acc, item in zip((sq_s, sq_a, sq_e), arrived(u, everything)):
            acc[...] += item
        return carry

    with jax.named_scope("wait_y0"):
        for i in range(1, pieces):
            copy_y0(i).wait_recv()

        @pl.when(c == 0)
        def _():
            wait_for(direct, r_top)
            for u in range(2):
                recv[1, u, strip(0)] = jnp.zeros((upper, LANES), BF)
                base[0:upper, u * LANES:(u + 1) * LANES] += direct[0, u].astype(F32) + direct[1, u].astype(F32)

        @pl.when(c == 1)
        def _():
            copy_y0(0).wait_recv()

    lax.fori_loop(0, 2, settle, 0)

    @pl.when(c == 1)
    def _():
        for i in order:
            copy_end(i).start()
        with jax.named_scope("wait_lin"):
            copy_lin.wait_recv()
        lin_out[...] = lin[...] + lin_in[...]
        copy_far.start()

    @pl.when(inner)
    def _():
        with jax.named_scope("wait_d2"):
            copy_d2.wait_recv()
        copy_d3.start()

    @pl.when(lower_z)
    def _():
        with jax.named_scope("wait_z2"):
            copy_z2.wait_recv()
        copy_z3.start()

    def settle_chunk(k, carry):
        with jax.named_scope("wait_y"):
            @pl.when(k != 2)
            def _():
                copy_y(k).wait_recv()

            @pl.when((k == 2) & upper_z)
            def _():
                rest_4.wait_recv()
                with jax.named_scope("wait_z3"):
                    copy_z3.wait_recv()

            @pl.when((k == 2) & jnp.logical_not(upper_z))
            def _():
                whole_4.wait_recv()

            @pl.when((k == 2) & outer)
            def _():
                rest_5.wait_recv()
                with jax.named_scope("wait_d3"):
                    copy_d3.wait_recv()

            @pl.when((k == 2) & jnp.logical_not(outer))
            def _():
                whole_5.wait_recv()

        settle(2 * k, 0)
        settle(2 * k + 1, 0)
        return carry

    with jax.named_scope("settle"):
        lax.fori_loop(1, 2, settle_chunk, 0)
        lax.fori_loop(3, chunks - 1, settle_chunk, 0)
    half_of = slice(1, n_pop)
    with jax.named_scope("wait_lr"):
        wait_for(lall.at[half_of], r_l)
        wait_for(rall.at[half_of], r_r)
        wait_for(ranked.at[half_of], r_u)
    with jax.named_scope("turn"):
        for d in range(n_pop):
            place = pl.ds(pl.multiple_of(flip(p, d) * mem, mem), mem)
            right_all[place, :] = rall[d]
            left_v[place, :] = lall[d].astype(F32)
        left_t[...] = left_v[...].T
    with jax.named_scope("wait_y8"):
        copy_y(chunks - 1, 1).wait_recv()
    settle(last - 1, 0)
    lax.fori_loop(2, 3, settle_chunk, 0)
    before = nt_dot(row_picker(4), halves((sq_s[...], sq_a[...], sq_e[...], sq_t[...])))
    picker = row_picker(3)
    for i in order:
        part = slice(i * LANES, (i + 1) * LANES)
        with jax.named_scope("wait_end"):
            copy_end(i).wait_recv()
        with jax.named_scope("end"):
            post[i] = (before[:, part] + nt_dot(picker, halves(arrived(last, part))))[0:4]

            @pl.when(c == 0)
            def _():
                copy_post(i, 3).start()
                copy_post(i, 1).start()

            @pl.when(c == 1)
            def _():
                copy_post(i, 2).start()

    others = marks.at[half_of]

    @pl.when(c == 1)
    def _():
        with jax.named_scope("wait_far"):
            copy_far.wait_recv()
        own = lin_out[...] + lin_far[...]
        lifted = own[0:mem] * (SIGMA / math.sqrt(full))
        lifted2 = lifted * lifted
        extra_s = 2.0 * lifted * own[2 * mem:3 * mem] + lifted2 * norm_r
        extra_a = 2.0 * lifted * own[3 * mem:4 * mem] + lifted2 * norm_gr
        extra_e = lifted * own[mem:2 * mem]
        with jax.named_scope("wait_post"):
            wait_for(post_in, r_post)
        with jax.named_scope("errors"):
            late = jnp.concatenate([post[i] + post_in[0, i] + post_in[1, i] + post_in[2, i] for i in range(pieces)], axis=1)
            meansq = (late[0:1] + extra_s) / full
            inverse = lax.rsqrt(meansq + EPSILON)
            errors = inverse * inverse * (late[1:2] + extra_a) - 2.0 * inverse * (late[2:3] + extra_e) + late[3:4]
            summed = jnp.sum(errors, axis=1, keepdims=True)
            spot = lax.broadcasted_iota(jnp.int32, (mem, LANES), 0) + p * mem
            here = lax.broadcasted_iota(jnp.int32, (mem, LANES), 1) == spot
            marks[0] = jnp.sum(jnp.where(here, summed, 0.0), axis=0, keepdims=True)
            for d in range(n_pop - 1, -1, -1):
                copy_f(d, 0).start()
                if d > 0:
                    copy_f(d, 1).start()

    @pl.when(c == 0)
    def _():
        with jax.named_scope("wait_f"):
            wait_for(marks, r_f)

    @pl.when(c == 1)
    def _():
        with jax.named_scope("wait_f"):
            wait_for(others, r_f)

    fits[0:1] = sum((marks[d] for d in range(1, n_pop)), marks[0])
    fits[1:2] = sum((ranked[d] for d in range(1, n_pop)), ranked[0])
    for which in range(2):
        wait_for(send.at[which, 2:units], sent)
    wait_for(send.at[2], sent)
    wait_for(first_v, sent)
    wait_for(lall.at[half_of], sent)
    wait_for(rall.at[half_of], sent)
    wait_for(ranked.at[half_of], sent)
    for core in range(2):
        @pl.when(c == core)
        def _(core=core):
            for i in range(core, pieces):
                copy_a0(i).wait_send()
            for i in range(1 - core, pieces):
                copy_y0(i).wait_send()
            if core == 1:
                for item in swapped:
                    item.wait_send()
            if core == 1:
                @pl.when(inner)
                def _():
                    copy_d2.wait_send()
                    copy_d3.wait_send()

                @pl.when(lower_z)
                def _():
                    copy_z2.wait_send()
                    copy_z3.wait_send()

            if core == 0:
                copy_lin.wait_send()
                wait_for(post_in.at[0:2], sent)
            else:
                copy_far.wait_send()
                wait_for(post_in.at[0], sent)
                wait_for(marks, sent)
                wait_for(others, sent)


def in_hbm(x):
    return pltpu.with_memory_space_constraint(x, pltpu.HBM)


def fused_shards(
    n_pop, n_mp, context, out_weight, residual, target, norm_gain, left_factors, right_factors, member_ranks
):
    tok, width = context.shape
    full = out_weight.shape[1]
    mem = left_factors.shape[0]
    rows = full // n_pop
    chunks = width // BLK
    units = width // LANES
    pieces = tok // LANES
    ranks = member_ranks.reshape(1, mem)
    anywhere = pl.BlockSpec(memory_space=pltpu.HBM)
    vmem = pl.BlockSpec(memory_space=pltpu.VMEM)
    dma = pltpu.SemaphoreType.DMA
    acc = pltpu.VMEM((tok, LANES), F32)
    group = pltpu.VMEM((4 * mem, tok), F32)
    base, left_t, right_all, fits = pl.pallas_call(
        functools.partial(kernel, n_pop, n_mp),
        name="es_step",
        out_shape=(
            jax.ShapeDtypeStruct((tok, width), F32),
            jax.ShapeDtypeStruct((rows, n_pop * mem), F32),
            jax.ShapeDtypeStruct((n_pop * mem, width), BF),
            jax.ShapeDtypeStruct((2, n_pop * mem), F32),
        ),
        in_specs=[anywhere] * 8,
        out_specs=[vmem] * 4,
        scratch_shapes=[
            pltpu.VMEM((4, chunks, width, BLK), BF),
            pltpu.VMEM((tok, width), BF),
            pltpu.VMEM((tok, width), BF),
            pltpu.VMEM((tok, width), BF),
            pltpu.VMEM((mem, width), BF),
            pltpu.VMEM((1, full), F32),
            pltpu.VMEM((mem, full), BF),
            pltpu.VMEM((1, mem), jnp.int32),
            pltpu.VMEM((3, units, tok, LANES), BF),
            pltpu.VMEM((3, units, tok, LANES), BF),
            pltpu.VMEM((2, 96, LANES), BF),
            pltpu.VMEM((2, 2, 96, LANES), BF),
            pltpu.VMEM((n_pop, mem, rows), BF),
            pltpu.VMEM((n_pop, mem, width), BF),
            acc, acc, acc, acc,
            group, group, group, group,
            pltpu.VMEM((pieces, 4, LANES), F32),
            pltpu.VMEM((n_mp - 1, pieces, 4, LANES), F32),
            pltpu.VMEM((2 * LANES, LANES), BF),
            pltpu.VMEM((2 * LANES, LANES), BF),
            pltpu.VMEM((112, LANES), BF),
            pltpu.VMEM((112, LANES), BF),
            pltpu.VMEM((112, LANES), BF),
            pltpu.VMEM((112, LANES), BF),
            pltpu.VMEM((n_pop, 1, LANES), F32),
            pltpu.VMEM((n_pop * mem, rows), F32),
            pltpu.VMEM((n_pop, 1, LANES), F32),
            dma((2,)),
            dma((2,)),
            dma((3,)),
            dma,
            dma((chunks - 1 + pieces,)),
            dma((chunks + 2 * pieces,)),
        ]
        + [dma] * 6
        + [dma((2,))] * 2
        + [dma] * 4
        + [pltpu.SemaphoreType.REGULAR((3,))],
        compiler_params=pltpu.CompilerParams(
            collective_id=0,
            has_side_effects=True,
            vmem_limit_bytes=48 * 1024 * 1024,
        ),
    )(
        *map(in_hbm, (
            context, out_weight, residual, target, norm_gain.reshape(1, full), left_factors,
            right_factors, ranks,
        ))
    )
    count_all = n_pop * mem
    update, base, fitness = pl.pallas_call(
        functools.partial(finish, n_pop, math.sqrt(count_all) / SIGMA, tok * full),
        name="es_update",
        out_shape=(
            jax.ShapeDtypeStruct((rows, width), F32),
            jax.ShapeDtypeStruct((tok, width), F32),
            jax.ShapeDtypeStruct((1, mem), F32),
        ),
        in_specs=[vmem] * 4,
        out_specs=[anywhere] * 3,
        scratch_shapes=[
            pltpu.VMEM((rows, width), F32),
            pltpu.VMEM((1, mem), F32),
            dma,
        ],
        compiler_params=pltpu.CompilerParams(
            vmem_limit_bytes=16 * 1024 * 1024
        ),
    )(left_t, right_all, base, fits)
    return (update, fitness.reshape(mem), base)


def finish(n_pop, scale, count, left_t, right_all, base_in, fits, update, base, fit, held, fit_v, sem):
    steps = held.shape[0] // 128
    mem = fit_v.shape[1]
    members = n_pop * mem
    copies = [
        pltpu.make_async_copy(base_in, base, sem),
        pltpu.make_async_copy(fit_v, fit, sem),
    ]
    copies[0].start()
    all_fit = fits[0:1] * (-1.0 / count)
    centre = all_fit - jnp.sum(all_fit, axis=1, keepdims=True) / members
    deviation = jnp.sqrt(jnp.sum(centre * centre, axis=1, keepdims=True) / members + 1e-05)
    weight = fits[1:2] + centre / deviation / members
    for i in range(steps):
        part = slice(i * 128, (i + 1) * 128)
        weighted = (left_t[part, :] * weight).astype(BF)
        held[part, :] = jnp.dot(weighted, right_all[...], preferred_element_type=F32) * scale
        copies.append(pltpu.make_async_copy(held.at[part], update.at[part], sem))
        copies[-1].start()
    p = lax.axis_index("pop")
    mine = jnp.zeros((1, mem), F32)
    for d in range(n_pop):
        mine = mine + jnp.where(p == d, 1.0, 0.0) * all_fit[:, d * mem:(d + 1) * mem]
    fit_v[...] = mine
    copies[1].start()
    for item in copies:
        item.wait()


def chosen(n_pop, n_mp, context, out_weight, *rest):
    tok, width = context.shape
    mem = rest[3].shape[0]
    full = out_weight.shape[1]
    chunks = width // BLK
    if n_mp == 4 and n_pop == 8 and width % BLK == 0 and chunks > 3 and (full // n_pop) % 128 == 0 and tok == 3 * LANES and mem == 16:
        return fused_shards(n_pop, n_mp, context, out_weight, *rest)
    return shards(context, out_weight, *rest)


def solution(mesh):
    in_specs = (
        P("pop", "mp"),
        P("mp", None),
        P("pop", "mp"),
        P("pop", "mp"),
        P(),
        P("pop", None),
        P("pop", None),
        P("pop"),
    )
    out_specs = (P("pop", "mp"), P("pop"), P("pop", "mp"))
    return jax.shard_map(
        functools.partial(chosen, mesh.shape["pop"], mesh.shape["mp"]), mesh=mesh, in_specs=in_specs, out_specs=out_specs, check_vma=False)
```
